128 devices in a mesh: dp: 8 (over y, core), expert: 16 (over x, z).
Axes of the slice: x: 4, y: 4, z: 4, core: 2. Of those that a mesh axis runs over, the one named last changes fastest.
Arguments:
- hidden_in: bfloat16 [8192, 7168], P(('dp', 'expert')), may hold values from -6 to 6
- norm_gain: float32 [7168], replicated, may hold values from 0.25 to 4
- route_logits: float32 [8192, 8], P(('dp', 'expert')), may hold values from -6 to 6
- expert_ids: int32 [8192, 8], P(('dp', 'expert')), may hold values from 0 to 255, as said below
- w_gate: bfloat16 [16, 7168, 2048], P('dp', None, 'expert'), may hold values from -0.0625 to 0.0625
- w_up: bfloat16 [16, 7168, 2048], P('dp', None, 'expert'), may hold values from -0.0625 to 0.0625
- w_down: bfloat16 [16, 2048, 7168], P('dp', 'expert'), may hold values from -0.125 to 0.125
- w_latent: bfloat16 [7168, 576], P(('dp', 'expert')), may hold values from -0.0625 to 0.0625
- kv_gain: float32 [512], replicated, may hold values from 0.25 to 4
- queries: bfloat16 [8192, 36864], P(('dp', 'expert')), may hold values from -240 to 240
- page_pool: bfloat16 [16384, 9216], P(('dp', 'expert')), may hold values from -6 to 6
- page_table: int32 [8192, 6], P(('dp', 'expert')), may hold values from 0 to 159
- kv_lengths: int32 [8192], P(('dp', 'expert')), may hold values from 1 to 96, 393216 in all
- migration: int32 [8, 16, 8, 4], P('dp', 'expert'), may hold values from 0 to 127
Outputs:
- hidden_out: bfloat16 [8192, 7168], P(('dp', 'expert'))
- attended: bfloat16 [8192, 32768], P(('dp', 'expert'))
The draws below stay inside these ranges and needn't reach their ends.
Inputs may be any that keep to these rules, and one draw needn't show every extreme that they name: `expert_ids`: each row names 8 different experts, at most one of them below 16. The rows of one device name one window expert at most 4 times; in every draw one window expert is named exactly 4 times by the rows of every device.
All inputs are finite; a program needn't handle non-finite values. No bound on the sum of `kv_lengths` on one device may be relied on, other than what follows from the above.
Results may differ from the reference program's by a relative error of at most 0.038.
Values may be sent and summed in bfloat16 or wider, within the bound.
No kernel may reach another device: no remote copies, remote signals or barrier semaphores. Data moves between devices by JAX's collectives and lax.ppermute only.
A program may use at most 192 MiB of HBM per device.

```python
import math
import jax
import jax.numpy as jnp
import numpy as np
from jax import lax

D = 7168
MOE_FF = 2048
NEXP = 256
TOP = 8
HEADS = 64
LATENT = 512
ROPE = 64
PAGE = 16
MAXP = 6
CAP = 4
MCAP = 4
TOK_DEV = 64
POOL_DEV = 128
WIN = 16
FF_DEV = 128
KVW = 576
ROWS = 8192
POOLS = 16384
EXTENDED = 160
N_DP = 8
N_EXPERT = 16


def draw_expert_ids(key, part):
    blocks = ROWS // TOK_DEV
    stride = TOK_DEV // CAP
    keys = jax.random.split(key, 6)
    full_one = jax.random.randint(keys[0], (), 0, WIN)
    counts = jax.random.randint(keys[1], (blocks, WIN), 1, CAP + 1)
    counts = jnp.where(jnp.arange(WIN)[None, :] == full_one, CAP, counts)
    orders = jax.vmap(lambda k: jax.random.permutation(k, WIN))(jax.random.split(keys[2], blocks))
    shifts = jax.random.randint(keys[3], (blocks, 1), 0, TOK_DEV)
    offsets = (jnp.arange(TOK_DEV)[None, :] - shifts) % TOK_DEV
    residue = offsets % stride
    level = offsets // stride
    inside = residue < WIN
    expert_of = jnp.take_along_axis(orders, jnp.minimum(residue, WIN - 1), axis=1)
    count_of = jnp.take_along_axis(counts, expert_of, axis=1)
    inside = inside & (level < count_of)
    position = jax.random.randint(keys[4], (blocks, TOK_DEV), 0, TOP)
    base = jax.random.randint(keys[5], (blocks, TOK_DEV), 0, NEXP - WIN)
    outside = WIN + (base[:, :, None] + jnp.arange(TOP)[None, None, :]) % (NEXP - WIN)
    place = inside[:, :, None] & (jnp.arange(TOP)[None, None, :] == position[:, :, None])
    ids = jnp.where(place, expert_of[:, :, None], outside)
    return ids.reshape(ROWS, TOP).astype(jnp.int32)


def draw_queries(key, part):
    values = jnp.clip(jax.random.normal(key, (ROWS, HEADS * KVW), jnp.float32), -6.0, 6.0)
    return values.astype(jnp.bfloat16)


def plant(values, stream_key, smallest, largest):
    longest = values.shape.index(max(values.shape))
    spots = []
    for shift in (0, 1):
        where = [jax.random.randint(jax.random.fold_in(stream_key, axis), (), 0, length) for axis, length in enumerate(values.shape)]
        where[longest] = (where[longest] + shift) % values.shape[longest]
        spots.append(tuple(where))
    return values.at[spots[0]].set(smallest).at[spots[1]].set(largest)


def shard_levels(key, extent, cuts, low, high):
    level, own = 1.0, jax.random.fold_in(key, 6)
    for dim, blocks in cuts:
        draws = jnp.exp(jax.random.uniform(jax.random.fold_in(own, dim), (blocks,), jnp.float32, low / len(cuts), high / len(cuts)))
        level = level * jnp.repeat(draws, extent[dim] // blocks).reshape([-1 if axis == dim else 1 for axis in range(len(extent))])
    return level


def profile(count, total, limit, skew):
    portions = [(1 << 20) // math.isqrt(rank ** skew) + 1 for rank in range(2, count + 1)]
    rest, given = total - limit - (count - 1), [1] * (count - 1)
    while rest > 0:
        candidates = [i for i in range(count - 1) if given[i] < limit]
        whole, budget = sum([portions[i] for i in candidates]), rest
        for i in candidates:
            addition = min(limit - given[i], max(1, budget * portions[i] // whole), rest)
            given[i] = given[i] + addition
            rest = rest - addition
    return np.array([limit] + given)


def uneven(own_key, amount, total, bound, slope):
    if amount == 2:
        one = jax.random.randint(own_key, (), max(1, total - bound), min(bound, total - 1) + 1)
        return jnp.stack([one, total - one])
    lengths = jnp.asarray(profile(amount, total, bound, slope), jnp.int32)
    couples = (amount - 1) // 2
    giver, taker = lengths[1:1 + 2 * couples:2], lengths[2:2 + 2 * couples:2]
    margin = jnp.minimum(giver - 1, bound - taker)
    shifted = jax.random.randint(jax.random.fold_in(own_key, 1), (couples,), 0, 1 << 20) % (margin + 1)
    lengths = lengths.at[1:1 + 2 * couples:2].set(giver - shifted).at[2:2 + 2 * couples:2].set(taker + shifted)
    return lengths[jax.random.permutation(jax.random.fold_in(own_key, 2), amount)]


def gaussian(own_key, shape, deviation, reach, pieces=(), kind=jnp.bfloat16):
    level = shard_levels(own_key, shape, pieces, -0.22, 0.18) if pieces else 1.0
    entries = jax.random.normal(own_key, shape, jnp.float32) * deviation * level
    return jnp.minimum(jnp.maximum(entries, -reach), reach).astype(kind)


def setup_inputs(seed: int = 0) -> dict:
    key_of = jax.random.split(jax.random.key(seed), 15)
    hidden_in = gaussian(key_of[0], (ROWS, D), 1.0, 6.0, ((0, 128),))
    norm_gain = jnp.clip(jnp.exp(jax.random.uniform(key_of[1], (D,), jnp.float32, math.log(0.25), math.log(4.0))), 0.25, 4.0)
    route_logits = gaussian(key_of[2], (ROWS, TOP), 1.5, 6.0, ((0, 128),), jnp.float32)
    expert_ids = draw_expert_ids(jax.random.fold_in(key_of[14], 71), 0)
    w_gate = gaussian(key_of[4], (WIN, D, MOE_FF), D ** -0.5, 0.0625, ((0, 8), (2, 16)))
    w_up = gaussian(key_of[5], (WIN, D, MOE_FF), D ** -0.5, 0.0625, ((0, 8), (2, 16)))
    w_down = gaussian(key_of[6], (WIN, MOE_FF, D), MOE_FF ** -0.5, 0.125, ((0, 8), (1, 16)))
    w_latent = gaussian(key_of[7], (D, KVW), D ** -0.5, 0.0625, ((0, 128),))
    kv_gain = jnp.clip(jnp.exp(jax.random.uniform(key_of[8], (LATENT,), jnp.float32, math.log(0.25), math.log(4.0))), 0.25, 4.0)
    queries = draw_queries(jax.random.fold_in(key_of[14], 71), 0)
    page_pool = gaussian(key_of[10], (POOLS, PAGE * KVW), 1.0, 6.0, ((0, 128),))
    page_table = plant(jax.random.randint(key_of[11], (ROWS, MAXP), 0, EXTENDED), jax.random.fold_in(key_of[11], 1), 0, EXTENDED - 1).astype(jnp.int32)
    kv_lengths = uneven(key_of[12], ROWS, ROWS * MAXP * PAGE // 2, MAXP * PAGE, 2).astype(jnp.int32)
    migration = plant(jax.random.randint(key_of[13], (N_DP, N_EXPERT, N_DP, MCAP), 0, POOL_DEV), jax.random.fold_in(key_of[13], 1), 0, POOL_DEV - 1).astype(jnp.int32)
    return {"hidden_in": hidden_in, "norm_gain": norm_gain, "route_logits": route_logits, "expert_ids": expert_ids, "w_gate": w_gate, "w_up": w_up, "w_down": w_down, "w_latent": w_latent, "kv_gain": kv_gain, "queries": queries, "page_pool": page_pool, "page_table": page_table, "kv_lengths": kv_lengths, "migration": migration}


softmax_scale = 192.0 ** (-0.5)
routed_scale = 2.5
norm_eps = 1e-06

def rms_rows(values, gain):
    stat = lax.optimization_barrier(jnp.mean(values * values, axis=-1, keepdims=True))
    return values * lax.rsqrt(stat + norm_eps) * gain

def rotate_keys(rope_part, position):
    half = ROPE // 2
    freq = 10000.0 ** (-jnp.arange(half, dtype=jnp.float32) / half)
    angle = position[:, None] * freq[None, :]
    first = rope_part[:, :half]
    second = rope_part[:, half:]
    cosine = jnp.cos(angle)
    sine = jnp.sin(angle)
    return jnp.concatenate([first * cosine - second * sine, second * cosine + first * sine], axis=1)

def reference(hidden_in, norm_gain, route_logits, expert_ids, w_gate, w_up, w_down, w_latent, kv_gain, queries, page_pool, page_table, kv_lengths, migration):
    devices = N_DP * N_EXPERT
    x_wide = hidden_in.astype(jnp.float32)
    normed = rms_rows(x_wide, norm_gain).astype(jnp.bfloat16)
    in_window = expert_ids < WIN
    has = jnp.any(in_window, axis=1)
    chosen = lax.optimization_barrier(jnp.sum(jnp.where(in_window, expert_ids, 0), axis=1)).astype(jnp.int32)
    sigma = jax.nn.sigmoid(route_logits)
    weight = routed_scale * lax.optimization_barrier(jnp.sum(jnp.where(in_window, sigma, 0.0), axis=1)) / lax.optimization_barrier(jnp.sum(sigma, axis=1))
    onehot = ((chosen[:, None] == jnp.arange(WIN, dtype=jnp.int32)[None, :]) & has[:, None]).astype(jnp.int32)
    onehot = onehot.reshape(devices, TOK_DEV, WIN)
    rank = jnp.cumsum(onehot, axis=1) - onehot
    slot = lax.optimization_barrier(jnp.sum(rank * onehot, axis=2)).reshape(ROWS).astype(jnp.int32)
    source = jnp.arange(ROWS, dtype=jnp.int32) // TOK_DEV
    column = (source * CAP + slot).astype(jnp.int32)
    target = jnp.where(has, chosen, WIN).astype(jnp.int32)
    buffers = jnp.zeros((WIN, devices * CAP, D), jnp.bfloat16).at[target, column].set(normed, mode='drop')

    def expert_apply(operands):
        rows_in, gate_w, up_w, down_w = operands
        gate = jnp.dot(rows_in, gate_w, preferred_element_type=jnp.float32)
        upper = jnp.dot(rows_in, up_w, preferred_element_type=jnp.float32)
        active = (jax.nn.silu(gate) * upper).astype(jnp.bfloat16)
        active = active.reshape(rows_in.shape[0], N_EXPERT, FF_DEV).astype(jnp.float32)
        down_parts = down_w.reshape(N_EXPERT, FF_DEV, D).astype(jnp.float32)
        partial_value = jnp.einsum('nsf,sfd->snd', active, down_parts, precision=lax.Precision.HIGHEST).astype(jnp.bfloat16)
        return lax.optimization_barrier(jnp.sum(partial_value.astype(jnp.float32), axis=0)).astype(jnp.bfloat16)
    outputs = lax.map(expert_apply, (buffers, w_gate, w_up, w_down))
    picked = outputs[jnp.minimum(chosen, WIN - 1), column].astype(jnp.float32)
    hidden_out = (x_wide + (weight * has.astype(jnp.float32))[:, None] * picked).astype(jnp.bfloat16)
    projected = jnp.dot(hidden_out, w_latent, preferred_element_type=jnp.float32)
    latent = rms_rows(projected[:, :LATENT], kv_gain)
    rotary = rotate_keys(projected[:, LATENT:], kv_lengths.astype(jnp.float32))
    new_key = jnp.concatenate([latent, rotary], axis=1).astype(jnp.bfloat16)
    dp_index = source // N_EXPERT
    ex_index = source % N_EXPERT
    own_page = page_table < POOL_DEV
    moved = jnp.maximum(page_table - POOL_DEV, 0)
    from_dp = moved // MCAP
    from_slot = moved % MCAP
    remote = migration[from_dp, ex_index[:, None], dp_index[:, None], from_slot]
    global_page = jnp.where(own_page, source[:, None] * POOL_DEV + page_table, (from_dp * N_EXPERT + ex_index[:, None]) * POOL_DEV + remote).astype(jnp.int32)

    def attend(operands):
        query_rows, pages, length, fresh = operands
        keys = page_pool[pages].reshape(TOK_DEV, MAXP * PAGE, KVW).astype(jnp.float32)
        query = query_rows.reshape(TOK_DEV, HEADS, KVW).astype(jnp.float32)
        fresh_wide = fresh.astype(jnp.float32)
        scores = jnp.einsum('rhc,rtc->rht', query, keys, precision=lax.Precision.HIGHEST) * softmax_scale
        own = jnp.einsum('rhc,rc->rh', query, fresh_wide, precision=lax.Precision.HIGHEST) * softmax_scale
        valid = jnp.arange(MAXP * PAGE, dtype=jnp.int32)[None, None, :] < length[:, None, None]
        top = jnp.maximum(lax.optimization_barrier(jnp.max(jnp.where(valid, scores, -1e+30), axis=2)), own)
        expo = jnp.where(valid, jnp.exp(scores - top[:, :, None]), 0.0)
        expo_own = jnp.exp(own - top)
        total = lax.optimization_barrier(jnp.sum(expo, axis=2)) + expo_own
        probs = (expo / total[:, :, None]).astype(jnp.bfloat16).astype(jnp.float32)
        probs_own = (expo_own / total).astype(jnp.bfloat16).astype(jnp.float32)
        result = jnp.einsum('rht,rtc->rhc', probs, keys[:, :, :LATENT], precision=lax.Precision.HIGHEST)
        result = result + probs_own[:, :, None] * fresh_wide[:, None, :LATENT]
        return result.astype(jnp.bfloat16).reshape(TOK_DEV, HEADS * LATENT)
    attended = lax.map(attend, (queries.reshape(devices, TOK_DEV, HEADS * KVW), global_page.reshape(devices, TOK_DEV, MAXP), kv_lengths.reshape(devices, TOK_DEV), new_key.reshape(devices, TOK_DEV, KVW)))
    return (hidden_out, attended.reshape(ROWS, HEADS * LATENT))
```

```python
import functools

import jax
import jax.numpy as jnp
from jax import lax
from jax.experimental import pallas as pl
from jax.experimental.pallas import tpu as pltpu
from jax.sharding import PartitionSpec as P

HEADS = 64
LATENT = 512
PAGE = 16
MAXP = 6
CAP = 4
MCAP = 4
KVW = 576
SIDE = 4

softmax_scale = 192.0 ** (-0.5)
routed_scale = 2.5
norm_eps = 1e-06
MIB = 1 << 20


def rms_rows(values, gain):
    stat = jnp.mean(values * values, axis=-1, keepdims=True)
    return values * lax.rsqrt(stat + norm_eps) * gain


def shift(value, axis, step):
    pairs = []
    for x in range(SIDE):
        for z in range(SIDE):
            to_x = (x + step) % SIDE if axis == "x" else x
            to_z = (z + step) % SIDE if axis == "z" else z
            pairs.append((x * SIDE + z, to_x * SIDE + to_z))
    return lax.ppermute(value, "expert", pairs)


def ffn_kernel(expert, count, rows, parts, *refs):
    xs = refs[:count]
    gate_hbm, up_hbm, down_hbm = refs[count : count + 3]
    outs = refs[count + 3 : 2 * count + 3]
    x_buf, w_buf, d_buf, o_buf, acc, in_sem, d_sem, out_sem = refs[2 * count + 3 :]
    depth = gate_hbm.shape[1]
    piece = depth // parts

    def loads(c):
        cut = pl.ds(pl.multiple_of(c * piece, piece), piece)
        yield pltpu.make_async_copy(
            gate_hbm.at[expert, cut], w_buf.at[cut, pl.ds(0, 128)], in_sem.at[c, 0]
        )
        yield pltpu.make_async_copy(
            up_hbm.at[expert, cut], w_buf.at[cut, pl.ds(128, 128)], in_sem.at[c, 1]
        )
        at = 0
        for i in range(count):
            yield pltpu.make_async_copy(
                xs[i].at[:, cut], x_buf.at[pl.ds(at, rows[i]), cut], in_sem.at[c, 2 + i]
            )
            at += rows[i]

    def stores(c):
        cut = pl.ds(pl.multiple_of(c * piece, piece), piece)
        at = 0
        for i in range(count):
            yield pltpu.make_async_copy(
                o_buf.at[pl.ds(at, rows[i]), cut], outs[i].at[:, cut], out_sem.at[c, i]
            )
            at += rows[i]

    for c in range(parts):
        for copy in loads(c):
            copy.start()
    down = pltpu.make_async_copy(down_hbm.at[expert], d_buf, d_sem)
    down.start()
    acc[...] = jnp.zeros_like(acc)

    @pl.loop(0, parts)
    def _(c):
        for copy in loads(c):
            copy.wait()
        cut = pl.ds(pl.multiple_of(c * piece, piece), piece)
        acc[...] += jnp.dot(x_buf[:, cut], w_buf[cut, :], preferred_element_type=jnp.float32)

    gate = acc[:, :128]
    active = (gate / (1.0 + jnp.exp(-gate)) * acc[:, 128:]).astype(jnp.bfloat16)
    down.wait()

    @pl.loop(0, parts)
    def _(c):
        cut = pl.ds(pl.multiple_of(c * piece, piece), piece)
        o_buf[:, cut] = jnp.dot(active, d_buf[:, cut], preferred_element_type=jnp.float32).astype(
            jnp.bfloat16
        )
        for copy in stores(c):
            copy.start()

    @pl.loop(0, parts)
    def _(c):
        for copy in stores(c):
            copy.wait()


def ffn(blocks, expert, w_gate, w_up, w_down):
    rows = tuple(block.shape[0] for block in blocks)
    count, total, depth, parts = len(rows), sum(rows), w_gate.shape[1], 4
    return pl.pallas_call(
        functools.partial(ffn_kernel, expert, count, rows, parts),
        out_shape=[jax.ShapeDtypeStruct(block.shape, jnp.bfloat16) for block in blocks],
        in_specs=[pl.BlockSpec(memory_space=pl.ANY)] * (count + 3),
        out_specs=[pl.BlockSpec(memory_space=pl.ANY)] * count,
        scratch_shapes=[
            pltpu.VMEM((total, depth), jnp.bfloat16),
            pltpu.VMEM((depth, 256), jnp.bfloat16),
            pltpu.VMEM((128, depth), jnp.bfloat16),
            pltpu.VMEM((total, depth), jnp.bfloat16),
            pltpu.VMEM((total, 256), jnp.float32),
            pltpu.SemaphoreType.DMA((parts, 2 + count)),
            pltpu.SemaphoreType.DMA,
            pltpu.SemaphoreType.DMA((parts, count)),
        ],
        compiler_params=pltpu.CompilerParams(vmem_limit_bytes=24 * MIB),
        cost_estimate=pl.CostEstimate(
            flops=2 * total * depth * 384,
            bytes_accessed=2 * depth * (384 + 2 * total),
            transcendentals=total * 128,
        ),
        name="ffn",
    )(*blocks, w_gate, w_up, w_down)


def attend_kernel(per_step, table, lengths, q_ref, pages_ref, out_ref, top_ref, total_ref):
    first = pl.program_id(0) * per_step
    for r in range(per_step):
        row = first + r
        keys = jnp.concatenate([pages_ref[table[row * MAXP + p]] for p in range(MAXP)], axis=0)
        scores = (
            lax.dot_general(
                keys, q_ref[r], (((1,), (1,)), ((), ())), preferred_element_type=jnp.float32
            )
            * softmax_scale
        )
        valid = lax.broadcasted_iota(jnp.int32, scores.shape, 0) < lengths[row]
        scores = jnp.where(valid, scores, -1e30)
        top = jnp.max(scores, axis=0, keepdims=True)
        expo = jnp.where(valid, jnp.exp(scores - top), 0.0)
        total = jnp.sum(expo, axis=0, keepdims=True)
        probs = (expo / total).astype(jnp.bfloat16)
        out_ref[r] = lax.dot_general(
            probs, keys[:, :LATENT], (((0,), (0,)), ((), ())), preferred_element_type=jnp.float32
        ).astype(jnp.bfloat16)
        top_ref[r : r + 1, :] = top
        total_ref[r : r + 1, :] = total


def attend_cached(query, pages, page_table, kv_lengths):
    rows, per_step = query.shape[0], 8
    return pl.pallas_call(
        functools.partial(attend_kernel, per_step),
        out_shape=[
            jax.ShapeDtypeStruct((rows, HEADS, LATENT), jnp.bfloat16),
            jax.ShapeDtypeStruct((rows, HEADS), jnp.float32),
            jax.ShapeDtypeStruct((rows, HEADS), jnp.float32),
        ],
        grid_spec=pltpu.PrefetchScalarGridSpec(
            num_scalar_prefetch=2,
            grid=(rows // per_step,),
            in_specs=[
                pl.BlockSpec((per_step, HEADS, KVW), lambda i, t, n: (i, 0, 0)),
                pl.BlockSpec(pages.shape, lambda i, t, n: (0, 0, 0)),
            ],
            out_specs=[
                pl.BlockSpec((per_step, HEADS, LATENT), lambda i, t, n: (i, 0, 0)),
                pl.BlockSpec((per_step, HEADS), lambda i, t, n: (i, 0)),
                pl.BlockSpec((per_step, HEADS), lambda i, t, n: (i, 0)),
            ],
        ),
        compiler_params=pltpu.CompilerParams(vmem_limit_bytes=24 * MIB),
        cost_estimate=pl.CostEstimate(
            flops=2 * rows * HEADS * MAXP * PAGE * (KVW + LATENT),
            bytes_accessed=2 * (query.size + pages.size + rows * HEADS * LATENT),
            transcendentals=rows * HEADS * MAXP * PAGE,
        ),
        name="attend_cached",
    )(page_table.reshape(rows * MAXP), kv_lengths, query, pages)


def tail_kernel(
    parts,
    hidden_ref,
    back_ref,
    gain_ref,
    cos_ref,
    sin_ref,
    top_ref,
    total_ref,
    place_ref,
    w_hbm,
    q_hbm,
    o_hbm,
    hidden_out_ref,
    out_ref,
    w_buf,
    q_buf,
    o_buf,
    key_buf,
    own_buf,
    keep_buf,
    w_sem,
    q_sem,
    o_sem,
):
    width = hidden_ref.shape[1]
    piece = width // parts
    q_piece = q_hbm.shape[1] // parts_q
    o_piece = o_hbm.shape[1] // parts_q
    w_loads, q_loads, o_loads = [], [], []
    for c in range(parts):
        cut = pl.ds(c * piece, piece)
        w_loads.append(pltpu.make_async_copy(w_hbm.at[cut], w_buf.at[cut], w_sem.at[c]))
    for c in range(parts_q):
        cut = pl.ds(c * q_piece, q_piece)
        q_loads.append(pltpu.make_async_copy(q_hbm.at[:, cut], q_buf.at[:, cut], q_sem.at[c]))
        cut = pl.ds(c * o_piece, o_piece)
        o_loads.append(pltpu.make_async_copy(o_hbm.at[:, cut], o_buf.at[:, cut], o_sem.at[c]))
    for copy in w_loads + q_loads + o_loads:
        copy.start()
    place = place_ref[...]
    pick = (place != 0.0).astype(jnp.bfloat16)
    weight = jnp.sum(place, axis=1, keepdims=True)
    projected = jnp.zeros((hidden_ref.shape[0], KVW), jnp.float32)
    for c in range(parts):
        cut = slice(c * piece, (c + 1) * piece)
        picked = jnp.dot(pick, back_ref[:, cut], preferred_element_type=jnp.float32)
        hidden = (hidden_ref[:, cut].astype(jnp.float32) + weight * picked).astype(jnp.bfloat16)
        hidden_out_ref[:, cut] = hidden
        w_loads[c].wait()
        projected += jnp.dot(hidden, w_buf[cut, :], preferred_element_type=jnp.float32)
    latent = rms_rows(projected[:, :LATENT], gain_ref[...])
    first = projected[:, LATENT : LATENT + 32]
    second = projected[:, LATENT + 32 :]
    cosine, sine = cos_ref[...], sin_ref[...]
    new_key = jnp.concatenate(
        [latent, first * cosine - second * sine, second * cosine + first * sine], axis=1
    )
    new_key = new_key.astype(jnp.bfloat16).astype(jnp.float32)
    key_buf[...] = jnp.concatenate([new_key, new_key], axis=1)
    lane = lax.broadcasted_iota(jnp.int32, (8, 128), 1)
    head = lax.broadcasted_iota(jnp.int32, (8, HEADS), 1)
    blocks = hidden_ref.shape[0] // 8
    own_buf[...] = jnp.zeros_like(own_buf)
    for copy in q_loads:
        copy.wait()

    @pl.loop(0, HEADS // 2)
    def _(j):
        for b in range(blocks):
            rows = slice(8 * b, 8 * b + 8)
            cut = pl.ds(pl.multiple_of(j * 2 * KVW, 2 * KVW), 2 * KVW)
            product = q_buf[rows, cut].astype(jnp.float32) * key_buf[rows, :]
            tiles = [product[:, 128 * i : 128 * (i + 1)] for i in range(9)]
            low = tiles[0] + tiles[1] + tiles[2] + tiles[3] + jnp.where(lane < 64, tiles[4], 0.0)
            high = tiles[5] + tiles[6] + tiles[7] + tiles[8] + jnp.where(lane < 64, 0.0, tiles[4])
            low = jnp.sum(low, axis=1, keepdims=True)
            high = jnp.sum(high, axis=1, keepdims=True)
            own_buf[rows, :] += jnp.where(head == 2 * j, low, 0.0) + jnp.where(
                head == 2 * j + 1, high, 0.0
            )

    own = own_buf[...] * softmax_scale
    top_old = top_ref[...]
    top = jnp.maximum(top_old, own)
    part = total_ref[...] * jnp.exp(top_old - top)
    part_own = jnp.exp(own - top)
    inverse = 1.0 / (part + part_own)
    keep_buf[...] = part * inverse
    own_buf[...] = (part_own * inverse).astype(jnp.bfloat16).astype(jnp.float32)
    for copy in o_loads:
        copy.wait()

    @pl.loop(0, HEADS)
    def _(h):
        for b in range(blocks):
            rows = slice(8 * b, 8 * b + 8)
            keep = jnp.sum(jnp.where(head == h, keep_buf[rows, :], 0.0), axis=1, keepdims=True)
            add = jnp.sum(jnp.where(head == h, own_buf[rows, :], 0.0), axis=1, keepdims=True)
            cut = pl.ds(pl.multiple_of(h * LATENT, LATENT), LATENT)
            out_ref[rows, cut] = (
                o_buf[rows, cut].astype(jnp.float32) * keep + add * key_buf[rows, :LATENT]
            ).astype(jnp.bfloat16)


parts_q = 4


def tail(hidden_in, back, kv_gain, cosine, sine, top, total, place_weight, w_all, queries, o):
    rows, width = hidden_in.shape
    parts = 7
    vmem = pl.BlockSpec(memory_space=pltpu.VMEM)
    hbm = pl.BlockSpec(memory_space=pl.ANY)
    return pl.pallas_call(
        functools.partial(tail_kernel, parts),
        out_shape=[
            jax.ShapeDtypeStruct((rows, width), jnp.bfloat16),
            jax.ShapeDtypeStruct((rows, HEADS * LATENT), jnp.bfloat16),
        ],
        in_specs=[vmem] * 8 + [hbm] * 3,
        out_specs=[vmem] * 2,
        scratch_shapes=[
            pltpu.VMEM(w_all.shape, jnp.bfloat16),
            pltpu.VMEM(queries.shape, jnp.bfloat16),
            pltpu.VMEM(o.shape, jnp.bfloat16),
            pltpu.VMEM((rows, 2 * KVW), jnp.float32),
            pltpu.VMEM((rows, HEADS), jnp.float32),
            pltpu.VMEM((rows, HEADS), jnp.float32),
            pltpu.SemaphoreType.DMA((parts,)),
            pltpu.SemaphoreType.DMA((parts_q,)),
            pltpu.SemaphoreType.DMA((parts_q,)),
        ],
        compiler_params=pltpu.CompilerParams(vmem_limit_bytes=48 * MIB),
        cost_estimate=pl.CostEstimate(
            flops=2 * rows * width * KVW,
            bytes_accessed=2 * (w_all.size + queries.size + 2 * o.size),
            transcendentals=rows * HEADS * 2,
        ),
        name="tail",
    )(
        hidden_in,
        back,
        kv_gain.reshape(1, LATENT),
        cosine,
        sine,
        top,
        total,
        place_weight,
        w_all,
        queries,
        o,
    )


def plus(*terms):
    total = terms[0].astype(jnp.float32)
    for term in terms[1:]:
        total = total + term.astype(jnp.float32)
    return total.astype(jnp.bfloat16)


def after(values, *others):
    return lax.optimization_barrier((values, others))[0]


def near(block, axis):
    return shift(block, axis, 1), shift(block, axis, -1)


def far(below, above, axis):
    half = below.shape[0] // 2
    return shift(below[:half], axis, 1), shift(above[half:], axis, -1)


def body(
    hidden_in,
    norm_gain,
    route_logits,
    expert_ids,
    w_gate,
    w_up,
    w_down,
    w_latent,
    kv_gain,
    queries,
    page_pool,
    page_table,
    kv_lengths,
    migration,
):
    dp_count = lax.axis_size("dp")
    ex_count = lax.axis_size("expert")
    row_count = hidden_in.shape[0]
    local_experts = w_gate.shape[0]
    window = local_experts * dp_count
    width = hidden_in.shape[1]
    x_wide = hidden_in.astype(jnp.float32)
    normed = rms_rows(x_wide, norm_gain).astype(jnp.bfloat16)
    in_window = expert_ids < window
    has = jnp.any(in_window, axis=1)
    chosen = jnp.sum(jnp.where(in_window, expert_ids, 0), axis=1)
    sigma = jax.nn.sigmoid(route_logits)
    weight = (
        routed_scale * jnp.sum(jnp.where(in_window, sigma, 0.0), axis=1) / jnp.sum(sigma, axis=1)
    )
    onehot = ((chosen[:, None] == jnp.arange(window)[None, :]) & has[:, None]).astype(jnp.int32)
    rank = jnp.cumsum(onehot, axis=0) - onehot
    slot = jnp.sum(rank * onehot, axis=1)
    slots = local_experts * CAP
    place = chosen * CAP + slot
    pick = (place[:, None] == jnp.arange(window * CAP)[None, :]) & has[:, None]
    packed = jnp.einsum(
        "rs,rd->sd", pick.astype(jnp.bfloat16), normed, preferred_element_type=jnp.float32
    ).astype(jnp.bfloat16)
    place_weight = jnp.where(pick, weight[:, None], 0.0)
    arrived = lax.all_to_all(
        packed.reshape(dp_count, slots, width), "dp", split_axis=0, concat_axis=0, tiled=True
    )
    axes = (("z", "x"), ("x", "z"))
    both = range(local_experts)
    rows = [
        arrived[:, k * CAP : (k + 1) * CAP].reshape(dp_count * CAP, width) for k in both
    ]

    sides = [near(rows[k], axes[k][0]) for k in both]
    w_local, flat_list = after((w_latent, migration.reshape(dp_count * MCAP)), rows[1])
    spread = lax.all_to_all(
        jnp.broadcast_to(w_local[None], (ex_count,) + w_latent.shape),
        "expert",
        split_axis=0,
        concat_axis=0,
        tiled=True,
    )
    outgoing = jnp.take(page_pool, flat_list, axis=0, mode="clip")
    incoming = lax.all_to_all(
        outgoing.reshape(dp_count, MCAP, page_pool.shape[1]),
        "dp",
        split_axis=0,
        concat_axis=0,
        tiled=True,
    )
    fars = [far(*sides[k], axes[k][0]) for k in both]
    group = [jnp.concatenate((rows[k],) + sides[k] + fars[k], axis=0) for k in both]
    sides = [near(group[k], axes[k][1]) for k in both]
    w_all = lax.all_gather(
        spread.reshape(ex_count * w_latent.shape[0], KVW), "dp", axis=0, tiled=True
    )
    query, pool = after((queries, page_pool), group[0], group[1])
    query = query.reshape(row_count, HEADS, KVW)
    pool = pool.reshape(pool.shape[0], PAGE, KVW)
    y_own = [ffn([group[k]], k, w_gate, w_up, w_down)[0] for k in both]
    sides = after(sides, query, pool, y_own)
    fars = [far(*sides[k], axes[k][1]) for k in both]
    y_side = [ffn(sides[k], k, w_gate, w_up, w_down) for k in both]
    half = group[0].shape[0] // 2
    early = [
        (shift(y_side[k][1][half:], axes[k][1], 1), shift(y_side[k][0][:half], axes[k][1], -1))
        for k in both
    ]
    fars = after(fars, y_side, spread, incoming)
    y_far = [ffn(fars[k], k, w_gate, w_up, w_down) for k in both]
    relay = [(shift(y_far[k][0], axes[k][1], 1), shift(y_far[k][1], axes[k][1], -1)) for k in both]
    incoming = after(incoming, y_far)
    pages = jnp.concatenate([pool, incoming.reshape(dp_count * MCAP, PAGE, KVW)], axis=0)
    cached, top, total = attend_cached(query, pages, page_table, kv_lengths)
    relay, early = after((relay, early), cached)
    late = [
        (
            shift(plus(y_side[k][1][:half], relay[k][0]), axes[k][1], 1),
            shift(plus(y_side[k][0][half:], relay[k][1]), axes[k][1], -1),
        )
        for k in both
    ]
    cached = cached.reshape(row_count, HEADS * LATENT)
    late = after(late, cached, w_all)
    finished = []
    for k in both:
        inner, n = axes[k][0], rows[k].shape[0]
        small = n // 2
        summed = plus(
            y_own[k],
            jnp.concatenate([late[k][0], early[k][0]], axis=0),
            jnp.concatenate([early[k][1], late[k][1]], axis=0),
        )
        own, t_below, t_above, t_far = (summed[i * n : (i + 1) * n] for i in range(4))
        relay_up = shift(t_far[:small], inner, 1)
        relay_down = shift(t_far[small:], inner, -1)
        from_below = shift(
            jnp.concatenate([plus(t_above[:small], relay_up), t_above[small:]], axis=0), inner, 1
        )
        from_above = shift(
            jnp.concatenate([t_below[:small], plus(t_below[small:], relay_down)], axis=0),
            inner,
            -1,
        )
        finished.append(plus(own, from_below, from_above).reshape(dp_count, CAP, width))
    back = lax.all_to_all(
        jnp.concatenate(finished, axis=1), "dp", split_axis=0, concat_axis=0, tiled=True
    ).reshape(window * CAP, width)

    half = (KVW - LATENT) // 2
    freq = 10000.0 ** (-jnp.arange(half, dtype=jnp.float32) / half)
    angle = kv_lengths.astype(jnp.float32)[:, None] * freq[None, :]
    return tuple(
        tail(
            hidden_in,
            back,
            kv_gain,
            jnp.cos(angle),
            jnp.sin(angle),
            top,
            total,
            place_weight,
            w_all,
            queries,
            cached,
        )
    )


def solution(mesh):
    return jax.shard_map(
        body,
        mesh=mesh,
        in_specs=(
            P(("dp", "expert"), None),
            P(),
            P(("dp", "expert"), None),
            P(("dp", "expert"), None),
            P("dp", None, "expert"),
            P("dp", None, "expert"),
            P("dp", "expert", None),
            P(("dp", "expert"), None),
            P(),
            P(("dp", "expert"), None),
            P(("dp", "expert"), None),
            P(("dp", "expert"), None),
            P(("dp", "expert")),
            P("dp", "expert", None, None),
        ),
        out_specs=(P(("dp", "expert"), None), P(("dp", "expert"), None)),
        check_vma=False,
    )
```

```python
import functools

import jax
import jax.numpy as jnp
from jax import lax
from jax.experimental import pallas as pl
from jax.experimental.pallas import tpu as pltpu
from jax.sharding import PartitionSpec as P

HEADS = 64
LATENT = 512
PAGE = 16
MAXP = 6
CAP = 4
MCAP = 4
KVW = 576
SIDE = 4

softmax_scale = 192.0 ** (-0.5)
routed_scale = 2.5
norm_eps = 1e-06
MIB = 1 << 20


def rms_rows(values, gain):
    stat = jnp.mean(values * values, axis=-1, keepdims=True)
    return values * lax.rsqrt(stat + norm_eps) * gain


def shift(value, axis, step):
    pairs = []
    for x in range(SIDE):
        for z in range(SIDE):
            to_x = (x + step) % SIDE if axis == "x" else x
            to_z = (z + step) % SIDE if axis == "z" else z
            pairs.append((x * SIDE + z, to_x * SIDE + to_z))
    return lax.ppermute(value, "expert", pairs)


def ffn_kernel(expert, count, rows, parts, *refs):
    xs = refs[:count]
    gate_hbm, up_hbm, down_hbm = refs[count : count + 3]
    outs = refs[count + 3 : 2 * count + 3]
    x_buf, w_buf, d_buf, o_buf, acc, in_sem, d_sem, out_sem = refs[2 * count + 3 :]
    depth = gate_hbm.shape[1]
    piece = depth // parts

    def loads(c):
        cut = pl.ds(pl.multiple_of(c * piece, piece), piece)
        yield pltpu.make_async_copy(
            gate_hbm.at[expert, cut], w_buf.at[cut, pl.ds(0, 128)], in_sem.at[c, 0]
        )
        yield pltpu.make_async_copy(
            up_hbm.at[expert, cut], w_buf.at[cut, pl.ds(128, 128)], in_sem.at[c, 1]
        )
        at = 0
        for i in range(count):
            yield pltpu.make_async_copy(
                xs[i].at[:, cut], x_buf.at[pl.ds(at, rows[i]), cut], in_sem.at[c, 2 + i]
            )
            at += rows[i]

    def stores(c):
        cut = pl.ds(pl.multiple_of(c * piece, piece), piece)
        at = 0
        for i in range(count):
            yield pltpu.make_async_copy(
                o_buf.at[pl.ds(at, rows[i]), cut], outs[i].at[:, cut], out_sem.at[c, i]
            )
            at += rows[i]

    for c in range(parts):
        for copy in loads(c):
            copy.start()
    down = pltpu.make_async_copy(down_hbm.at[expert], d_buf, d_sem)
    down.start()
    acc[...] = jnp.zeros_like(acc)

    @pl.loop(0, parts)
    def _(c):
        for copy in loads(c):
            copy.wait()
        cut = pl.ds(pl.multiple_of(c * piece, piece), piece)
        acc[...] += jnp.dot(x_buf[:, cut], w_buf[cut, :], preferred_element_type=jnp.float32)

    gate = acc[:, :128]
    active = (gate / (1.0 + jnp.exp(-gate)) * acc[:, 128:]).astype(jnp.bfloat16)
    down.wait()

    @pl.loop(0, parts)
    def _(c):
        cut = pl.ds(pl.multiple_of(c * piece, piece), piece)
        o_buf[:, cut] = jnp.dot(active, d_buf[:, cut], preferred_element_type=jnp.float32).astype(
            jnp.bfloat16
        )
        for copy in stores(c):
            copy.start()

    @pl.loop(0, parts)
    def _(c):
        for copy in stores(c):
            copy.wait()


def ffn(blocks, expert, w_gate, w_up, w_down):
    rows = tuple(block.shape[0] for block in blocks)
    count, total, depth, parts = len(rows), sum(rows), w_gate.shape[1], 4
    return pl.pallas_call(
        functools.partial(ffn_kernel, expert, count, rows, parts),
        out_shape=[jax.ShapeDtypeStruct(block.shape, jnp.bfloat16) for block in blocks],
        in_specs=[pl.BlockSpec(memory_space=pl.ANY)] * (count + 3),
        out_specs=[pl.BlockSpec(memory_space=pl.ANY)] * count,
        scratch_shapes=[
            pltpu.VMEM((total, depth), jnp.bfloat16),
            pltpu.VMEM((depth, 256), jnp.bfloat16),
            pltpu.VMEM((128, depth), jnp.bfloat16),
            pltpu.VMEM((total, depth), jnp.bfloat16),
            pltpu.VMEM((total, 256), jnp.float32),
            pltpu.SemaphoreType.DMA((parts, 2 + count)),
            pltpu.SemaphoreType.DMA,
            pltpu.SemaphoreType.DMA((parts, count)),
        ],
        compiler_params=pltpu.CompilerParams(vmem_limit_bytes=58 * MIB),
        cost_estimate=pl.CostEstimate(
            flops=2 * total * depth * 384,
            bytes_accessed=2 * depth * (384 + 2 * total),
            transcendentals=total * 128,
        ),
        name="ffn",
    )(*blocks, w_gate, w_up, w_down)


def attend_kernel(
    step, table, lengths, q_ref, pool_ref, more_ref, out_ref, top_ref, total_ref, wide, pages, q_buf, o_buf
):
    pair = 2 * KVW

    def split(chunk):
        chunk = chunk.astype(jnp.float32)
        return chunk[:, :640], pltpu.roll(chunk[:, 512:], KVW, 1)

    def spread(target, value, start, stride):
        for i in range(5):
            target[i, pl.ds(start, value.shape[0], stride=stride), :] = value[
                :, 128 * i : 128 * (i + 1)
            ]

    def joined(source, rows):
        lanes = [source[i, rows, :] for i in range(4)] + [source[4, rows, : KVW - LATENT]]
        return jnp.concatenate(lanes, axis=1).astype(jnp.bfloat16)

    @pl.when(pl.program_id(0) == 0)
    def _():
        for source, base in ((pool_ref, 0), (more_ref, pool_ref.shape[0])):

            @pl.loop(0, source.shape[0] // 16)
            def _(b):
                rows = pl.ds(pl.multiple_of(b * 16, 16), 16)
                for u in range(PAGE // 2):
                    even, odd = split(source[rows, pair * u : pair * (u + 1)])
                    spread(wide, even, 2 * u, PAGE)
                    spread(wide, odd, 2 * u + 1, PAGE)
                pages[pl.ds(pl.multiple_of((base + b * 16) * PAGE, 256), 256), :] = joined(
                    wide, slice(None)
                )

    @pl.loop(0, HEADS // 2, unroll=4)
    def _(u):
        even, odd = split(q_ref[:, pl.ds(pl.multiple_of(u * pair, 128), pair)])
        spread(q_buf, even, 2 * u, HEADS)
        spread(q_buf, odd, 2 * u + 1, HEADS)

    first = pl.program_id(0) * step
    for r in range(step):
        row = first + r
        keys = jnp.concatenate(
            [
                pages[pl.ds(pl.multiple_of(table[row * MAXP + p] * PAGE, PAGE), PAGE), :]
                for p in range(MAXP)
            ],
            axis=0,
        )
        query = joined(q_buf, slice(r * HEADS, (r + 1) * HEADS))
        scores = (
            lax.dot_general(
                keys, query, (((1,), (1,)), ((), ())), preferred_element_type=jnp.float32
            )
            * softmax_scale
        )
        valid = lax.broadcasted_iota(jnp.int32, scores.shape, 0) < lengths[row]
        scores = jnp.where(valid, scores, -1e30)
        top = jnp.max(scores, axis=0, keepdims=True)
        expo = jnp.where(valid, jnp.exp(scores - top), 0.0)
        total = jnp.sum(expo, axis=0, keepdims=True)
        probs = (expo / total).astype(jnp.bfloat16)
        result = lax.dot_general(
            probs, keys[:, :LATENT], (((0,), (0,)), ((), ())), preferred_element_type=jnp.float32
        )
        for i in range(4):
            o_buf[i, r * HEADS : (r + 1) * HEADS, :] = result[:, 128 * i : 128 * (i + 1)]
        top_ref[r : r + 1, :] = top
        total_ref[r : r + 1, :] = total

    @pl.loop(0, HEADS, unroll=4)
    def _(h):
        for i in range(4):
            out_ref[:, pl.ds(pl.multiple_of(h * LATENT + 128 * i, 128), 128)] = o_buf[
                i, pl.ds(h, step, stride=HEADS), :
            ].astype(jnp.bfloat16)


def attend_cached(queries, pool, more, page_table, kv_lengths):
    rows, step = queries.shape[0], 16
    entries = (pool.shape[0] + more.shape[0]) * PAGE
    whole = lambda i, t, n: (0, 0)
    block = lambda i, t, n: (i, 0)
    return pl.pallas_call(
        functools.partial(attend_kernel, step),
        out_shape=[
            jax.ShapeDtypeStruct((rows, HEADS * LATENT), jnp.bfloat16),
            jax.ShapeDtypeStruct((rows, HEADS), jnp.float32),
            jax.ShapeDtypeStruct((rows, HEADS), jnp.float32),
        ],
        grid_spec=pltpu.PrefetchScalarGridSpec(
            num_scalar_prefetch=2,
            grid=(rows // step,),
            in_specs=[
                pl.BlockSpec((step, queries.shape[1]), block),
                pl.BlockSpec(pool.shape, whole),
                pl.BlockSpec(more.shape, whole),
            ],
            out_specs=[
                pl.BlockSpec((step, HEADS * LATENT), block),
                pl.BlockSpec((step, HEADS), block),
                pl.BlockSpec((step, HEADS), block),
            ],
            scratch_shapes=[
                pltpu.VMEM((5, 16 * PAGE, 128), jnp.float32),
                pltpu.VMEM((entries, KVW), jnp.bfloat16),
                pltpu.VMEM((5, step * HEADS, 128), jnp.float32),
                pltpu.VMEM((4, step * HEADS, 128), jnp.float32),
            ],
        ),
        compiler_params=pltpu.CompilerParams(vmem_limit_bytes=58 * MIB),
        cost_estimate=pl.CostEstimate(
            flops=2 * rows * HEADS * MAXP * PAGE * (KVW + LATENT),
            bytes_accessed=2 * (queries.size + entries * KVW + rows * HEADS * LATENT),
            transcendentals=rows * HEADS * MAXP * PAGE,
        ),
        name="attend_cached",
    )(page_table.reshape(rows * MAXP), kv_lengths, queries, pool, more)


def pack_kernel(own, below, above, far, low, high, sem):
    n = own.shape[0]
    copies = [
        pltpu.make_async_copy(source, target.at[pl.ds(at, n)], sem.at[i])
        for i, (source, target, at) in enumerate(
            ((own, low, 0), (below, low, n), (above, high, 0), (far, high, n))
        )
    ]
    for copy in copies:
        copy.start()
    for copy in copies:
        copy.wait()


def pack(own, below, above, far):
    shape = jax.ShapeDtypeStruct((2 * own.shape[0], own.shape[1]), own.dtype)
    hbm = pl.BlockSpec(memory_space=pl.ANY)
    return pl.pallas_call(
        pack_kernel,
        out_shape=[shape, shape],
        in_specs=[hbm] * 4,
        out_specs=[hbm] * 2,
        scratch_shapes=[pltpu.SemaphoreType.DMA((4,))],
        compiler_params=pltpu.CompilerParams(vmem_limit_bytes=58 * MIB),
        cost_estimate=pl.CostEstimate(
            flops=0, bytes_accessed=16 * own.size, transcendentals=0
        ),
        name="pack",
    )(own, below, above, far)


def tail_kernel(
    parts,
    hidden_ref,
    back_ref,
    gain_ref,
    cos_ref,
    sin_ref,
    top_ref,
    total_ref,
    place_ref,
    w_hbm,
    q_hbm,
    o_hbm,
    hidden_out_ref,
    out_ref,
    w_buf,
    q_buf,
    o_buf,
    key_buf,
    own_buf,
    keep_buf,
    w_sem,
    q_sem,
    o_sem,
):
    width = hidden_ref.shape[1]
    piece = width // parts
    q_piece = q_hbm.shape[1] // parts_q
    o_piece = o_hbm.shape[1] // parts_q
    w_loads, q_loads, o_loads = [], [], []
    for c in range(parts):
        cut = pl.ds(c * piece, piece)
        w_loads.append(pltpu.make_async_copy(w_hbm.at[cut], w_buf.at[cut], w_sem.at[c]))
    for c in range(parts_q):
        cut = pl.ds(c * q_piece, q_piece)
        q_loads.append(pltpu.make_async_copy(q_hbm.at[:, cut], q_buf.at[:, cut], q_sem.at[c]))
        cut = pl.ds(c * o_piece, o_piece)
        o_loads.append(pltpu.make_async_copy(o_hbm.at[:, cut], o_buf.at[:, cut], o_sem.at[c]))
    for copy in w_loads + q_loads + o_loads:
        copy.start()
    place = place_ref[...]
    pick = (place != 0.0).astype(jnp.bfloat16)
    weight = jnp.sum(place, axis=1, keepdims=True)
    projected = jnp.zeros((hidden_ref.shape[0], KVW), jnp.float32)
    for c in range(parts):
        cut = slice(c * piece, (c + 1) * piece)
        picked = jnp.dot(pick, back_ref[:, cut], preferred_element_type=jnp.float32)
        hidden = (hidden_ref[:, cut].astype(jnp.float32) + weight * picked).astype(jnp.bfloat16)
        hidden_out_ref[:, cut] = hidden
        w_loads[c].wait()
        projected += jnp.dot(hidden, w_buf[cut, :], preferred_element_type=jnp.float32)
    latent = rms_rows(projected[:, :LATENT], gain_ref[...])
    first = projected[:, LATENT : LATENT + 32]
    second = projected[:, LATENT + 32 :]
    cosine, sine = cos_ref[...], sin_ref[...]
    new_key = jnp.concatenate(
        [latent, first * cosine - second * sine, second * cosine + first * sine], axis=1
    )
    new_key = new_key.astype(jnp.bfloat16).astype(jnp.float32)
    key_buf[...] = jnp.concatenate([new_key, new_key], axis=1)
    lane = lax.broadcasted_iota(jnp.int32, (8, 128), 1)
    head = lax.broadcasted_iota(jnp.int32, (8, HEADS), 1)
    blocks = hidden_ref.shape[0] // 8
    own_buf[...] = jnp.zeros_like(own_buf)
    for copy in q_loads:
        copy.wait()

    @pl.loop(0, HEADS // 2)
    def _(j):
        for b in range(blocks):
            rows = slice(8 * b, 8 * b + 8)
            cut = pl.ds(pl.multiple_of(j * 2 * KVW, 2 * KVW), 2 * KVW)
            product = q_buf[rows, cut].astype(jnp.float32) * key_buf[rows, :]
            tiles = [product[:, 128 * i : 128 * (i + 1)] for i in range(9)]
            low = tiles[0] + tiles[1] + tiles[2] + tiles[3] + jnp.where(lane < 64, tiles[4], 0.0)
            high = tiles[5] + tiles[6] + tiles[7] + tiles[8] + jnp.where(lane < 64, 0.0, tiles[4])
            low = jnp.sum(low, axis=1, keepdims=True)
            high = jnp.sum(high, axis=1, keepdims=True)
            own_buf[rows, :] += jnp.where(head == 2 * j, low, 0.0) + jnp.where(
                head == 2 * j + 1, high, 0.0
            )

    own = own_buf[...] * softmax_scale
    top_old = top_ref[...]
    top = jnp.maximum(top_old, own)
    part = total_ref[...] * jnp.exp(top_old - top)
    part_own = jnp.exp(own - top)
    inverse = 1.0 / (part + part_own)
    keep_buf[...] = part * inverse
    own_buf[...] = (part_own * inverse).astype(jnp.bfloat16).astype(jnp.float32)
    for copy in o_loads:
        copy.wait()

    @pl.loop(0, HEADS)
    def _(h):
        for b in range(blocks):
            rows = slice(8 * b, 8 * b + 8)
            keep = jnp.sum(jnp.where(head == h, keep_buf[rows, :], 0.0), axis=1, keepdims=True)
            add = jnp.sum(jnp.where(head == h, own_buf[rows, :], 0.0), axis=1, keepdims=True)
            cut = pl.ds(pl.multiple_of(h * LATENT, LATENT), LATENT)
            out_ref[rows, cut] = (
                o_buf[rows, cut].astype(jnp.float32) * keep + add * key_buf[rows, :LATENT]
            ).astype(jnp.bfloat16)


parts_q = 4


def tail(hidden_in, back, kv_gain, cosine, sine, top, total, place_weight, w_all, queries, o):
    rows, width = hidden_in.shape
    parts = 7
    vmem = pl.BlockSpec(memory_space=pltpu.VMEM)
    hbm = pl.BlockSpec(memory_space=pl.ANY)
    return pl.pallas_call(
        functools.partial(tail_kernel, parts),
        out_shape=[
            jax.ShapeDtypeStruct((rows, width), jnp.bfloat16),
            jax.ShapeDtypeStruct((rows, HEADS * LATENT), jnp.bfloat16),
        ],
        in_specs=[vmem] * 8 + [hbm] * 3,
        out_specs=[vmem] * 2,
        scratch_shapes=[
            pltpu.VMEM(w_all.shape, jnp.bfloat16),
            pltpu.VMEM(queries.shape, jnp.bfloat16),
            pltpu.VMEM(o.shape, jnp.bfloat16),
            pltpu.VMEM((rows, 2 * KVW), jnp.float32),
            pltpu.VMEM((rows, HEADS), jnp.float32),
            pltpu.VMEM((rows, HEADS), jnp.float32),
            pltpu.SemaphoreType.DMA((parts,)),
            pltpu.SemaphoreType.DMA((parts_q,)),
            pltpu.SemaphoreType.DMA((parts_q,)),
        ],
        compiler_params=pltpu.CompilerParams(vmem_limit_bytes=48 * MIB),
        cost_estimate=pl.CostEstimate(
            flops=2 * rows * width * KVW,
            bytes_accessed=2 * (w_all.size + queries.size + 2 * o.size),
            transcendentals=rows * HEADS * 2,
        ),
        name="tail",
    )(
        hidden_in,
        back,
        kv_gain.reshape(1, LATENT),
        cosine,
        sine,
        top,
        total,
        place_weight,
        w_all,
        queries,
        o,
    )


def plus(*terms):
    total = terms[0].astype(jnp.float32)
    for term in terms[1:]:
        total = total + term.astype(jnp.float32)
    return total.astype(jnp.bfloat16)


def after(values, *others):
    return lax.optimization_barrier((values, others))[0]


def body(
    hidden_in,
    norm_gain,
    route_logits,
    expert_ids,
    w_gate,
    w_up,
    w_down,
    w_latent,
    kv_gain,
    queries,
    page_pool,
    page_table,
    kv_lengths,
    migration,
):
    dp_count = lax.axis_size("dp")
    ex_count = lax.axis_size("expert")
    row_count = hidden_in.shape[0]
    local_experts = w_gate.shape[0]
    window = local_experts * dp_count
    width = hidden_in.shape[1]
    x_wide = hidden_in.astype(jnp.float32)
    normed = rms_rows(x_wide, norm_gain).astype(jnp.bfloat16)
    in_window = expert_ids < window
    has = jnp.any(in_window, axis=1)
    chosen = jnp.sum(jnp.where(in_window, expert_ids, 0), axis=1)
    sigma = jax.nn.sigmoid(route_logits)
    weight = (
        routed_scale * jnp.sum(jnp.where(in_window, sigma, 0.0), axis=1) / jnp.sum(sigma, axis=1)
    )
    onehot = ((chosen[:, None] == jnp.arange(window)[None, :]) & has[:, None]).astype(jnp.int32)
    rank = jnp.cumsum(onehot, axis=0) - onehot
    slot = jnp.sum(rank * onehot, axis=1)
    slots = local_experts * CAP
    place = chosen * CAP + slot
    pick = (place[:, None] == jnp.arange(window * CAP)[None, :]) & has[:, None]
    packed = jnp.einsum(
        "rs,rd->sd", pick.astype(jnp.bfloat16), normed, preferred_element_type=jnp.float32
    ).astype(jnp.bfloat16)
    place_weight = jnp.where(pick, weight[:, None], 0.0)
    arrived = lax.all_to_all(
        packed.reshape(dp_count, slots, width), "dp", split_axis=0, concat_axis=0, tiled=True
    )
    outgoing = jnp.take(page_pool, migration.reshape(dp_count * MCAP), axis=0, mode="clip")
    arrived = after(arrived, outgoing)
    axes = (("z", "x"), ("x", "z"))
    both = range(local_experts)
    rows = [
        arrived[:, k * CAP : (k + 1) * CAP].reshape(dp_count * CAP, width) for k in both
    ]

    incoming = lax.all_to_all(
        outgoing.reshape(dp_count, MCAP, page_pool.shape[1]),
        "dp",
        split_axis=0,
        concat_axis=0,
        tiled=True,
    ).reshape(dp_count * MCAP, page_pool.shape[1])
    below = [shift(rows[k], axes[k][0], 1) for k in both]
    above = [shift(rows[k], axes[k][0], -1) for k in both]
    below, above = after((below, above))
    beyond = [shift(below[k], axes[k][0], 1) for k in both]
    beyond = after(beyond)
    low, high = zip(*(pack(rows[k], below[k], above[k], beyond[k]) for k in both))
    low, high = after((low, high))
    below_low = [shift(low[k], axes[k][1], 1) for k in both]
    above_high = [shift(high[k], axes[k][1], -1) for k in both]
    below_high = [shift(high[k], axes[k][1], 1) for k in both]
    above_low = [shift(low[k], axes[k][1], -1) for k in both]
    query, pool = after((queries, page_pool), low, high)
    cached, top, total = attend_cached(query, pool, incoming, page_table, kv_lengths)
    w_local = after(w_latent, cached)
    spread = lax.all_to_all(
        jnp.broadcast_to(w_local[None], (ex_count,) + w_latent.shape),
        "expert",
        split_axis=0,
        concat_axis=0,
        tiled=True,
    )
    below_low, above_high = after((below_low, above_high), cached)
    far_low = [shift(below_low[k], axes[k][1], 1) for k in both]
    far_high = [shift(above_high[k], axes[k][1], -1) for k in both]
    w_all = lax.all_gather(
        spread.reshape(ex_count * w_latent.shape[0], KVW), "dp", axis=0, tiled=True
    )
    weights = (w_gate, w_up, w_down)
    y_own = [ffn([low[k], high[k]], k, *weights) for k in both]
    below_high, above_low = after((below_high, above_low), y_own)
    y_side = [
        ffn([below_low[k], below_high[k], above_low[k], above_high[k]], k, *weights) for k in both
    ]
    early_up = [shift(y_side[k][3], axes[k][1], 1) for k in both]
    early_down = [shift(y_side[k][0], axes[k][1], -1) for k in both]
    far_low, far_high = after((far_low, far_high), y_side, spread)
    y_far = [ffn([far_low[k], far_high[k]], k, *weights) for k in both]
    relay_up = [shift(y_far[k][0], axes[k][1], 1) for k in both]
    relay_down = [shift(y_far[k][1], axes[k][1], -1) for k in both]
    early_up, early_down, relay_up, relay_down = after((early_up, early_down, relay_up, relay_down))
    late_up = [shift(plus(y_side[k][2], relay_up[k]), axes[k][1], 1) for k in both]
    late_down = [shift(plus(y_side[k][1], relay_down[k]), axes[k][1], -1) for k in both]
    late_up, late_down = after((late_up, late_down), w_all)
    n = rows[0].shape[0]
    terms_low = [(y_own[k][0], late_up[k], early_down[k]) for k in both]
    terms_high = [(y_own[k][1], early_up[k], late_down[k]) for k in both]
    for_far = [plus(*(term[n:] for term in terms_high[k])) for k in both]
    for_below = [plus(*(term[n:] for term in terms_low[k])) for k in both]
    relayed = [shift(for_far[k], axes[k][0], 1) for k in both]
    from_above = [shift(for_below[k], axes[k][0], -1) for k in both]
    relayed, from_above = after((relayed, from_above))
    from_below = [
        shift(plus(*(term[:n] for term in terms_high[k]), relayed[k]), axes[k][0], 1) for k in both
    ]
    from_below = after(from_below)
    finished = [
        plus(*(term[:n] for term in terms_low[k]), from_below[k], from_above[k]).reshape(
            dp_count, CAP, width
        )
        for k in both
    ]
    back = lax.all_to_all(
        jnp.concatenate(finished, axis=1), "dp", split_axis=0, concat_axis=0, tiled=True
    ).reshape(window * CAP, width)

    half = (KVW - LATENT) // 2
    freq = 10000.0 ** (-jnp.arange(half, dtype=jnp.float32) / half)
    angle = kv_lengths.astype(jnp.float32)[:, None] * freq[None, :]
    return tuple(
        tail(
            hidden_in,
            back,
            kv_gain,
            jnp.cos(angle),
            jnp.sin(angle),
            top,
            total,
            place_weight,
            w_all,
            queries,
            cached,
        )
    )


def solution(mesh):
    return jax.shard_map(
        body,
        mesh=mesh,
        in_specs=(
            P(("dp", "expert"), None),
            P(),
            P(("dp", "expert"), None),
            P(("dp", "expert"), None),
            P("dp", None, "expert"),
            P("dp", None, "expert"),
            P("dp", "expert", None),
            P(("dp", "expert"), None),
            P(),
            P(("dp", "expert"), None),
            P(("dp", "expert"), None),
            P(("dp", "expert"), None),
            P(("dp", "expert")),
            P("dp", "expert", None, None),
        ),
        out_specs=(P(("dp", "expert"), None), P(("dp", "expert"), None)),
        check_vma=False,
    )
```

```python
import functools

import jax
import jax.numpy as jnp
from jax import lax
from jax.experimental import pallas as pl
from jax.experimental.pallas import tpu as pltpu
from jax.sharding import PartitionSpec as P

HEADS = 64
LATENT = 512
PAGE = 16
MAXP = 6
CAP = 4
MCAP = 4
KVW = 576
SIDE = 4

softmax_scale = 192.0 ** (-0.5)
routed_scale = 2.5
norm_eps = 1e-06
MIB = 1 << 20


def rms_rows(values, gain):
    stat = jnp.mean(values * values, axis=-1, keepdims=True)
    return values * lax.rsqrt(stat + norm_eps) * gain


def shift(value, axis, step):
    pairs = []
    for x in range(SIDE):
        for z in range(SIDE):
            to_x = (x + step) % SIDE if axis == "x" else x
            to_z = (z + step) % SIDE if axis == "z" else z
            pairs.append((x * SIDE + z, to_x * SIDE + to_z))
    return lax.ppermute(value, "expert", pairs)


def ffn_kernel(count, rows, parts, *refs):
    experts = 2
    xs = refs[: experts * count]
    gate_hbm, up_hbm, down_hbm = refs[experts * count : experts * count + 3]
    outs = refs[experts * count + 3 : 2 * experts * count + 3]
    x_buf, w_buf, d_buf, o_buf, acc, in_sem, d_sem, out_sem = refs[2 * experts * count + 3 :]
    depth = gate_hbm.shape[1]
    piece = depth // parts

    def loads(e, c):
        cut = pl.ds(pl.multiple_of(c * piece, piece), piece)
        yield pltpu.make_async_copy(
            gate_hbm.at[e, cut], w_buf.at[e, cut, pl.ds(0, 128)], in_sem.at[e, c, 0]
        )
        yield pltpu.make_async_copy(
            up_hbm.at[e, cut], w_buf.at[e, cut, pl.ds(128, 128)], in_sem.at[e, c, 1]
        )
        for i in range(count):
            yield pltpu.make_async_copy(
                xs[e * count + i].at[:, cut],
                x_buf.at[e, pl.ds(i * rows, rows), cut],
                in_sem.at[e, c, 2 + i],
            )

    def stores(e, c):
        cut = pl.ds(pl.multiple_of(c * piece, piece), piece)
        for i in range(count):
            yield pltpu.make_async_copy(
                o_buf.at[e, pl.ds(i * rows, rows), cut],
                outs[e * count + i].at[:, cut],
                out_sem.at[e, c, i],
            )

    down = []
    for e in range(experts):
        for c in range(parts):
            for copy in loads(e, c):
                copy.start()
        down.append(pltpu.make_async_copy(down_hbm.at[e], d_buf.at[e], d_sem.at[e]))
        down[e].start()
    for e in range(experts):
        acc[...] = jnp.zeros_like(acc)

        @pl.loop(0, parts)
        def _(c):
            for copy in loads(e, c):
                copy.wait()
            cut = pl.ds(pl.multiple_of(c * piece, piece), piece)
            acc[...] += jnp.dot(
                x_buf[e, :, cut], w_buf[e, cut, :], preferred_element_type=jnp.float32
            )

        gate = acc[:, :128]
        active = (gate / (1.0 + jnp.exp(-gate)) * acc[:, 128:]).astype(jnp.bfloat16)
        down[e].wait()

        @pl.loop(0, parts)
        def _(c):
            cut = pl.ds(pl.multiple_of(c * piece, piece), piece)
            o_buf[e, :, cut] = jnp.dot(
                active, d_buf[e, :, cut], preferred_element_type=jnp.float32
            ).astype(jnp.bfloat16)
            for copy in stores(e, c):
                copy.start()

    for e in range(experts):

        @pl.loop(0, parts)
        def _(c):
            for copy in stores(e, c):
                copy.wait()


def ffn(blocks, w_gate, w_up, w_down):
    experts, count = len(blocks), len(blocks[0])
    flat = [block for part in blocks for block in part]
    rows, depth, parts = flat[0].shape[0], w_gate.shape[1], 7
    total = rows * count
    done = pl.pallas_call(
        functools.partial(ffn_kernel, count, rows, parts),
        out_shape=[jax.ShapeDtypeStruct(block.shape, jnp.bfloat16) for block in flat],
        in_specs=[pl.BlockSpec(memory_space=pl.ANY)] * (len(flat) + 3),
        out_specs=[pl.BlockSpec(memory_space=pl.ANY)] * len(flat),
        scratch_shapes=[
            pltpu.VMEM((experts, total, depth), jnp.bfloat16),
            pltpu.VMEM((experts, depth, 256), jnp.bfloat16),
            pltpu.VMEM((experts, 128, depth), jnp.bfloat16),
            pltpu.VMEM((experts, total, depth), jnp.bfloat16),
            pltpu.VMEM((total, 256), jnp.float32),
            pltpu.SemaphoreType.DMA((experts, parts, 2 + count)),
            pltpu.SemaphoreType.DMA((experts,)),
            pltpu.SemaphoreType.DMA((experts, parts, count)),
        ],
        compiler_params=pltpu.CompilerParams(vmem_limit_bytes=58 * MIB),
        cost_estimate=pl.CostEstimate(
            flops=2 * experts * total * depth * 384,
            bytes_accessed=2 * experts * depth * (384 + 2 * total),
            transcendentals=experts * total * 128,
        ),
        name="ffn",
    )(*flat, w_gate, w_up, w_down)
    return [done[e * count : (e + 1) * count] for e in range(experts)]


def attend_kernel(
    step, table, lengths, q_ref, pool_hbm, more_hbm, out_ref, top_ref, total_ref, pages, sem
):
    own_pages = pool_hbm.shape[0]

    @pl.when(pl.program_id(0) == 0)
    def _():
        copies = [
            pltpu.make_async_copy(pool_hbm, pages.at[pl.ds(0, own_pages)], sem.at[0]),
            pltpu.make_async_copy(
                more_hbm, pages.at[pl.ds(own_pages, more_hbm.shape[0])], sem.at[1]
            ),
        ]
        for copy in copies:
            copy.start()
        for copy in copies:
            copy.wait()

    first = pl.program_id(0) * step
    keys = [
        jnp.concatenate([pages[table[(first + r) * MAXP + p]] for p in range(MAXP)], axis=0)
        for r in range(step)
    ]
    scores = jnp.concatenate(
        [
            lax.dot_general(
                keys[r], q_ref[r], (((1,), (1,)), ((), ())), preferred_element_type=jnp.float32
            )
            for r in range(step)
        ],
        axis=1,
    )
    scores = scores * softmax_scale
    column = lax.broadcasted_iota(jnp.int32, (1, step * HEADS), 1) // HEADS
    length = jnp.zeros_like(column)
    for r in range(step):
        length = jnp.where(column == r, lengths[first + r], length)
    valid = lax.broadcasted_iota(jnp.int32, scores.shape, 0) < length
    scores = jnp.where(valid, scores, -1e30)
    top = jnp.max(scores, axis=0, keepdims=True)
    expo = jnp.where(valid, jnp.exp(scores - top), 0.0)
    total = jnp.sum(expo, axis=0, keepdims=True)
    probs = (expo / total).astype(jnp.bfloat16)
    for r in range(step):
        cut = slice(r * HEADS, (r + 1) * HEADS)
        out_ref[r] = lax.dot_general(
            probs[:, cut],
            keys[r][:, :LATENT],
            (((0,), (0,)), ((), ())),
            preferred_element_type=jnp.float32,
        ).astype(jnp.bfloat16)
        top_ref[r : r + 1, :] = top[:, cut]
        total_ref[r : r + 1, :] = total[:, cut]


def attend_cached(query, pool, more, page_table, kv_lengths):
    rows, step = query.shape[0], 8
    entries = pool.shape[0] + more.shape[0]
    hbm = pl.BlockSpec(memory_space=pl.ANY)
    return pl.pallas_call(
        functools.partial(attend_kernel, step),
        out_shape=[
            jax.ShapeDtypeStruct((rows, HEADS, LATENT), jnp.bfloat16),
            jax.ShapeDtypeStruct((rows, HEADS), jnp.float32),
            jax.ShapeDtypeStruct((rows, HEADS), jnp.float32),
        ],
        grid_spec=pltpu.PrefetchScalarGridSpec(
            num_scalar_prefetch=2,
            grid=(rows // step,),
            in_specs=[pl.BlockSpec((step, HEADS, KVW), lambda i, t, n: (i, 0, 0)), hbm, hbm],
            out_specs=[
                pl.BlockSpec((step, HEADS, LATENT), lambda i, t, n: (i, 0, 0)),
                pl.BlockSpec((step, HEADS), lambda i, t, n: (i, 0)),
                pl.BlockSpec((step, HEADS), lambda i, t, n: (i, 0)),
            ],
            scratch_shapes=[
                pltpu.VMEM((entries, PAGE, KVW), jnp.bfloat16),
                pltpu.SemaphoreType.DMA((2,)),
            ],
        ),
        compiler_params=pltpu.CompilerParams(vmem_limit_bytes=58 * MIB),
        cost_estimate=pl.CostEstimate(
            flops=2 * rows * HEADS * MAXP * PAGE * (KVW + LATENT),
            bytes_accessed=2 * (query.size + entries * PAGE * KVW + rows * HEADS * LATENT),
            transcendentals=rows * HEADS * MAXP * PAGE,
        ),
        name="attend_cached",
    )(page_table.reshape(rows * MAXP), kv_lengths, query, pool, more)


def pack_kernel(count, *refs):
    blocks, halves = refs[: 4 * count], refs[4 * count : 6 * count]
    buf, in_sem, out_sem = refs[6 * count :]
    n = blocks[0].shape[0]
    loads = [
        pltpu.make_async_copy(blocks[i], buf.at[i // 2, pl.ds(i % 2 * n, n)], in_sem.at[i])
        for i in range(4 * count)
    ]
    stores = [
        pltpu.make_async_copy(buf.at[i], halves[i], out_sem.at[i]) for i in range(2 * count)
    ]
    for copy in loads:
        copy.start()
    for i in range(2 * count):
        loads[2 * i].wait()
        loads[2 * i + 1].wait()
        stores[i].start()
    for copy in stores:
        copy.wait()


def pack(groups):
    count, (n, width) = len(groups), groups[0][0].shape
    hbm = pl.BlockSpec(memory_space=pl.ANY)
    done = pl.pallas_call(
        functools.partial(pack_kernel, count),
        out_shape=[jax.ShapeDtypeStruct((2 * n, width), jnp.bfloat16)] * (2 * count),
        in_specs=[hbm] * (4 * count),
        out_specs=[hbm] * (2 * count),
        scratch_shapes=[
            pltpu.VMEM((2 * count, 2 * n, width), jnp.bfloat16),
            pltpu.SemaphoreType.DMA((4 * count,)),
            pltpu.SemaphoreType.DMA((2 * count,)),
        ],
        compiler_params=pltpu.CompilerParams(vmem_limit_bytes=58 * MIB),
        cost_estimate=pl.CostEstimate(
            flops=0, bytes_accessed=16 * count * n * width, transcendentals=0
        ),
        name="pack",
    )(*(block for group in groups for block in group))
    return done[0::2], done[1::2]


def tail_kernel(
    parts,
    hidden_ref,
    back_ref,
    gain_ref,
    cos_ref,
    sin_ref,
    top_ref,
    total_ref,
    place_ref,
    w_hbm,
    q_hbm,
    o_hbm,
    hidden_out_ref,
    out_ref,
    w_buf,
    q_buf,
    o_buf,
    key_buf,
    own_buf,
    keep_buf,
    w_sem,
    q_sem,
    o_sem,
):
    width = hidden_ref.shape[1]
    piece = width // parts
    q_piece = q_hbm.shape[1] // parts_q
    o_piece = o_hbm.shape[1] // parts_q
    w_loads, q_loads, o_loads = [], [], []
    for c in range(parts):
        cut = pl.ds(c * piece, piece)
        w_loads.append(pltpu.make_async_copy(w_hbm.at[cut], w_buf.at[cut], w_sem.at[c]))
    for c in range(parts_q):
        cut = pl.ds(c * q_piece, q_piece)
        q_loads.append(pltpu.make_async_copy(q_hbm.at[:, cut], q_buf.at[:, cut], q_sem.at[c]))
        cut = pl.ds(c * o_piece, o_piece)
        o_loads.append(pltpu.make_async_copy(o_hbm.at[:, cut], o_buf.at[:, cut], o_sem.at[c]))
    for copy in w_loads + q_loads + o_loads:
        copy.start()
    place = place_ref[...]
    pick = (place != 0.0).astype(jnp.bfloat16)
    weight = jnp.sum(place, axis=1, keepdims=True)
    projected = jnp.zeros((hidden_ref.shape[0], KVW), jnp.float32)
    for c in range(parts):
        cut = slice(c * piece, (c + 1) * piece)
        picked = jnp.dot(pick, back_ref[:, cut], preferred_element_type=jnp.float32)
        hidden = (hidden_ref[:, cut].astype(jnp.float32) + weight * picked).astype(jnp.bfloat16)
        hidden_out_ref[:, cut] = hidden
        w_loads[c].wait()
        projected += jnp.dot(hidden, w_buf[cut, :], preferred_element_type=jnp.float32)
    latent = rms_rows(projected[:, :LATENT], gain_ref[...])
    first = projected[:, LATENT : LATENT + 32]
    second = projected[:, LATENT + 32 :]
    cosine, sine = cos_ref[...], sin_ref[...]
    new_key = jnp.concatenate(
        [latent, first * cosine - second * sine, second * cosine + first * sine], axis=1
    )
    new_key = new_key.astype(jnp.bfloat16).astype(jnp.float32)
    key_buf[...] = jnp.concatenate([new_key, new_key], axis=1)
    lane = lax.broadcasted_iota(jnp.int32, (8, 128), 1)
    head = lax.broadcasted_iota(jnp.int32, (8, HEADS), 1)
    blocks = hidden_ref.shape[0] // 8
    own_buf[...] = jnp.zeros_like(own_buf)
    for copy in q_loads:
        copy.wait()

    @pl.loop(0, HEADS // 2)
    def _(j):
        for b in range(blocks):
            rows = slice(8 * b, 8 * b + 8)
            cut = pl.ds(pl.multiple_of(j * 2 * KVW, 2 * KVW), 2 * KVW)
            product = q_buf[rows, cut].astype(jnp.float32) * key_buf[rows, :]
            tiles = [product[:, 128 * i : 128 * (i + 1)] for i in range(9)]
            low = tiles[0] + tiles[1] + tiles[2] + tiles[3] + jnp.where(lane < 64, tiles[4], 0.0)
            high = tiles[5] + tiles[6] + tiles[7] + tiles[8] + jnp.where(lane < 64, 0.0, tiles[4])
            low = jnp.sum(low, axis=1, keepdims=True)
            high = jnp.sum(high, axis=1, keepdims=True)
            own_buf[rows, :] += jnp.where(head == 2 * j, low, 0.0) + jnp.where(
                head == 2 * j + 1, high, 0.0
            )

    own = own_buf[...] * softmax_scale
    top_old = top_ref[...]
    top = jnp.maximum(top_old, own)
    part = total_ref[...] * jnp.exp(top_old - top)
    part_own = jnp.exp(own - top)
    inverse = 1.0 / (part + part_own)
    keep_buf[...] = part * inverse
    own_buf[...] = (part_own * inverse).astype(jnp.bfloat16).astype(jnp.float32)
    for copy in o_loads:
        copy.wait()

    @pl.loop(0, HEADS)
    def _(h):
        for b in range(blocks):
            rows = slice(8 * b, 8 * b + 8)
            keep = jnp.sum(jnp.where(head == h, keep_buf[rows, :], 0.0), axis=1, keepdims=True)
            add = jnp.sum(jnp.where(head == h, own_buf[rows, :], 0.0), axis=1, keepdims=True)
            cut = pl.ds(pl.multiple_of(h * LATENT, LATENT), LATENT)
            out_ref[rows, cut] = (
                o_buf[rows, cut].astype(jnp.float32) * keep + add * key_buf[rows, :LATENT]
            ).astype(jnp.bfloat16)


parts_q = 4


def tail(hidden_in, back, kv_gain, cosine, sine, top, total, place_weight, w_all, queries, o):
    rows, width = hidden_in.shape
    parts = 7
    vmem = pl.BlockSpec(memory_space=pltpu.VMEM)
    hbm = pl.BlockSpec(memory_space=pl.ANY)
    return pl.pallas_call(
        functools.partial(tail_kernel, parts),
        out_shape=[
            jax.ShapeDtypeStruct((rows, width), jnp.bfloat16),
            jax.ShapeDtypeStruct((rows, HEADS * LATENT), jnp.bfloat16),
        ],
        in_specs=[vmem] * 8 + [hbm] * 3,
        out_specs=[vmem] * 2,
        scratch_shapes=[
            pltpu.VMEM(w_all.shape, jnp.bfloat16),
            pltpu.VMEM(queries.shape, jnp.bfloat16),
            pltpu.VMEM(o.shape, jnp.bfloat16),
            pltpu.VMEM((rows, 2 * KVW), jnp.float32),
            pltpu.VMEM((rows, HEADS), jnp.float32),
            pltpu.VMEM((rows, HEADS), jnp.float32),
            pltpu.SemaphoreType.DMA((parts,)),
            pltpu.SemaphoreType.DMA((parts_q,)),
            pltpu.SemaphoreType.DMA((parts_q,)),
        ],
        compiler_params=pltpu.CompilerParams(vmem_limit_bytes=48 * MIB),
        cost_estimate=pl.CostEstimate(
            flops=2 * rows * width * KVW,
            bytes_accessed=2 * (w_all.size + queries.size + 2 * o.size),
            transcendentals=rows * HEADS * 2,
        ),
        name="tail",
    )(
        hidden_in,
        back,
        kv_gain.reshape(1, LATENT),
        cosine,
        sine,
        top,
        total,
        place_weight,
        w_all,
        queries,
        o,
    )


def plus(*terms):
    total = terms[0].astype(jnp.float32)
    for term in terms[1:]:
        total = total + term.astype(jnp.float32)
    return total.astype(jnp.bfloat16)


def after(values, *others):
    return lax.optimization_barrier((values, others))[0]


def body(
    hidden_in,
    norm_gain,
    route_logits,
    expert_ids,
    w_gate,
    w_up,
    w_down,
    w_latent,
    kv_gain,
    queries,
    page_pool,
    page_table,
    kv_lengths,
    migration,
):
    dp_count = lax.axis_size("dp")
    ex_count = lax.axis_size("expert")
    row_count = hidden_in.shape[0]
    local_experts = w_gate.shape[0]
    window = local_experts * dp_count
    width = hidden_in.shape[1]
    x_wide = hidden_in.astype(jnp.float32)
    normed = rms_rows(x_wide, norm_gain).astype(jnp.bfloat16)
    in_window = expert_ids < window
    has = jnp.any(in_window, axis=1)
    chosen = jnp.sum(jnp.where(in_window, expert_ids, 0), axis=1)
    sigma = jax.nn.sigmoid(route_logits)
    weight = (
        routed_scale * jnp.sum(jnp.where(in_window, sigma, 0.0), axis=1) / jnp.sum(sigma, axis=1)
    )
    onehot = ((chosen[:, None] == jnp.arange(window)[None, :]) & has[:, None]).astype(jnp.int32)
    rank = jnp.cumsum(onehot, axis=0) - onehot
    slot = jnp.sum(rank * onehot, axis=1)
    slots = local_experts * CAP
    place = chosen * CAP + slot
    pick = (place[:, None] == jnp.arange(window * CAP)[None, :]) & has[:, None]
    packed = jnp.einsum(
        "rs,rd->sd", pick.astype(jnp.bfloat16), normed, preferred_element_type=jnp.float32
    ).astype(jnp.bfloat16)
    place_weight = jnp.where(pick, weight[:, None], 0.0)
    arrived = lax.all_to_all(
        packed.reshape(dp_count, slots, width), "dp", split_axis=0, concat_axis=0, tiled=True
    )
    outgoing = jnp.take(page_pool, migration.reshape(dp_count * MCAP), axis=0, mode="clip")
    query = queries.reshape(row_count, HEADS, KVW)
    arrived = after(arrived, outgoing, query)
    w_all = lax.all_gather(w_latent, ("dp", "expert"), axis=0, tiled=True)
    axes = (("z", "x"), ("x", "z"))
    both = range(local_experts)
    rows = [
        arrived[:, k * CAP : (k + 1) * CAP].reshape(dp_count * CAP, width) for k in both
    ]

    incoming = lax.all_to_all(
        outgoing.reshape(dp_count, MCAP, page_pool.shape[1]),
        "dp",
        split_axis=0,
        concat_axis=0,
        tiled=True,
    ).reshape(dp_count * MCAP, page_pool.shape[1])
    below = [shift(rows[k], axes[k][0], 1) for k in both]
    above = [shift(rows[k], axes[k][0], -1) for k in both]
    below, above = after((below, above))
    beyond = [shift(below[k], axes[k][0], 1) for k in both]
    pool = after(page_pool, rows).reshape(page_pool.shape[0], PAGE, KVW)
    more = incoming.reshape(dp_count * MCAP, PAGE, KVW)
    beyond = after(beyond, pool, more)
    low, high = pack([(rows[k], below[k], above[k], beyond[k]) for k in both])
    below_low = [shift(low[k], axes[k][1], 1) for k in both]
    above_high = [shift(high[k], axes[k][1], -1) for k in both]
    pool = after(pool, low, high)
    cached, top, total = attend_cached(query, pool, more, page_table, kv_lengths)
    low, high = after((low, high), cached)
    below_high = [shift(high[k], axes[k][1], 1) for k in both]
    above_low = [shift(low[k], axes[k][1], -1) for k in both]
    weights = (w_gate, w_up, w_down)
    y_first = ffn([[low[k], high[k], below_low[k], above_high[k]] for k in both], *weights)
    below_low, above_high, below_high, above_low = after(
        (below_low, above_high, below_high, above_low), y_first
    )
    far_low = [shift(below_low[k], axes[k][1], 1) for k in both]
    far_high = [shift(above_high[k], axes[k][1], -1) for k in both]
    y_second = ffn([[below_high[k], above_low[k]] for k in both], *weights)
    y_first = after(y_first, y_second)
    early_down = [shift(y_first[k][2], axes[k][1], -1) for k in both]
    early_up = [shift(y_first[k][3], axes[k][1], 1) for k in both]
    far_low, far_high = after((far_low, far_high), y_second)
    y_far = ffn([[far_low[k], far_high[k]] for k in both], *weights)
    y_far, early_down, early_up = after((y_far, early_down, early_up))
    relay_up = [shift(y_far[k][0], axes[k][1], 1) for k in both]
    relay_down = [shift(y_far[k][1], axes[k][1], -1) for k in both]
    cached = after(cached, y_far).reshape(row_count, HEADS * LATENT)
    relay_up, relay_down = after((relay_up, relay_down), cached)
    late_up = [shift(plus(y_second[k][1], relay_up[k]), axes[k][1], 1) for k in both]
    late_down = [shift(plus(y_second[k][0], relay_down[k]), axes[k][1], -1) for k in both]
    late_up, late_down = after((late_up, late_down), w_all)
    n = rows[0].shape[0]
    terms_low = [(y_first[k][0], late_up[k], early_down[k]) for k in both]
    terms_high = [(y_first[k][1], early_up[k], late_down[k]) for k in both]
    for_far = [plus(*(term[n:] for term in terms_high[k])) for k in both]
    for_below = [plus(*(term[n:] for term in terms_low[k])) for k in both]
    relayed = [shift(for_far[k], axes[k][0], 1) for k in both]
    from_above = [shift(for_below[k], axes[k][0], -1) for k in both]
    relayed, from_above = after((relayed, from_above))
    from_below = [
        shift(plus(*(term[:n] for term in terms_high[k]), relayed[k]), axes[k][0], 1) for k in both
    ]
    from_below = after(from_below)
    finished = [
        plus(*(term[:n] for term in terms_low[k]), from_below[k], from_above[k]).reshape(
            dp_count, CAP, width
        )
        for k in both
    ]
    back = lax.all_to_all(
        jnp.concatenate(finished, axis=1), "dp", split_axis=0, concat_axis=0, tiled=True
    ).reshape(window * CAP, width)

    half = (KVW - LATENT) // 2
    freq = 10000.0 ** (-jnp.arange(half, dtype=jnp.float32) / half)
    angle = kv_lengths.astype(jnp.float32)[:, None] * freq[None, :]
    return tuple(
        tail(
            hidden_in,
            back,
            kv_gain,
            jnp.cos(angle),
            jnp.sin(angle),
            top,
            total,
            place_weight,
            w_all,
            queries,
            cached,
        )
    )


def solution(mesh):
    return jax.shard_map(
        body,
        mesh=mesh,
        in_specs=(
            P(("dp", "expert"), None),
            P(),
            P(("dp", "expert"), None),
            P(("dp", "expert"), None),
            P("dp", None, "expert"),
            P("dp", None, "expert"),
            P("dp", "expert", None),
            P(("dp", "expert"), None),
            P(),
            P(("dp", "expert"), None),
            P(("dp", "expert"), None),
            P(("dp", "expert"), None),
            P(("dp", "expert")),
            P("dp", "expert", None, None),
        ),
        out_specs=(P(("dp", "expert"), None), P(("dp", "expert"), None)),
        check_vma=False,
    )
```

```python
import functools

import jax
import jax.numpy as jnp
from jax import lax
from jax.experimental import pallas as pl
from jax.experimental.pallas import tpu as pltpu
from jax.sharding import PartitionSpec as P

HEADS = 64
LATENT = 512
PAGE = 16
MAXP = 6
CAP = 4
MCAP = 4
KVW = 576
SIDE = 4

softmax_scale = 192.0 ** (-0.5)
routed_scale = 2.5
norm_eps = 1e-06
MIB = 1 << 20


def rms_rows(values, gain):
    stat = jnp.mean(values * values, axis=-1, keepdims=True)
    return values * lax.rsqrt(stat + norm_eps) * gain


def shift(value, axis, step):
    pairs = []
    for x in range(SIDE):
        for z in range(SIDE):
            to_x = (x + step) % SIDE if axis == "x" else x
            to_z = (z + step) % SIDE if axis == "z" else z
            pairs.append((x * SIDE + z, to_x * SIDE + to_z))
    return lax.ppermute(value, "expert", pairs)


def ffn_kernel(count, rows, parts, *refs):
    xs = refs[:count]
    gate_hbm, up_hbm, down_hbm = refs[count : count + 3]
    outs = refs[count + 3 : 2 * count + 3]
    x_buf, w_buf, d_buf, o_buf, acc, in_sem, w_sem, d_sem, out_sem = refs[2 * count + 3 :]
    depth = gate_hbm.shape[1]
    piece = depth // parts

    def loads(c):
        cut = pl.ds(pl.multiple_of(c * piece, piece), piece)
        for e in range(2):
            for j, source in enumerate((gate_hbm, up_hbm)):
                yield pltpu.make_async_copy(
                    source.at[e, cut],
                    w_buf.at[cut, pl.ds(256 * e + 128 * j, 128)],
                    w_sem.at[c, 2 * e + j],
                )
        for i in range(count):
            yield pltpu.make_async_copy(
                xs[i].at[:, cut], x_buf.at[pl.ds(i * rows, rows), cut], in_sem.at[c, i]
            )

    def stores(c):
        cut = pl.ds(pl.multiple_of(c * piece, piece), piece)
        for i in range(count):
            yield pltpu.make_async_copy(
                o_buf.at[pl.ds(i * rows, rows), cut], outs[i].at[:, cut], out_sem.at[c, i]
            )

    @pl.loop(0, parts)
    def _(c):
        for copy in loads(c):
            copy.start()

    down = [
        pltpu.make_async_copy(down_hbm.at[e], d_buf.at[pl.ds(128 * e, 128)], d_sem.at[e])
        for e in range(2)
    ]
    for copy in down:
        copy.start()
    acc[...] = jnp.zeros_like(acc)

    @pl.loop(0, parts)
    def _(c):
        for copy in loads(c):
            copy.wait()
        cut = pl.ds(pl.multiple_of(c * piece, piece), piece)
        acc[...] += jnp.dot(x_buf[:, cut], w_buf[cut, :], preferred_element_type=jnp.float32)

    first = lax.broadcasted_iota(jnp.int32, (rows * count, 128), 0) % (2 * CAP) < CAP
    gate = jnp.where(first, acc[:, :128], acc[:, 256:384])
    up = jnp.where(first, acc[:, 128:256], acc[:, 384:])
    active = gate / (1.0 + jnp.exp(-gate)) * up
    active = jnp.concatenate(
        [jnp.where(first, active, 0.0), jnp.where(first, 0.0, active)], axis=1
    ).astype(jnp.bfloat16)
    for copy in down:
        copy.wait()

    @pl.loop(0, parts)
    def _(c):
        cut = pl.ds(pl.multiple_of(c * piece, piece), piece)
        o_buf[:, cut] = jnp.dot(active, d_buf[:, cut], preferred_element_type=jnp.float32).astype(
            jnp.bfloat16
        )
        for copy in stores(c):
            copy.start()

    @pl.loop(0, parts)
    def _(c):
        for copy in stores(c):
            copy.wait()


def ffn(blocks, w_gate, w_up, w_down):
    chains, per_chain = len(blocks), len(blocks[0])
    flat = [block for part in blocks for block in part]
    count, rows, depth, parts = len(flat), flat[0].shape[0], w_gate.shape[1], 4
    total = rows * count
    done = pl.pallas_call(
        functools.partial(ffn_kernel, count, rows, parts),
        out_shape=[jax.ShapeDtypeStruct(block.shape, jnp.bfloat16) for block in flat],
        in_specs=[pl.BlockSpec(memory_space=pl.ANY)] * (count + 3),
        out_specs=[pl.BlockSpec(memory_space=pl.ANY)] * count,
        scratch_shapes=[
            pltpu.VMEM((total, depth), jnp.bfloat16),
            pltpu.VMEM((depth, 512), jnp.bfloat16),
            pltpu.VMEM((256, depth), jnp.bfloat16),
            pltpu.VMEM((total, depth), jnp.bfloat16),
            pltpu.VMEM((total, 512), jnp.float32),
            pltpu.SemaphoreType.DMA((parts, count)),
            pltpu.SemaphoreType.DMA((parts, 4)),
            pltpu.SemaphoreType.DMA((2,)),
            pltpu.SemaphoreType.DMA((parts, count)),
        ],
        compiler_params=pltpu.CompilerParams(vmem_limit_bytes=58 * MIB),
        cost_estimate=pl.CostEstimate(
            flops=2 * total * depth * 768,
            bytes_accessed=2 * depth * (768 + 2 * total),
            transcendentals=total * 128,
        ),
        name="ffn",
    )(*flat, w_gate, w_up, w_down)
    return [done[k * per_chain : (k + 1) * per_chain] for k in range(chains)]


def attend_kernel(
    step, table, lengths, q_ref, pool_hbm, more_hbm, out_ref, top_ref, total_ref, pages, sem
):
    own_pages = pool_hbm.shape[0]

    @pl.when(pl.program_id(0) == 0)
    def _():
        copies = [
            pltpu.make_async_copy(pool_hbm, pages.at[pl.ds(0, own_pages)], sem.at[0]),
            pltpu.make_async_copy(
                more_hbm, pages.at[pl.ds(own_pages, more_hbm.shape[0])], sem.at[1]
            ),
        ]
        for copy in copies:
            copy.start()
        for copy in copies:
            copy.wait()

    first = pl.program_id(0) * step
    keys = [
        jnp.concatenate([pages[table[(first + r) * MAXP + p]] for p in range(MAXP)], axis=0)
        for r in range(step)
    ]
    scores = jnp.concatenate(
        [
            lax.dot_general(
                keys[r], q_ref[r], (((1,), (1,)), ((), ())), preferred_element_type=jnp.float32
            )
            for r in range(step)
        ],
        axis=1,
    )
    scores = scores * softmax_scale
    column = lax.broadcasted_iota(jnp.int32, (1, step * HEADS), 1) // HEADS
    length = jnp.zeros_like(column)
    for r in range(step):
        length = jnp.where(column == r, lengths[first + r], length)
    valid = lax.broadcasted_iota(jnp.int32, scores.shape, 0) < length
    scores = jnp.where(valid, scores, -1e30)
    top = jnp.max(scores, axis=0, keepdims=True)
    expo = jnp.where(valid, jnp.exp(scores - top), 0.0)
    total = jnp.sum(expo, axis=0, keepdims=True)
    probs = (expo / total).astype(jnp.bfloat16)
    for r in range(step):
        cut = slice(r * HEADS, (r + 1) * HEADS)
        out_ref[r] = lax.dot_general(
            probs[:, cut],
            keys[r][:, :LATENT],
            (((0,), (0,)), ((), ())),
            preferred_element_type=jnp.float32,
        ).astype(jnp.bfloat16)
        top_ref[r : r + 1, :] = top[:, cut]
        total_ref[r : r + 1, :] = total[:, cut]


def attend_cached(query, pool, more, page_table, kv_lengths):
    rows, step = query.shape[0], 8
    entries = pool.shape[0] + more.shape[0]
    hbm = pl.BlockSpec(memory_space=pl.ANY)
    return pl.pallas_call(
        functools.partial(attend_kernel, step),
        out_shape=[
            jax.ShapeDtypeStruct((rows, HEADS, LATENT), jnp.bfloat16),
            jax.ShapeDtypeStruct((rows, HEADS), jnp.float32),
            jax.ShapeDtypeStruct((rows, HEADS), jnp.float32),
        ],
        grid_spec=pltpu.PrefetchScalarGridSpec(
            num_scalar_prefetch=2,
            grid=(rows // step,),
            in_specs=[pl.BlockSpec((step, HEADS, KVW), lambda i, t, n: (i, 0, 0)), hbm, hbm],
            out_specs=[
                pl.BlockSpec((step, HEADS, LATENT), lambda i, t, n: (i, 0, 0)),
                pl.BlockSpec((step, HEADS), lambda i, t, n: (i, 0)),
                pl.BlockSpec((step, HEADS), lambda i, t, n: (i, 0)),
            ],
            scratch_shapes=[
                pltpu.VMEM((entries, PAGE, KVW), jnp.bfloat16),
                pltpu.SemaphoreType.DMA((2,)),
            ],
        ),
        compiler_params=pltpu.CompilerParams(vmem_limit_bytes=58 * MIB),
        cost_estimate=pl.CostEstimate(
            flops=2 * rows * HEADS * MAXP * PAGE * (KVW + LATENT),
            bytes_accessed=2 * (query.size + entries * PAGE * KVW + rows * HEADS * LATENT),
            transcendentals=rows * HEADS * MAXP * PAGE,
        ),
        name="attend_cached",
    )(page_table.reshape(rows * MAXP), kv_lengths, query, pool, more)


def pack_kernel(count, *refs):
    blocks, joined = refs[: 2 * count], refs[2 * count : 3 * count]
    buf, in_sem, out_sem = refs[3 * count :]
    n = blocks[0].shape[0]
    loads = [
        pltpu.make_async_copy(blocks[i], buf.at[i // 2, pl.ds(i % 2 * n, n)], in_sem.at[i])
        for i in range(2 * count)
    ]
    stores = [pltpu.make_async_copy(buf.at[i], joined[i], out_sem.at[i]) for i in range(count)]
    for copy in loads:
        copy.start()
    for i in range(count):
        loads[2 * i].wait()
        loads[2 * i + 1].wait()
        stores[i].start()
    for copy in stores:
        copy.wait()


def pack(pairs):
    count, (n, width) = len(pairs), pairs[0][0].shape
    hbm = pl.BlockSpec(memory_space=pl.ANY)
    return pl.pallas_call(
        functools.partial(pack_kernel, count),
        out_shape=[jax.ShapeDtypeStruct((2 * n, width), jnp.bfloat16)] * count,
        in_specs=[hbm] * (2 * count),
        out_specs=[hbm] * count,
        scratch_shapes=[
            pltpu.VMEM((count, 2 * n, width), jnp.bfloat16),
            pltpu.SemaphoreType.DMA((2 * count,)),
            pltpu.SemaphoreType.DMA((count,)),
        ],
        compiler_params=pltpu.CompilerParams(vmem_limit_bytes=58 * MIB),
        cost_estimate=pl.CostEstimate(
            flops=0, bytes_accessed=8 * count * n * width, transcendentals=0
        ),
        name="pack",
    )(*(block for pair in pairs for block in pair))


def tail_kernel(
    parts,
    groups,
    hidden_ref,
    back_ref,
    gain_ref,
    cos_ref,
    sin_ref,
    top_ref,
    total_ref,
    place_ref,
    w_hbm,
    q_hbm,
    o_hbm,
    hidden_out_hbm,
    out_hbm,
    w_ref,
    q_ref,
    o_ref,
    hidden_buf,
    key_buf,
    own_buf,
    keep_buf,
    w_sem,
    q_sem,
    o_sem,
    hidden_sem,
    out_sem,
):
    width = hidden_ref.shape[1]
    piece = width // parts
    per_group = HEADS // groups
    span, q_span = per_group * LATENT, per_group * KVW

    def w_load(c):
        cut = pl.ds(pl.multiple_of(c * piece, piece), piece)
        return pltpu.make_async_copy(w_hbm.at[cut], w_ref.at[cut], w_sem.at[c])

    def q_load(g):
        cut = pl.ds(pl.multiple_of(g * q_span, 128), q_span)
        return pltpu.make_async_copy(q_hbm.at[:, cut], q_ref.at[:, cut], q_sem.at[g])

    def o_load(g):
        cut = pl.ds(pl.multiple_of(g * span, span), span)
        return pltpu.make_async_copy(o_hbm.at[:, cut], o_ref.at[:, cut], o_sem.at[g])

    def store(g):
        cut = pl.ds(pl.multiple_of(g * span, span), span)
        return pltpu.make_async_copy(o_ref.at[:, cut], out_hbm.at[:, cut], out_sem.at[g])

    for c in range(parts):
        w_load(c).start()

    @pl.loop(0, groups)
    def _(g):
        q_load(g).start()

    @pl.loop(0, groups)
    def _(g):
        o_load(g).start()

    place = place_ref[...]
    pick = (place != 0.0).astype(jnp.bfloat16)
    weight = jnp.sum(place, axis=1, keepdims=True)
    projected = jnp.zeros((hidden_ref.shape[0], KVW), jnp.float32)
    for c in range(parts):
        cut = slice(c * piece, (c + 1) * piece)
        picked = jnp.dot(pick, back_ref[:, cut], preferred_element_type=jnp.float32)
        hidden = (hidden_ref[:, cut].astype(jnp.float32) + weight * picked).astype(jnp.bfloat16)
        hidden_buf[:, cut] = hidden
        w_load(c).wait()
        projected += jnp.dot(hidden, w_ref[cut, :], preferred_element_type=jnp.float32)
    hidden_copy = pltpu.make_async_copy(hidden_buf, hidden_out_hbm, hidden_sem)
    hidden_copy.start()
    latent = rms_rows(projected[:, :LATENT], gain_ref[...])
    first = projected[:, LATENT : LATENT + 32]
    second = projected[:, LATENT + 32 :]
    cosine, sine = cos_ref[...], sin_ref[...]
    new_key = jnp.concatenate(
        [latent, first * cosine - second * sine, second * cosine + first * sine], axis=1
    )
    new_key = new_key.astype(jnp.bfloat16).astype(jnp.float32)
    key_buf[...] = jnp.concatenate([new_key, new_key], axis=1)
    lane = lax.broadcasted_iota(jnp.int32, (8, 128), 1)
    head = lax.broadcasted_iota(jnp.int32, (8, HEADS), 1)
    blocks = hidden_ref.shape[0] // 8
    own_buf[...] = jnp.zeros_like(own_buf)

    @pl.loop(0, HEADS // 2)
    def _(j):
        @pl.when(j % (per_group // 2) == 0)
        def _():
            q_load(j // (per_group // 2)).wait()

        cut = pl.ds(pl.multiple_of(j * 2 * KVW, 128), 2 * KVW)
        for b in range(blocks):
            rows = slice(8 * b, 8 * b + 8)
            product = q_ref[rows, cut].astype(jnp.float32) * key_buf[rows, :]
            tiles = [product[:, 128 * i : 128 * (i + 1)] for i in range(9)]
            low = (tiles[0] + tiles[1]) + (tiles[2] + tiles[3]) + jnp.where(lane < 64, tiles[4], 0.0)
            high = (tiles[5] + tiles[6]) + (tiles[7] + tiles[8])
            high = high + jnp.where(lane < 64, 0.0, tiles[4])
            low = jnp.sum(low, axis=1, keepdims=True)
            high = jnp.sum(high, axis=1, keepdims=True)
            own_buf[rows, :] = jnp.where(
                head == 2 * j, low, jnp.where(head == 2 * j + 1, high, own_buf[rows, :])
            )

    own = own_buf[...] * softmax_scale
    top_old = top_ref[...]
    top = jnp.maximum(top_old, own)
    part = total_ref[...] * jnp.exp(top_old - top)
    part_own = jnp.exp(own - top)
    inverse = 1.0 / (part + part_own)
    keep_buf[...] = part * inverse
    own_buf[...] = (part_own * inverse).astype(jnp.bfloat16).astype(jnp.float32)

    @pl.loop(0, groups)
    def _(g):
        o_load(g).wait()
        for b in range(blocks):
            rows = slice(8 * b, 8 * b + 8)
            key_low = key_buf[rows, :LATENT]
            keeps, adds = keep_buf[rows, :], own_buf[rows, :]
            for i in range(per_group):
                h = g * per_group + i
                keep = jnp.sum(jnp.where(head == h, keeps, 0.0), axis=1, keepdims=True)
                add = jnp.sum(jnp.where(head == h, adds, 0.0), axis=1, keepdims=True)
                cut = pl.ds(pl.multiple_of(h * LATENT, LATENT), LATENT)
                o_ref[rows, cut] = (
                    o_ref[rows, cut].astype(jnp.float32) * keep + add * key_low
                ).astype(jnp.bfloat16)
        store(g).start()

    @pl.loop(0, groups)
    def _(g):
        store(g).wait()

    hidden_copy.wait()


def tail(hidden_in, back, kv_gain, cosine, sine, top, total, place_weight, w_all, queries, o):
    rows, width = hidden_in.shape
    parts, groups = 7, 8
    vmem = pl.BlockSpec(memory_space=pltpu.VMEM)
    hbm = pl.BlockSpec(memory_space=pl.ANY)
    return pl.pallas_call(
        functools.partial(tail_kernel, parts, groups),
        out_shape=[
            jax.ShapeDtypeStruct((rows, width), jnp.bfloat16),
            jax.ShapeDtypeStruct((rows, HEADS * LATENT), jnp.bfloat16),
        ],
        in_specs=[vmem] * 8 + [hbm] * 3,
        out_specs=[hbm] * 2,
        scratch_shapes=[
            pltpu.VMEM(w_all.shape, jnp.bfloat16),
            pltpu.VMEM(queries.shape, jnp.bfloat16),
            pltpu.VMEM(o.shape, jnp.bfloat16),
            pltpu.VMEM((rows, width), jnp.bfloat16),
            pltpu.VMEM((rows, 2 * KVW), jnp.float32),
            pltpu.VMEM((rows, HEADS), jnp.float32),
            pltpu.VMEM((rows, HEADS), jnp.float32),
            pltpu.SemaphoreType.DMA((parts,)),
            pltpu.SemaphoreType.DMA((groups,)),
            pltpu.SemaphoreType.DMA((groups,)),
            pltpu.SemaphoreType.DMA,
            pltpu.SemaphoreType.DMA((groups,)),
        ],
        compiler_params=pltpu.CompilerParams(vmem_limit_bytes=40 * MIB),
        cost_estimate=pl.CostEstimate(
            flops=2 * rows * width * KVW,
            bytes_accessed=2 * (w_all.size + queries.size + 2 * o.size),
            transcendentals=rows * HEADS * 2,
        ),
        name="tail",
    )(
        hidden_in,
        back,
        kv_gain.reshape(1, LATENT),
        cosine,
        sine,
        top,
        total,
        place_weight,
        w_all,
        queries,
        o,
    )


def plus(*terms):
    total = terms[0].astype(jnp.float32)
    for term in terms[1:]:
        total = total + term.astype(jnp.float32)
    return total.astype(jnp.bfloat16)


def after(values, *others):
    return lax.optimization_barrier((values, others))[0]


def body(
    hidden_in,
    norm_gain,
    route_logits,
    expert_ids,
    w_gate,
    w_up,
    w_down,
    w_latent,
    kv_gain,
    queries,
    page_pool,
    page_table,
    kv_lengths,
    migration,
):
    dp_count = lax.axis_size("dp")
    ex_count = lax.axis_size("expert")
    row_count = hidden_in.shape[0]
    local_experts = w_gate.shape[0]
    window = local_experts * dp_count
    width = hidden_in.shape[1]
    x_wide = hidden_in.astype(jnp.float32)
    normed = rms_rows(x_wide, norm_gain).astype(jnp.bfloat16)
    in_window = expert_ids < window
    has = jnp.any(in_window, axis=1)
    chosen = jnp.sum(jnp.where(in_window, expert_ids, 0), axis=1)
    sigma = jax.nn.sigmoid(route_logits)
    weight = (
        routed_scale * jnp.sum(jnp.where(in_window, sigma, 0.0), axis=1) / jnp.sum(sigma, axis=1)
    )
    onehot = ((chosen[:, None] == jnp.arange(window)[None, :]) & has[:, None]).astype(jnp.int32)
    rank = jnp.cumsum(onehot, axis=0) - onehot
    slot = jnp.sum(rank * onehot, axis=1)
    slots = local_experts * CAP
    place = chosen * CAP + slot
    pick = (place[:, None] == jnp.arange(window * CAP)[None, :]) & has[:, None]
    packed = jnp.einsum(
        "rs,rd->sd", pick.astype(jnp.bfloat16), normed, preferred_element_type=jnp.float32
    ).astype(jnp.bfloat16)
    place_weight = jnp.where(pick, weight[:, None], 0.0)
    arrived = lax.all_to_all(
        packed.reshape(dp_count, slots, width), "dp", split_axis=0, concat_axis=0, tiled=True
    )
    outgoing = jnp.take(page_pool, migration.reshape(dp_count * MCAP), axis=0, mode="clip")
    query = queries.reshape(row_count, HEADS, KVW)
    arrived = after(arrived, outgoing, query)
    arrived = arrived.reshape(window * CAP, width)
    axes = (("z", "x"), ("x", "z"))
    both = range(2)
    n = arrived.shape[0] // 2
    rows = [arrived[k * n : (k + 1) * n] for k in both]
    weights = (w_gate, w_up, w_down)

    below = [shift(rows[k], axes[k][0], 1) for k in both]
    above = [shift(rows[k], axes[k][0], -1) for k in both]
    incoming = lax.all_to_all(
        after(outgoing, arrived).reshape(dp_count, MCAP, page_pool.shape[1]),
        "dp",
        split_axis=0,
        concat_axis=0,
        tiled=True,
    ).reshape(dp_count * MCAP, page_pool.shape[1])
    below, above = after((below, above))
    beyond = [shift(above[k], axes[k][0], -1) for k in both]
    low = pack([(rows[k], below[k]) for k in both])
    below_low = [shift(low[k], axes[k][1], 1) for k in both]
    low_too, beyond = after((low, beyond))
    above_low = [shift(low_too[k], axes[k][1], -1) for k in both]
    w_local, pool = after((w_latent, page_pool), low, incoming)
    spread = lax.all_to_all(
        jnp.broadcast_to(w_local[None], (ex_count,) + w_latent.shape),
        "expert",
        split_axis=0,
        concat_axis=0,
        tiled=True,
    ).reshape(ex_count * w_latent.shape[0], KVW)
    pool = pool.reshape(page_pool.shape[0], PAGE, KVW)
    more = incoming.reshape(dp_count * MCAP, PAGE, KVW)
    high = pack([(above[k], beyond[k]) for k in both])
    high = after(high, pool, more)
    below_low, above_low = after((below_low, above_low), spread)
    w_all = lax.all_gather(spread, "dp", axis=0, tiled=True)
    below_high = [shift(high[k], axes[k][1], 1) for k in both]
    above_high = [shift(high[k], axes[k][1], -1) for k in both]
    y_first = ffn([[low[k], high[k], below_low[k], above_low[k]] for k in both], *weights)
    below_low, above_high, below_high, above_low = after(
        (below_low, above_high, below_high, above_low), y_first
    )
    far_low = [shift(below_low[k], axes[k][1], 1) for k in both]
    far_high = [shift(above_high[k], axes[k][1], -1) for k in both]
    y_second = ffn([[below_high[k], above_high[k]] for k in both], *weights)
    y_first = after(y_first, y_second)
    early_down = [shift(y_first[k][2], axes[k][1], -1) for k in both]
    early_up = [shift(y_second[k][1], axes[k][1], 1) for k in both]
    far_low, far_high = after((far_low, far_high), y_second)
    y_far = ffn([[far_low[k], far_high[k]] for k in both], *weights)
    y_far, early_down, early_up = after((y_far, early_down, early_up))
    relay_up = [shift(y_far[k][0], axes[k][1], 1) for k in both]
    relay_down = [shift(y_far[k][1], axes[k][1], -1) for k in both]
    query = after(query, y_far)
    cached, top, total = attend_cached(query, pool, more, page_table, kv_lengths)
    relay_up, relay_down = after((relay_up, relay_down), cached)
    late_up = [shift(plus(y_first[k][3], relay_up[k]), axes[k][1], 1) for k in both]
    late_down = [shift(plus(y_second[k][0], relay_down[k]), axes[k][1], -1) for k in both]
    cached = cached.reshape(row_count, HEADS * LATENT)
    late_up, late_down = after((late_up, late_down), cached)
    terms_low = [(y_first[k][0], late_up[k], early_down[k]) for k in both]
    terms_high = [(y_first[k][1], early_up[k], late_down[k]) for k in both]
    for_far = [plus(*(term[n:] for term in terms_high[k])) for k in both]
    for_below = [plus(*(term[n:] for term in terms_low[k])) for k in both]
    relayed = [shift(for_far[k], axes[k][0], 1) for k in both]
    from_above = [shift(for_below[k], axes[k][0], -1) for k in both]
    relayed, from_above = after((relayed, from_above))
    from_below = [
        shift(plus(*(term[:n] for term in terms_high[k]), relayed[k]), axes[k][0], 1) for k in both
    ]
    from_below = after(from_below)
    finished = [
        plus(*(term[:n] for term in terms_low[k]), from_below[k], from_above[k]) for k in both
    ]
    back = lax.all_to_all(
        jnp.concatenate(finished, axis=0).reshape(dp_count, slots, width),
        "dp",
        split_axis=0,
        concat_axis=0,
        tiled=True,
    ).reshape(window * CAP, width)

    half = (KVW - LATENT) // 2
    freq = 10000.0 ** (-jnp.arange(half, dtype=jnp.float32) / half)
    angle = kv_lengths.astype(jnp.float32)[:, None] * freq[None, :]
    return tuple(
        tail(
            hidden_in,
            back,
            kv_gain,
            jnp.cos(angle),
            jnp.sin(angle),
            top,
            total,
            place_weight,
            w_all,
            queries,
            cached,
        )
    )


def solution(mesh):
    return jax.shard_map(
        body,
        mesh=mesh,
        in_specs=(
            P(("dp", "expert"), None),
            P(),
            P(("dp", "expert"), None),
            P(("dp", "expert"), None),
            P("dp", None, "expert"),
            P("dp", None, "expert"),
            P("dp", "expert", None),
            P(("dp", "expert"), None),
            P(),
            P(("dp", "expert"), None),
            P(("dp", "expert"), None),
            P(("dp", "expert"), None),
            P(("dp", "expert")),
            P("dp", "expert", None, None),
        ),
        out_specs=(P(("dp", "expert"), None), P(("dp", "expert"), None)),
        check_vma=False,
    )
```

```python
import functools

import jax
import jax.numpy as jnp
from jax import lax
from jax.experimental import pallas as pl
from jax.experimental.pallas import tpu as pltpu
from jax.sharding import PartitionSpec as P

HEADS = 64
LATENT = 512
PAGE = 16
MAXP = 6
CAP = 4
MCAP = 4
KVW = 576
SIDE = 4

softmax_scale = 192.0 ** (-0.5)
routed_scale = 2.5
norm_eps = 1e-06
MIB = 1 << 20


def rms_rows(values, gain):
    stat = jnp.mean(values * values, axis=-1, keepdims=True)
    return values * lax.rsqrt(stat + norm_eps) * gain


def shift(value, axis, step):
    pairs = []
    for x in range(SIDE):
        for z in range(SIDE):
            to_x = (x + step) % SIDE if axis == "x" else x
            to_z = (z + step) % SIDE if axis == "z" else z
            pairs.append((x * SIDE + z, to_x * SIDE + to_z))
    return lax.ppermute(value, "expert", pairs)


def ffn_kernel(count, rows, parts, *refs):
    xs = refs[:count]
    gate_hbm, up_hbm, down_hbm = refs[count : count + 3]
    outs = refs[count + 3 : 2 * count + 3]
    x_buf, w_buf, d_buf, o_buf, acc, in_sem, w_sem, d_sem, out_sem = refs[2 * count + 3 :]
    depth = gate_hbm.shape[1]
    piece = depth // parts

    def loads(c):
        cut = pl.ds(pl.multiple_of(c * piece, piece), piece)
        for e in range(2):
            for j, source in enumerate((gate_hbm, up_hbm)):
                yield pltpu.make_async_copy(
                    source.at[e, cut],
                    w_buf.at[cut, pl.ds(256 * e + 128 * j, 128)],
                    w_sem.at[c, 2 * e + j],
                )
        for i in range(count):
            yield pltpu.make_async_copy(
                xs[i].at[:, cut], x_buf.at[pl.ds(i * rows, rows), cut], in_sem.at[c, i]
            )

    def stores(c):
        cut = pl.ds(pl.multiple_of(c * piece, piece), piece)
        for i in range(count):
            yield pltpu.make_async_copy(
                o_buf.at[pl.ds(i * rows, rows), cut], outs[i].at[:, cut], out_sem.at[c, i]
            )

    @pl.loop(0, parts)
    def _(c):
        for copy in loads(c):
            copy.start()

    down = [
        pltpu.make_async_copy(down_hbm.at[e], d_buf.at[pl.ds(128 * e, 128)], d_sem.at[e])
        for e in range(2)
    ]
    for copy in down:
        copy.start()
    acc[...] = jnp.zeros_like(acc)

    @pl.loop(0, parts)
    def _(c):
        for copy in loads(c):
            copy.wait()
        cut = pl.ds(pl.multiple_of(c * piece, piece), piece)
        acc[...] += jnp.dot(x_buf[:, cut], w_buf[cut, :], preferred_element_type=jnp.float32)

    first = lax.broadcasted_iota(jnp.int32, (rows * count, 128), 0) % (2 * CAP) < CAP
    gate = jnp.where(first, acc[:, :128], acc[:, 256:384])
    up = jnp.where(first, acc[:, 128:256], acc[:, 384:])
    active = gate / (1.0 + jnp.exp(-gate)) * up
    active = jnp.concatenate(
        [jnp.where(first, active, 0.0), jnp.where(first, 0.0, active)], axis=1
    ).astype(jnp.bfloat16)
    for copy in down:
        copy.wait()

    @pl.loop(0, parts)
    def _(c):
        cut = pl.ds(pl.multiple_of(c * piece, piece), piece)
        o_buf[:, cut] = jnp.dot(active, d_buf[:, cut], preferred_element_type=jnp.float32).astype(
            jnp.bfloat16
        )
        for copy in stores(c):
            copy.start()

    @pl.loop(0, parts)
    def _(c):
        for copy in stores(c):
            copy.wait()


def ffn(blocks, w_gate, w_up, w_down):
    chains, per_chain = len(blocks), len(blocks[0])
    flat = [block for part in blocks for block in part]
    count, rows, depth, parts = len(flat), flat[0].shape[0], w_gate.shape[1], 4
    total = rows * count
    done = pl.pallas_call(
        functools.partial(ffn_kernel, count, rows, parts),
        out_shape=[jax.ShapeDtypeStruct(block.shape, jnp.bfloat16) for block in flat],
        in_specs=[pl.BlockSpec(memory_space=pl.ANY)] * (count + 3),
        out_specs=[pl.BlockSpec(memory_space=pl.ANY)] * count,
        scratch_shapes=[
            pltpu.VMEM((total, depth), jnp.bfloat16),
            pltpu.VMEM((depth, 512), jnp.bfloat16),
            pltpu.VMEM((256, depth), jnp.bfloat16),
            pltpu.VMEM((total, depth), jnp.bfloat16),
            pltpu.VMEM((total, 512), jnp.float32),
            pltpu.SemaphoreType.DMA((parts, count)),
            pltpu.SemaphoreType.DMA((parts, 4)),
            pltpu.SemaphoreType.DMA((2,)),
            pltpu.SemaphoreType.DMA((parts, count)),
        ],
        compiler_params=pltpu.CompilerParams(vmem_limit_bytes=58 * MIB),
        cost_estimate=pl.CostEstimate(
            flops=2 * total * depth * 768,
            bytes_accessed=2 * depth * (768 + 2 * total),
            transcendentals=total * 128,
        ),
        name="ffn",
    )(*flat, w_gate, w_up, w_down)
    return [done[k * per_chain : (k + 1) * per_chain] for k in range(chains)]


def attend_kernel(
    step, table, lengths, q_ref, pool_hbm, more_hbm, out_ref, top_ref, total_ref, pages, sem
):
    own_pages = pool_hbm.shape[0]

    @pl.when(pl.program_id(0) == 0)
    def _():
        copies = [
            pltpu.make_async_copy(pool_hbm, pages.at[pl.ds(0, own_pages)], sem.at[0]),
            pltpu.make_async_copy(
                more_hbm, pages.at[pl.ds(own_pages, more_hbm.shape[0])], sem.at[1]
            ),
        ]
        for copy in copies:
            copy.start()
        for copy in copies:
            copy.wait()

    first = pl.program_id(0) * step
    keys = [
        jnp.concatenate([pages[table[(first + r) * MAXP + p]] for p in range(MAXP)], axis=0)
        for r in range(step)
    ]
    scores = jnp.concatenate(
        [
            lax.dot_general(
                keys[r], q_ref[r], (((1,), (1,)), ((), ())), preferred_element_type=jnp.float32
            )
            for r in range(step)
        ],
        axis=1,
    )
    scores = scores * softmax_scale
    column = lax.broadcasted_iota(jnp.int32, (1, step * HEADS), 1) // HEADS
    length = jnp.zeros_like(column)
    for r in range(step):
        length = jnp.where(column == r, lengths[first + r], length)
    valid = lax.broadcasted_iota(jnp.int32, scores.shape, 0) < length
    scores = jnp.where(valid, scores, -1e30)
    top = jnp.max(scores, axis=0, keepdims=True)
    expo = jnp.where(valid, jnp.exp(scores - top), 0.0)
    total = jnp.sum(expo, axis=0, keepdims=True)
    probs = (expo / total).astype(jnp.bfloat16)
    for r in range(step):
        cut = slice(r * HEADS, (r + 1) * HEADS)
        out_ref[r] = lax.dot_general(
            probs[:, cut],
            keys[r][:, :LATENT],
            (((0,), (0,)), ((), ())),
            preferred_element_type=jnp.float32,
        ).astype(jnp.bfloat16)
        top_ref[r : r + 1, :] = top[:, cut]
        total_ref[r : r + 1, :] = total[:, cut]


def attend_cached(query, pool, more, page_table, kv_lengths):
    rows, step = query.shape[0], 8
    entries = pool.shape[0] + more.shape[0]
    hbm = pl.BlockSpec(memory_space=pl.ANY)
    return pl.pallas_call(
        functools.partial(attend_kernel, step),
        out_shape=[
            jax.ShapeDtypeStruct((rows, HEADS, LATENT), jnp.bfloat16),
            jax.ShapeDtypeStruct((rows, HEADS), jnp.float32),
            jax.ShapeDtypeStruct((rows, HEADS), jnp.float32),
        ],
        grid_spec=pltpu.PrefetchScalarGridSpec(
            num_scalar_prefetch=2,
            grid=(rows // step,),
            in_specs=[pl.BlockSpec((step, HEADS, KVW), lambda i, t, n: (i, 0, 0)), hbm, hbm],
            out_specs=[
                pl.BlockSpec((step, HEADS, LATENT), lambda i, t, n: (i, 0, 0)),
                pl.BlockSpec((step, HEADS), lambda i, t, n: (i, 0)),
                pl.BlockSpec((step, HEADS), lambda i, t, n: (i, 0)),
            ],
            scratch_shapes=[
                pltpu.VMEM((entries, PAGE, KVW), jnp.bfloat16),
                pltpu.SemaphoreType.DMA((2,)),
            ],
        ),
        compiler_params=pltpu.CompilerParams(vmem_limit_bytes=58 * MIB),
        cost_estimate=pl.CostEstimate(
            flops=2 * rows * HEADS * MAXP * PAGE * (KVW + LATENT),
            bytes_accessed=2 * (query.size + entries * PAGE * KVW + rows * HEADS * LATENT),
            transcendentals=rows * HEADS * MAXP * PAGE,
        ),
        name="attend_cached",
    )(page_table.reshape(rows * MAXP), kv_lengths, query, pool, more)


def pack_kernel(count, *refs):
    blocks, joined = refs[: 2 * count], refs[2 * count : 3 * count]
    buf, in_sem, out_sem = refs[3 * count :]
    n = blocks[0].shape[0]
    loads = [
        pltpu.make_async_copy(blocks[i], buf.at[i // 2, pl.ds(i % 2 * n, n)], in_sem.at[i])
        for i in range(2 * count)
    ]
    stores = [pltpu.make_async_copy(buf.at[i], joined[i], out_sem.at[i]) for i in range(count)]
    for copy in loads:
        copy.start()
    for i in range(count):
        loads[2 * i].wait()
        loads[2 * i + 1].wait()
        stores[i].start()
    for copy in stores:
        copy.wait()


def pack(pairs):
    count, (n, width) = len(pairs), pairs[0][0].shape
    hbm = pl.BlockSpec(memory_space=pl.ANY)
    return pl.pallas_call(
        functools.partial(pack_kernel, count),
        out_shape=[jax.ShapeDtypeStruct((2 * n, width), jnp.bfloat16)] * count,
        in_specs=[hbm] * (2 * count),
        out_specs=[hbm] * count,
        scratch_shapes=[
            pltpu.VMEM((count, 2 * n, width), jnp.bfloat16),
            pltpu.SemaphoreType.DMA((2 * count,)),
            pltpu.SemaphoreType.DMA((count,)),
        ],
        compiler_params=pltpu.CompilerParams(vmem_limit_bytes=58 * MIB),
        cost_estimate=pl.CostEstimate(
            flops=0, bytes_accessed=8 * count * n * width, transcendentals=0
        ),
        name="pack",
    )(*(block for pair in pairs for block in pair))


def tail_kernel(
    parts,
    groups,
    hidden_hbm,
    back_hbm,
    gain_ref,
    cos_ref,
    sin_ref,
    top_ref,
    total_ref,
    place_ref,
    w_hbm,
    q_hbm,
    o_hbm,
    hidden_out_hbm,
    out_hbm,
    w_ref,
    q_ref,
    o_ref,
    hidden_ref,
    back_ref,
    hidden_buf,
    key_buf,
    own_buf,
    keep_buf,
    in_sem,
    w_sem,
    q_sem,
    o_sem,
    hidden_sem,
    out_sem,
):
    width = hidden_ref.shape[1]
    loads = [
        pltpu.make_async_copy(back_hbm, back_ref, in_sem.at[0]),
        pltpu.make_async_copy(hidden_hbm, hidden_ref, in_sem.at[1]),
    ]
    for copy in loads:
        copy.start()
    piece = width // parts
    per_group = HEADS // groups
    span, q_span = per_group * LATENT, per_group * KVW

    def w_load(c):
        cut = pl.ds(pl.multiple_of(c * piece, piece), piece)
        return pltpu.make_async_copy(w_hbm.at[cut], w_ref.at[cut], w_sem.at[c])

    def q_load(g):
        cut = pl.ds(pl.multiple_of(g * q_span, 128), q_span)
        return pltpu.make_async_copy(q_hbm.at[:, cut], q_ref.at[:, cut], q_sem.at[g])

    def o_load(g):
        cut = pl.ds(pl.multiple_of(g * span, span), span)
        return pltpu.make_async_copy(o_hbm.at[:, cut], o_ref.at[:, cut], o_sem.at[g])

    def store(g):
        cut = pl.ds(pl.multiple_of(g * span, span), span)
        return pltpu.make_async_copy(o_ref.at[:, cut], out_hbm.at[:, cut], out_sem.at[g])

    for c in range(parts):
        w_load(c).start()

    @pl.loop(0, groups)
    def _(g):
        q_load(g).start()

    @pl.loop(0, groups)
    def _(g):
        o_load(g).start()

    place = place_ref[...]
    pick = (place != 0.0).astype(jnp.bfloat16)
    weight = jnp.sum(place, axis=1, keepdims=True)
    projected = jnp.zeros((hidden_ref.shape[0], KVW), jnp.float32)
    for copy in loads:
        copy.wait()
    for c in range(parts):
        cut = slice(c * piece, (c + 1) * piece)
        picked = jnp.dot(pick, back_ref[:, cut], preferred_element_type=jnp.float32)
        hidden = (hidden_ref[:, cut].astype(jnp.float32) + weight * picked).astype(jnp.bfloat16)
        hidden_buf[:, cut] = hidden
        w_load(c).wait()
        projected += jnp.dot(hidden, w_ref[cut, :], preferred_element_type=jnp.float32)
    hidden_copy = pltpu.make_async_copy(hidden_buf, hidden_out_hbm, hidden_sem)
    hidden_copy.start()
    latent = rms_rows(projected[:, :LATENT], gain_ref[...])
    first = projected[:, LATENT : LATENT + 32]
    second = projected[:, LATENT + 32 :]
    cosine, sine = cos_ref[...], sin_ref[...]
    new_key = jnp.concatenate(
        [latent, first * cosine - second * sine, second * cosine + first * sine], axis=1
    )
    new_key = new_key.astype(jnp.bfloat16).astype(jnp.float32)
    key_buf[...] = jnp.concatenate([new_key, new_key], axis=1)
    lane = lax.broadcasted_iota(jnp.int32, (8, 128), 1)
    head = lax.broadcasted_iota(jnp.int32, (8, HEADS), 1)
    blocks = hidden_ref.shape[0] // 8
    own_buf[...] = jnp.zeros_like(own_buf)

    @pl.loop(0, HEADS // 2)
    def _(j):
        @pl.when(j % (per_group // 2) == 0)
        def _():
            q_load(j // (per_group // 2)).wait()

        cut = pl.ds(pl.multiple_of(j * 2 * KVW, 128), 2 * KVW)
        for b in range(blocks):
            rows = slice(8 * b, 8 * b + 8)
            product = q_ref[rows, cut].astype(jnp.float32) * key_buf[rows, :]
            tiles = [product[:, 128 * i : 128 * (i + 1)] for i in range(9)]
            low = (tiles[0] + tiles[1]) + (tiles[2] + tiles[3]) + jnp.where(lane < 64, tiles[4], 0.0)
            high = (tiles[5] + tiles[6]) + (tiles[7] + tiles[8])
            high = high + jnp.where(lane < 64, 0.0, tiles[4])
            low = jnp.sum(low, axis=1, keepdims=True)
            high = jnp.sum(high, axis=1, keepdims=True)
            own_buf[rows, :] = jnp.where(
                head == 2 * j, low, jnp.where(head == 2 * j + 1, high, own_buf[rows, :])
            )

    own = own_buf[...] * softmax_scale
    top_old = top_ref[...]
    top = jnp.maximum(top_old, own)
    part = total_ref[...] * jnp.exp(top_old - top)
    part_own = jnp.exp(own - top)
    inverse = 1.0 / (part + part_own)
    keep_buf[...] = part * inverse
    own_buf[...] = (part_own * inverse).astype(jnp.bfloat16).astype(jnp.float32)

    @pl.loop(0, groups)
    def _(g):
        o_load(g).wait()
        for b in range(blocks):
            rows = slice(8 * b, 8 * b + 8)
            key_low = key_buf[rows, :LATENT]
            keeps, adds = keep_buf[rows, :], own_buf[rows, :]
            for i in range(per_group):
                h = g * per_group + i
                keep = jnp.sum(jnp.where(head == h, keeps, 0.0), axis=1, keepdims=True)
                add = jnp.sum(jnp.where(head == h, adds, 0.0), axis=1, keepdims=True)
                cut = pl.ds(pl.multiple_of(h * LATENT, LATENT), LATENT)
                o_ref[rows, cut] = (
                    o_ref[rows, cut].astype(jnp.float32) * keep + add * key_low
                ).astype(jnp.bfloat16)
        store(g).start()

    @pl.loop(0, groups)
    def _(g):
        store(g).wait()

    hidden_copy.wait()


def tail(hidden_in, back, kv_gain, cosine, sine, top, total, place_weight, w_all, queries, o):
    rows, width = hidden_in.shape
    parts, groups = 7, 8
    vmem = pl.BlockSpec(memory_space=pltpu.VMEM)
    hbm = pl.BlockSpec(memory_space=pl.ANY)
    return pl.pallas_call(
        functools.partial(tail_kernel, parts, groups),
        out_shape=[
            jax.ShapeDtypeStruct((rows, width), jnp.bfloat16),
            jax.ShapeDtypeStruct((rows, HEADS * LATENT), jnp.bfloat16),
        ],
        in_specs=[hbm] * 2 + [vmem] * 6 + [hbm] * 3,
        out_specs=[hbm] * 2,
        scratch_shapes=[
            pltpu.VMEM(w_all.shape, jnp.bfloat16),
            pltpu.VMEM(queries.shape, jnp.bfloat16),
            pltpu.VMEM(o.shape, jnp.bfloat16),
            pltpu.VMEM((rows, width), jnp.bfloat16),
            pltpu.VMEM(back.shape, jnp.bfloat16),
            pltpu.VMEM((rows, width), jnp.bfloat16),
            pltpu.VMEM((rows, 2 * KVW), jnp.float32),
            pltpu.VMEM((rows, HEADS), jnp.float32),
            pltpu.VMEM((rows, HEADS), jnp.float32),
            pltpu.SemaphoreType.DMA((2,)),
            pltpu.SemaphoreType.DMA((parts,)),
            pltpu.SemaphoreType.DMA((groups,)),
            pltpu.SemaphoreType.DMA((groups,)),
            pltpu.SemaphoreType.DMA,
            pltpu.SemaphoreType.DMA((groups,)),
        ],
        compiler_params=pltpu.CompilerParams(vmem_limit_bytes=58 * MIB),
        cost_estimate=pl.CostEstimate(
            flops=2 * rows * width * KVW,
            bytes_accessed=2 * (w_all.size + queries.size + 2 * o.size),
            transcendentals=rows * HEADS * 2,
        ),
        name="tail",
    )(
        hidden_in,
        back,
        kv_gain.reshape(1, LATENT),
        cosine,
        sine,
        top,
        total,
        place_weight,
        w_all,
        queries,
        o,
    )


def plus(*terms):
    total = terms[0].astype(jnp.float32)
    for term in terms[1:]:
        total = total + term.astype(jnp.float32)
    return total.astype(jnp.bfloat16)


def round_trip(piece, axis, index):
    rows = piece.shape[0]
    joined = jnp.zeros((SIDE * rows, piece.shape[1]), piece.dtype)
    for step in range(SIDE):
        part = piece if step == 0 else shift(piece, axis, -step)
        at = jnp.bitwise_and(index + step, SIDE - 1) * rows
        joined = lax.dynamic_update_slice_in_dim(joined, part, at, axis=0)
    return joined


def after(values, *others):
    return lax.optimization_barrier((values, others))[0]


def body(
    hidden_in,
    norm_gain,
    route_logits,
    expert_ids,
    w_gate,
    w_up,
    w_down,
    w_latent,
    kv_gain,
    queries,
    page_pool,
    page_table,
    kv_lengths,
    migration,
):
    dp_count = lax.axis_size("dp")
    ex_count = lax.axis_size("expert")
    row_count = hidden_in.shape[0]
    local_experts = w_gate.shape[0]
    window = local_experts * dp_count
    width = hidden_in.shape[1]
    x_wide = hidden_in.astype(jnp.float32)
    normed = rms_rows(x_wide, norm_gain).astype(jnp.bfloat16)
    in_window = expert_ids < window
    has = jnp.any(in_window, axis=1)
    chosen = jnp.sum(jnp.where(in_window, expert_ids, 0), axis=1)
    sigma = jax.nn.sigmoid(route_logits)
    weight = (
        routed_scale * jnp.sum(jnp.where(in_window, sigma, 0.0), axis=1) / jnp.sum(sigma, axis=1)
    )
    onehot = ((chosen[:, None] == jnp.arange(window)[None, :]) & has[:, None]).astype(jnp.int32)
    rank = jnp.cumsum(onehot, axis=0) - onehot
    slot = jnp.sum(rank * onehot, axis=1)
    slots = local_experts * CAP
    place = chosen * CAP + slot
    pick = (place[:, None] == jnp.arange(window * CAP)[None, :]) & has[:, None]
    packed = jnp.einsum(
        "rs,rd->sd", pick.astype(jnp.bfloat16), normed, preferred_element_type=jnp.float32
    ).astype(jnp.bfloat16)
    place_weight = jnp.where(pick, weight[:, None], 0.0)
    arrived = lax.all_to_all(
        packed.reshape(dp_count, slots, width), "dp", split_axis=0, concat_axis=0, tiled=True
    )
    outgoing = jnp.take(page_pool, migration.reshape(dp_count * MCAP), axis=0, mode="clip")
    query = queries.reshape(row_count, HEADS, KVW)
    arrived = after(arrived, outgoing, query)
    arrived = arrived.reshape(window * CAP, width)
    axes = (("z", "x"), ("x", "z"))
    both = range(2)
    n = arrived.shape[0] // 2
    rows = [arrived[k * n : (k + 1) * n] for k in both]
    weights = (w_gate, w_up, w_down)

    below = [shift(rows[k], axes[k][0], 1) for k in both]
    above = [shift(rows[k], axes[k][0], -1) for k in both]
    below, above = after((below, above))
    beyond = [shift(above[k], axes[k][0], -1) for k in both]
    low = pack([(rows[k], below[k]) for k in both])
    below_low = [shift(low[k], axes[k][1], 1) for k in both]
    low_too, beyond = after((low, beyond))
    above_low = [shift(low_too[k], axes[k][1], -1) for k in both]
    high = pack([(above[k], beyond[k]) for k in both])
    more = lax.all_to_all(
        after(outgoing, high).reshape(dp_count, MCAP, page_pool.shape[1]),
        "dp",
        split_axis=0,
        concat_axis=0,
        tiled=True,
    ).reshape(dp_count * MCAP, PAGE, KVW)
    pool = after(page_pool, high).reshape(page_pool.shape[0], PAGE, KVW)
    below_high = [shift(high[k], axes[k][1], 1) for k in both]
    above_high = [shift(high[k], axes[k][1], -1) for k in both]
    y_first = ffn([[low[k], high[k], below_low[k], above_low[k]] for k in both], *weights)
    below_low, above_high, below_high, above_low = after(
        (below_low, above_high, below_high, above_low), y_first, pool
    )
    far_low = [shift(below_low[k], axes[k][1], 1) for k in both]
    far_high = [shift(above_high[k], axes[k][1], -1) for k in both]
    y_second = ffn([[below_high[k], above_high[k]] for k in both], *weights)
    y_first = after(y_first, y_second)
    early_down = [shift(y_first[k][2], axes[k][1], -1) for k in both]
    early_up = [shift(y_second[k][1], axes[k][1], 1) for k in both]
    index = lax.axis_index("expert")
    w_line = round_trip(after(w_latent, y_first), "z", jnp.bitwise_and(index, SIDE - 1))
    far_low, far_high = after((far_low, far_high), y_second, w_line, more)
    y_far = ffn([[far_low[k], far_high[k]] for k in both], *weights)
    y_far, early_down, early_up = after((y_far, early_down, early_up))
    relay_up = [shift(y_far[k][0], axes[k][1], 1) for k in both]
    relay_down = [shift(y_far[k][1], axes[k][1], -1) for k in both]
    w_plane = round_trip(after(w_line, y_second), "x", jnp.right_shift(index, 2))
    w_all = lax.all_gather(w_plane, "dp", axis=0, tiled=True)
    query = after(query, y_far)
    cached, top, total = attend_cached(query, pool, more, page_table, kv_lengths)
    relay_up, relay_down = after((relay_up, relay_down), cached, w_plane)
    late_up = [shift(plus(y_first[k][3], relay_up[k]), axes[k][1], 1) for k in both]
    late_down = [shift(plus(y_second[k][0], relay_down[k]), axes[k][1], -1) for k in both]
    cached = cached.reshape(row_count, HEADS * LATENT)
    late_up, late_down = after((late_up, late_down), cached)
    terms_low = [(y_first[k][0], late_up[k], early_down[k]) for k in both]
    terms_high = [(y_first[k][1], early_up[k], late_down[k]) for k in both]
    for_far = [plus(*(term[n:] for term in terms_high[k])) for k in both]
    for_below = [plus(*(term[n:] for term in terms_low[k])) for k in both]
    relayed = [shift(for_far[k], axes[k][0], 1) for k in both]
    from_above = [shift(for_below[k], axes[k][0], -1) for k in both]
    relayed, from_above = after((relayed, from_above))
    from_below = [
        shift(plus(*(term[:n] for term in terms_high[k]), relayed[k]), axes[k][0], 1) for k in both
    ]
    from_below = after(from_below)
    finished = [
        plus(*(term[:n] for term in terms_low[k]), from_below[k], from_above[k]) for k in both
    ]
    back = lax.all_to_all(
        jnp.concatenate(finished, axis=0).reshape(dp_count, slots, width),
        "dp",
        split_axis=0,
        concat_axis=0,
        tiled=True,
    ).reshape(window * CAP, width)

    half = (KVW - LATENT) // 2
    freq = 10000.0 ** (-jnp.arange(half, dtype=jnp.float32) / half)
    angle = kv_lengths.astype(jnp.float32)[:, None] * freq[None, :]
    return tuple(
        tail(
            hidden_in,
            back,
            kv_gain,
            jnp.cos(angle),
            jnp.sin(angle),
            top,
            total,
            place_weight,
            w_all,
            queries,
            cached,
        )
    )


def solution(mesh):
    return jax.shard_map(
        body,
        mesh=mesh,
        in_specs=(
            P(("dp", "expert"), None),
            P(),
            P(("dp", "expert"), None),
            P(("dp", "expert"), None),
            P("dp", None, "expert"),
            P("dp", None, "expert"),
            P("dp", "expert", None),
            P(("dp", "expert"), None),
            P(),
            P(("dp", "expert"), None),
            P(("dp", "expert"), None),
            P(("dp", "expert"), None),
            P(("dp", "expert")),
            P("dp", "expert", None, None),
        ),
        out_specs=(P(("dp", "expert"), None), P(("dp", "expert"), None)),
        check_vma=False,
    )
```

```python
import functools

import jax
import jax.numpy as jnp
from jax import lax
from jax.experimental import pallas as pl
from jax.experimental.pallas import tpu as pltpu
from jax.sharding import PartitionSpec as P

HEADS = 64
LATENT = 512
PAGE = 16
MAXP = 6
CAP = 4
MCAP = 4
KVW = 576
SIDE = 4

softmax_scale = 192.0 ** (-0.5)
routed_scale = 2.5
norm_eps = 1e-06
MIB = 1 << 20


def rms_rows(values, gain):
    stat = jnp.mean(values * values, axis=-1, keepdims=True)
    return values * lax.rsqrt(stat + norm_eps) * gain


def shift(value, axis, step):
    pairs = []
    for x in range(SIDE):
        for z in range(SIDE):
            to_x = (x + step) % SIDE if axis == "x" else x
            to_z = (z + step) % SIDE if axis == "z" else z
            pairs.append((x * SIDE + z, to_x * SIDE + to_z))
    return lax.ppermute(value, "expert", pairs)


def ffn_kernel(count, rows, parts, *refs):
    xs = refs[:count]
    gate_hbm, up_hbm, down_hbm = refs[count : count + 3]
    outs = refs[count + 3 : 2 * count + 3]
    x_buf, w_buf, d_buf, o_buf, acc, in_sem, w_sem, d_sem, out_sem = refs[2 * count + 3 :]
    depth = gate_hbm.shape[1]
    piece = depth // parts

    def loads(c):
        cut = pl.ds(pl.multiple_of(c * piece, piece), piece)
        for e in range(2):
            for j, source in enumerate((gate_hbm, up_hbm)):
                yield pltpu.make_async_copy(
                    source.at[e, cut],
                    w_buf.at[cut, pl.ds(256 * e + 128 * j, 128)],
                    w_sem.at[c, 2 * e + j],
                )
        for i in range(count):
            yield pltpu.make_async_copy(
                xs[i].at[:, cut], x_buf.at[pl.ds(i * rows, rows), cut], in_sem.at[c, i]
            )

    def stores(c):
        cut = pl.ds(pl.multiple_of(c * piece, piece), piece)
        for i in range(count):
            yield pltpu.make_async_copy(
                o_buf.at[pl.ds(i * rows, rows), cut], outs[i].at[:, cut], out_sem.at[c, i]
            )

    @pl.loop(0, parts)
    def _(c):
        for copy in loads(c):
            copy.start()

    down = [
        pltpu.make_async_copy(down_hbm.at[e], d_buf.at[pl.ds(128 * e, 128)], d_sem.at[e])
        for e in range(2)
    ]
    for copy in down:
        copy.start()
    acc[...] = jnp.zeros_like(acc)

    @pl.loop(0, parts)
    def _(c):
        for copy in loads(c):
            copy.wait()
        cut = pl.ds(pl.multiple_of(c * piece, piece), piece)
        acc[...] += jnp.dot(x_buf[:, cut], w_buf[cut, :], preferred_element_type=jnp.float32)

    first = lax.broadcasted_iota(jnp.int32, (rows * count, 128), 0) % (2 * CAP) < CAP
    gate = jnp.where(first, acc[:, :128], acc[:, 256:384])
    up = jnp.where(first, acc[:, 128:256], acc[:, 384:])
    active = gate / (1.0 + jnp.exp(-gate)) * up
    active = jnp.concatenate(
        [jnp.where(first, active, 0.0), jnp.where(first, 0.0, active)], axis=1
    ).astype(jnp.bfloat16)
    for copy in down:
        copy.wait()

    @pl.loop(0, parts)
    def _(c):
        cut = pl.ds(pl.multiple_of(c * piece, piece), piece)
        o_buf[:, cut] = jnp.dot(active, d_buf[:, cut], preferred_element_type=jnp.float32).astype(
            jnp.bfloat16
        )
        for copy in stores(c):
            copy.start()

    @pl.loop(0, parts)
    def _(c):
        for copy in stores(c):
            copy.wait()


def ffn(blocks, w_gate, w_up, w_down):
    chains, per_chain = len(blocks), len(blocks[0])
    flat = [block for part in blocks for block in part]
    count, rows, depth, parts = len(flat), flat[0].shape[0], w_gate.shape[1], 4
    total = rows * count
    done = pl.pallas_call(
        functools.partial(ffn_kernel, count, rows, parts),
        out_shape=[jax.ShapeDtypeStruct(block.shape, jnp.bfloat16) for block in flat],
        in_specs=[pl.BlockSpec(memory_space=pl.ANY)] * (count + 3),
        out_specs=[pl.BlockSpec(memory_space=pl.ANY)] * count,
        scratch_shapes=[
            pltpu.VMEM((total, depth), jnp.bfloat16),
            pltpu.VMEM((depth, 512), jnp.bfloat16),
            pltpu.VMEM((256, depth), jnp.bfloat16),
            pltpu.VMEM((total, depth), jnp.bfloat16),
            pltpu.VMEM((total, 512), jnp.float32),
            pltpu.SemaphoreType.DMA((parts, count)),
            pltpu.SemaphoreType.DMA((parts, 4)),
            pltpu.SemaphoreType.DMA((2,)),
            pltpu.SemaphoreType.DMA((parts, count)),
        ],
        compiler_params=pltpu.CompilerParams(vmem_limit_bytes=58 * MIB),
        cost_estimate=pl.CostEstimate(
            flops=2 * total * depth * 768,
            bytes_accessed=2 * depth * (768 + 2 * total),
            transcendentals=total * 128,
        ),
        name="ffn",
    )(*flat, w_gate, w_up, w_down)
    return [done[k * per_chain : (k + 1) * per_chain] for k in range(chains)]


def attend_kernel(
    step, table, lengths, q_ref, pool_hbm, more_hbm, out_ref, top_ref, total_ref, pages, sem
):
    own_pages = pool_hbm.shape[0]

    @pl.when(pl.program_id(0) == 0)
    def _():
        copies = [
            pltpu.make_async_copy(pool_hbm, pages.at[pl.ds(0, own_pages)], sem.at[0]),
            pltpu.make_async_copy(
                more_hbm, pages.at[pl.ds(own_pages, more_hbm.shape[0])], sem.at[1]
            ),
        ]
        for copy in copies:
            copy.start()
        for copy in copies:
            copy.wait()

    first = pl.program_id(0) * step
    keys = [
        jnp.concatenate([pages[table[(first + r) * MAXP + p]] for p in range(MAXP)], axis=0)
        for r in range(step)
    ]
    scores = jnp.concatenate(
        [
            lax.dot_general(
                keys[r], q_ref[r], (((1,), (1,)), ((), ())), preferred_element_type=jnp.float32
            )
            for r in range(step)
        ],
        axis=1,
    )
    scores = scores * softmax_scale
    column = lax.broadcasted_iota(jnp.int32, (1, step * HEADS), 1) // HEADS
    length = jnp.zeros_like(column)
    for r in range(step):
        length = jnp.where(column == r, lengths[first + r], length)
    valid = lax.broadcasted_iota(jnp.int32, scores.shape, 0) < length
    scores = jnp.where(valid, scores, -1e30)
    top = jnp.max(scores, axis=0, keepdims=True)
    expo = jnp.where(valid, jnp.exp(scores - top), 0.0)
    total = jnp.sum(expo, axis=0, keepdims=True)
    probs = (expo / total).astype(jnp.bfloat16)
    for r in range(step):
        cut = slice(r * HEADS, (r + 1) * HEADS)
        out_ref[r] = lax.dot_general(
            probs[:, cut],
            keys[r][:, :LATENT],
            (((0,), (0,)), ((), ())),
            preferred_element_type=jnp.float32,
        ).astype(jnp.bfloat16)
        top_ref[r : r + 1, :] = top[:, cut]
        total_ref[r : r + 1, :] = total[:, cut]


def attend_cached(query, pool, more, page_table, kv_lengths):
    rows, step = query.shape[0], 8
    entries = pool.shape[0] + more.shape[0]
    hbm = pl.BlockSpec(memory_space=pl.ANY)
    return pl.pallas_call(
        functools.partial(attend_kernel, step),
        out_shape=[
            jax.ShapeDtypeStruct((rows, HEADS, LATENT), jnp.bfloat16),
            jax.ShapeDtypeStruct((rows, HEADS), jnp.float32),
            jax.ShapeDtypeStruct((rows, HEADS), jnp.float32),
        ],
        grid_spec=pltpu.PrefetchScalarGridSpec(
            num_scalar_prefetch=2,
            grid=(rows // step,),
            in_specs=[pl.BlockSpec((step, HEADS, KVW), lambda i, t, n: (i, 0, 0)), hbm, hbm],
            out_specs=[
                pl.BlockSpec((step, HEADS, LATENT), lambda i, t, n: (i, 0, 0)),
                pl.BlockSpec((step, HEADS), lambda i, t, n: (i, 0)),
                pl.BlockSpec((step, HEADS), lambda i, t, n: (i, 0)),
            ],
            scratch_shapes=[
                pltpu.VMEM((entries, PAGE, KVW), jnp.bfloat16),
                pltpu.SemaphoreType.DMA((2,)),
            ],
        ),
        compiler_params=pltpu.CompilerParams(vmem_limit_bytes=58 * MIB),
        cost_estimate=pl.CostEstimate(
            flops=2 * rows * HEADS * MAXP * PAGE * (KVW + LATENT),
            bytes_accessed=2 * (query.size + entries * PAGE * KVW + rows * HEADS * LATENT),
            transcendentals=rows * HEADS * MAXP * PAGE,
        ),
        name="attend_cached",
    )(page_table.reshape(rows * MAXP), kv_lengths, query, pool, more)


def pack_kernel(count, *refs):
    blocks, joined = refs[: 2 * count], refs[2 * count : 3 * count]
    buf, in_sem, out_sem = refs[3 * count :]
    n = blocks[0].shape[0]
    loads = [
        pltpu.make_async_copy(blocks[i], buf.at[i // 2, pl.ds(i % 2 * n, n)], in_sem.at[i])
        for i in range(2 * count)
    ]
    stores = [pltpu.make_async_copy(buf.at[i], joined[i], out_sem.at[i]) for i in range(count)]
    for copy in loads:
        copy.start()
    for i in range(count):
        loads[2 * i].wait()
        loads[2 * i + 1].wait()
        stores[i].start()
    for copy in stores:
        copy.wait()


def pack(pairs):
    count, (n, width) = len(pairs), pairs[0][0].shape
    hbm = pl.BlockSpec(memory_space=pl.ANY)
    return pl.pallas_call(
        functools.partial(pack_kernel, count),
        out_shape=[jax.ShapeDtypeStruct((2 * n, width), jnp.bfloat16)] * count,
        in_specs=[hbm] * (2 * count),
        out_specs=[hbm] * count,
        scratch_shapes=[
            pltpu.VMEM((count, 2 * n, width), jnp.bfloat16),
            pltpu.SemaphoreType.DMA((2 * count,)),
            pltpu.SemaphoreType.DMA((count,)),
        ],
        compiler_params=pltpu.CompilerParams(vmem_limit_bytes=58 * MIB),
        cost_estimate=pl.CostEstimate(
            flops=0, bytes_accessed=8 * count * n * width, transcendentals=0
        ),
        name="pack",
    )(*(block for pair in pairs for block in pair))


def tail_kernel(
    parts,
    groups,
    hidden_hbm,
    back_hbm,
    gain_ref,
    cos_ref,
    sin_ref,
    top_ref,
    total_ref,
    place_ref,
    w_hbm,
    q_hbm,
    o_hbm,
    hidden_out_hbm,
    out_hbm,
    w_ref,
    q_ref,
    o_ref,
    hidden_ref,
    back_ref,
    hidden_buf,
    key_buf,
    own_buf,
    keep_buf,
    in_sem,
    w_sem,
    q_sem,
    o_sem,
    hidden_sem,
    out_sem,
):
    width = hidden_ref.shape[1]
    loads = [
        pltpu.make_async_copy(back_hbm, back_ref, in_sem.at[0]),
        pltpu.make_async_copy(hidden_hbm, hidden_ref, in_sem.at[1]),
    ]
    for copy in loads:
        copy.start()
    piece = width // parts
    per_group = HEADS // groups
    span, q_span = per_group * LATENT, per_group * KVW

    def w_load(c):
        cut = pl.ds(pl.multiple_of(c * piece, piece), piece)
        return pltpu.make_async_copy(w_hbm.at[cut], w_ref.at[cut], w_sem.at[c])

    def q_load(g):
        cut = pl.ds(pl.multiple_of(g * q_span, 128), q_span)
        return pltpu.make_async_copy(q_hbm.at[:, cut], q_ref.at[:, cut], q_sem.at[g])

    def o_load(g):
        cut = pl.ds(pl.multiple_of(g * span, span), span)
        return pltpu.make_async_copy(o_hbm.at[:, cut], o_ref.at[:, cut], o_sem.at[g])

    def store(g):
        cut = pl.ds(pl.multiple_of(g * span, span), span)
        return pltpu.make_async_copy(o_ref.at[:, cut], out_hbm.at[:, cut], out_sem.at[g])

    for c in range(parts):
        w_load(c).start()

    @pl.loop(0, groups)
    def _(g):
        q_load(g).start()

    @pl.loop(0, groups)
    def _(g):
        o_load(g).start()

    place = place_ref[...]
    pick = (place != 0.0).astype(jnp.bfloat16)
    weight = jnp.sum(place, axis=1, keepdims=True)
    projected = jnp.zeros((hidden_ref.shape[0], KVW), jnp.float32)
    for copy in loads:
        copy.wait()
    for c in range(parts):
        cut = slice(c * piece, (c + 1) * piece)
        picked = jnp.dot(pick, back_ref[:, cut], preferred_element_type=jnp.float32)
        hidden = (hidden_ref[:, cut].astype(jnp.float32) + weight * picked).astype(jnp.bfloat16)
        hidden_buf[:, cut] = hidden
        w_load(c).wait()
        projected += jnp.dot(hidden, w_ref[cut, :], preferred_element_type=jnp.float32)
    hidden_copy = pltpu.make_async_copy(hidden_buf, hidden_out_hbm, hidden_sem)
    hidden_copy.start()
    latent = rms_rows(projected[:, :LATENT], gain_ref[...])
    first = projected[:, LATENT : LATENT + 32]
    second = projected[:, LATENT + 32 :]
    cosine, sine = cos_ref[...], sin_ref[...]
    new_key = jnp.concatenate(
        [latent, first * cosine - second * sine, second * cosine + first * sine], axis=1
    )
    new_key = new_key.astype(jnp.bfloat16).astype(jnp.float32)
    key_buf[...] = jnp.concatenate([new_key, new_key], axis=1)
    lane = lax.broadcasted_iota(jnp.int32, (8, 128), 1)
    head = lax.broadcasted_iota(jnp.int32, (8, HEADS), 1)
    blocks = hidden_ref.shape[0] // 8
    own_buf[...] = jnp.zeros_like(own_buf)

    @pl.loop(0, HEADS // 2)
    def _(j):
        @pl.when(j % (per_group // 2) == 0)
        def _():
            q_load(j // (per_group // 2)).wait()

        cut = pl.ds(pl.multiple_of(j * 2 * KVW, 128), 2 * KVW)
        for b in range(blocks):
            rows = slice(8 * b, 8 * b + 8)
            product = q_ref[rows, cut].astype(jnp.float32) * key_buf[rows, :]
            tiles = [product[:, 128 * i : 128 * (i + 1)] for i in range(9)]
            low = (tiles[0] + tiles[1]) + (tiles[2] + tiles[3]) + jnp.where(lane < 64, tiles[4], 0.0)
            high = (tiles[5] + tiles[6]) + (tiles[7] + tiles[8])
            high = high + jnp.where(lane < 64, 0.0, tiles[4])
            low = jnp.sum(low, axis=1, keepdims=True)
            high = jnp.sum(high, axis=1, keepdims=True)
            own_buf[rows, :] = jnp.where(
                head == 2 * j, low, jnp.where(head == 2 * j + 1, high, own_buf[rows, :])
            )

    own = own_buf[...] * softmax_scale
    top_old = top_ref[...]
    top = jnp.maximum(top_old, own)
    part = total_ref[...] * jnp.exp(top_old - top)
    part_own = jnp.exp(own - top)
    inverse = 1.0 / (part + part_own)
    keep_buf[...] = part * inverse
    own_buf[...] = (part_own * inverse).astype(jnp.bfloat16).astype(jnp.float32)

    @pl.loop(0, groups)
    def _(g):
        o_load(g).wait()
        for b in range(blocks):
            rows = slice(8 * b, 8 * b + 8)
            key_low = key_buf[rows, :LATENT]
            keeps, adds = keep_buf[rows, :], own_buf[rows, :]
            for i in range(per_group):
                h = g * per_group + i
                keep = jnp.sum(jnp.where(head == h, keeps, 0.0), axis=1, keepdims=True)
                add = jnp.sum(jnp.where(head == h, adds, 0.0), axis=1, keepdims=True)
                cut = pl.ds(pl.multiple_of(h * LATENT, LATENT), LATENT)
                o_ref[rows, cut] = (
                    o_ref[rows, cut].astype(jnp.float32) * keep + add * key_low
                ).astype(jnp.bfloat16)
        store(g).start()

    @pl.loop(0, groups)
    def _(g):
        store(g).wait()

    hidden_copy.wait()


def tail(hidden_in, back, kv_gain, cosine, sine, top, total, place_weight, w_all, queries, o):
    rows, width = hidden_in.shape
    parts, groups = 7, 8
    vmem = pl.BlockSpec(memory_space=pltpu.VMEM)
    hbm = pl.BlockSpec(memory_space=pl.ANY)
    return pl.pallas_call(
        functools.partial(tail_kernel, parts, groups),
        out_shape=[
            jax.ShapeDtypeStruct((rows, width), jnp.bfloat16),
            jax.ShapeDtypeStruct((rows, HEADS * LATENT), jnp.bfloat16),
        ],
        in_specs=[hbm] * 2 + [vmem] * 6 + [hbm] * 3,
        out_specs=[hbm] * 2,
        scratch_shapes=[
            pltpu.VMEM(w_all.shape, jnp.bfloat16),
            pltpu.VMEM(queries.shape, jnp.bfloat16),
            pltpu.VMEM(o.shape, jnp.bfloat16),
            pltpu.VMEM((rows, width), jnp.bfloat16),
            pltpu.VMEM(back.shape, jnp.bfloat16),
            pltpu.VMEM((rows, width), jnp.bfloat16),
            pltpu.VMEM((rows, 2 * KVW), jnp.float32),
            pltpu.VMEM((rows, HEADS), jnp.float32),
            pltpu.VMEM((rows, HEADS), jnp.float32),
            pltpu.SemaphoreType.DMA((2,)),
            pltpu.SemaphoreType.DMA((parts,)),
            pltpu.SemaphoreType.DMA((groups,)),
            pltpu.SemaphoreType.DMA((groups,)),
            pltpu.SemaphoreType.DMA,
            pltpu.SemaphoreType.DMA((groups,)),
        ],
        compiler_params=pltpu.CompilerParams(vmem_limit_bytes=58 * MIB),
        cost_estimate=pl.CostEstimate(
            flops=2 * rows * width * KVW,
            bytes_accessed=2 * (w_all.size + queries.size + 2 * o.size),
            transcendentals=rows * HEADS * 2,
        ),
        name="tail",
    )(
        hidden_in,
        back,
        kv_gain.reshape(1, LATENT),
        cosine,
        sine,
        top,
        total,
        place_weight,
        w_all,
        queries,
        o,
    )


def plus(*terms):
    total = terms[0].astype(jnp.float32)
    for term in terms[1:]:
        total = total + term.astype(jnp.float32)
    return total.astype(jnp.bfloat16)


def after(values, *others):
    return lax.optimization_barrier((values, others))[0]


def body(
    hidden_in,
    norm_gain,
    route_logits,
    expert_ids,
    w_gate,
    w_up,
    w_down,
    w_latent,
    kv_gain,
    queries,
    page_pool,
    page_table,
    kv_lengths,
    migration,
):
    dp_count = lax.axis_size("dp")
    ex_count = lax.axis_size("expert")
    row_count = hidden_in.shape[0]
    local_experts = w_gate.shape[0]
    window = local_experts * dp_count
    width = hidden_in.shape[1]
    w_plane = lax.all_gather(jnp.concatenate([w_latent] * 2, axis=0), "expert", axis=0, tiled=True)
    x_wide = hidden_in.astype(jnp.float32)
    normed = rms_rows(x_wide, norm_gain).astype(jnp.bfloat16)
    in_window = expert_ids < window
    has = jnp.any(in_window, axis=1)
    chosen = jnp.sum(jnp.where(in_window, expert_ids, 0), axis=1)
    sigma = jax.nn.sigmoid(route_logits)
    weight = (
        routed_scale * jnp.sum(jnp.where(in_window, sigma, 0.0), axis=1) / jnp.sum(sigma, axis=1)
    )
    onehot = ((chosen[:, None] == jnp.arange(window)[None, :]) & has[:, None]).astype(jnp.int32)
    rank = jnp.cumsum(onehot, axis=0) - onehot
    slot = jnp.sum(rank * onehot, axis=1)
    slots = local_experts * CAP
    place = chosen * CAP + slot
    pick = (place[:, None] == jnp.arange(window * CAP)[None, :]) & has[:, None]
    packed = jnp.einsum(
        "rs,rd->sd", pick.astype(jnp.bfloat16), normed, preferred_element_type=jnp.float32
    ).astype(jnp.bfloat16)
    place_weight = jnp.where(pick, weight[:, None], 0.0)
    arrived = lax.all_to_all(
        packed.reshape(dp_count, slots, width), "dp", split_axis=0, concat_axis=0, tiled=True
    )
    outgoing = jnp.take(page_pool, migration.reshape(dp_count * MCAP), axis=0, mode="clip")
    query = queries.reshape(row_count, HEADS, KVW)
    arrived = after(arrived, outgoing, query)
    arrived = arrived.reshape(window * CAP, width)
    axes = (("z", "x"), ("x", "z"))
    both = range(2)
    n = arrived.shape[0] // 2
    rows = [arrived[k * n : (k + 1) * n] for k in both]
    weights = (w_gate, w_up, w_down)

    below = [shift(rows[k], axes[k][0], 1) for k in both]
    above = [shift(rows[k], axes[k][0], -1) for k in both]
    below, above, w_plane = after((below, above, w_plane))
    w_plane = w_plane.reshape(ex_count, 2 * w_latent.shape[0], KVW)[:, : w_latent.shape[0]]
    w_all = lax.all_gather(
        w_plane.reshape(ex_count * w_latent.shape[0], KVW), "dp", axis=0, tiled=True
    )
    beyond = [shift(above[k], axes[k][0], -1) for k in both]
    low = pack([(rows[k], below[k]) for k in both])
    below_low = [shift(low[k], axes[k][1], 1) for k in both]
    low_too, beyond = after((low, beyond))
    above_low = [shift(low_too[k], axes[k][1], -1) for k in both]
    high = pack([(above[k], beyond[k]) for k in both])
    more = lax.all_to_all(
        after(outgoing, high).reshape(dp_count, MCAP, page_pool.shape[1]),
        "dp",
        split_axis=0,
        concat_axis=0,
        tiled=True,
    ).reshape(dp_count * MCAP, PAGE, KVW)
    pool = after(page_pool, high).reshape(page_pool.shape[0], PAGE, KVW)
    below_high = [shift(high[k], axes[k][1], 1) for k in both]
    above_high = [shift(high[k], axes[k][1], -1) for k in both]
    y_first = ffn([[low[k], high[k], below_low[k], above_low[k]] for k in both], *weights)
    below_low, above_high, below_high, above_low = after(
        (below_low, above_high, below_high, above_low), y_first, pool, more
    )
    far_low = [shift(below_low[k], axes[k][1], 1) for k in both]
    far_high = [shift(above_high[k], axes[k][1], -1) for k in both]
    y_second = ffn([[below_high[k], above_high[k]] for k in both], *weights)
    y_first = after(y_first, y_second)
    early_down = [shift(y_first[k][2], axes[k][1], -1) for k in both]
    early_up = [shift(y_second[k][1], axes[k][1], 1) for k in both]
    far_low, far_high = after((far_low, far_high), y_second)
    y_far = ffn([[far_low[k], far_high[k]] for k in both], *weights)
    y_far, early_down, early_up = after((y_far, early_down, early_up))
    relay_up = [shift(y_far[k][0], axes[k][1], 1) for k in both]
    relay_down = [shift(y_far[k][1], axes[k][1], -1) for k in both]
    query = after(query, y_far)
    cached, top, total = attend_cached(query, pool, more, page_table, kv_lengths)
    relay_up, relay_down = after((relay_up, relay_down), cached)
    late_up = [shift(plus(y_first[k][3], relay_up[k]), axes[k][1], 1) for k in both]
    late_down = [shift(plus(y_second[k][0], relay_down[k]), axes[k][1], -1) for k in both]
    cached = cached.reshape(row_count, HEADS * LATENT)
    late_up, late_down = after((late_up, late_down), cached)
    terms_low = [(y_first[k][0], late_up[k], early_down[k]) for k in both]
    terms_high = [(y_first[k][1], early_up[k], late_down[k]) for k in both]
    for_far = [plus(*(term[n:] for term in terms_high[k])) for k in both]
    for_below = [plus(*(term[n:] for term in terms_low[k])) for k in both]
    relayed = [shift(for_far[k], axes[k][0], 1) for k in both]
    from_above = [shift(for_below[k], axes[k][0], -1) for k in both]
    relayed, from_above = after((relayed, from_above))
    from_below = [
        shift(plus(*(term[:n] for term in terms_high[k]), relayed[k]), axes[k][0], 1) for k in both
    ]
    from_below = after(from_below)
    finished = [
        plus(*(term[:n] for term in terms_low[k]), from_below[k], from_above[k]) for k in both
    ]
    back = lax.all_to_all(
        jnp.concatenate(finished, axis=0).reshape(dp_count, slots, width),
        "dp",
        split_axis=0,
        concat_axis=0,
        tiled=True,
    ).reshape(window * CAP, width)

    half = (KVW - LATENT) // 2
    freq = 10000.0 ** (-jnp.arange(half, dtype=jnp.float32) / half)
    angle = kv_lengths.astype(jnp.float32)[:, None] * freq[None, :]
    return tuple(
        tail(
            hidden_in,
            back,
            kv_gain,
            jnp.cos(angle),
            jnp.sin(angle),
            top,
            total,
            place_weight,
            w_all,
            queries,
            cached,
        )
    )


def solution(mesh):
    return jax.shard_map(
        body,
        mesh=mesh,
        in_specs=(
            P(("dp", "expert"), None),
            P(),
            P(("dp", "expert"), None),
            P(("dp", "expert"), None),
            P("dp", None, "expert"),
            P("dp", None, "expert"),
            P("dp", "expert", None),
            P(("dp", "expert"), None),
            P(),
            P(("dp", "expert"), None),
            P(("dp", "expert"), None),
            P(("dp", "expert"), None),
            P(("dp", "expert")),
            P("dp", "expert", None, None),
        ),
        out_specs=(P(("dp", "expert"), None), P(("dp", "expert"), None)),
        check_vma=False,
    )
```

```python
import functools

import jax
import jax.numpy as jnp
from jax import lax
from jax.experimental import pallas as pl
from jax.experimental.pallas import tpu as pltpu
from jax.sharding import PartitionSpec as P

HEADS = 64
LATENT = 512
PAGE = 16
MAXP = 6
CAP = 4
MCAP = 4
KVW = 576
SIDE = 4

softmax_scale = 192.0 ** (-0.5)
routed_scale = 2.5
norm_eps = 1e-06
MIB = 1 << 20


def rms_rows(values, gain):
    stat = jnp.mean(values * values, axis=-1, keepdims=True)
    return values * lax.rsqrt(stat + norm_eps) * gain


def shift(value, axis, step):
    pairs = []
    for x in range(SIDE):
        for z in range(SIDE):
            to_x = (x + step) % SIDE if axis == "x" else x
            to_z = (z + step) % SIDE if axis == "z" else z
            pairs.append((x * SIDE + z, to_x * SIDE + to_z))
    return lax.ppermute(value, "expert", pairs)


def dispatch_kernel(
    window, parts, ids_ref, logits_ref, gain_ref, hidden_hbm, packed_hbm, place_ref, x_buf, out_buf, in_sem, out_sem
):
    rows, width = hidden_hbm.shape
    piece = width // parts

    def load(c):
        cut = pl.ds(c * piece, piece)
        return pltpu.make_async_copy(hidden_hbm.at[:, cut], x_buf.at[:, cut], in_sem.at[c])

    def store(c):
        cut = pl.ds(c * piece, piece)
        return pltpu.make_async_copy(out_buf.at[:, cut], packed_hbm.at[:, cut], out_sem.at[c])

    for c in range(parts):
        load(c).start()
    ids = ids_ref[...]
    inside = ids < window
    has = jnp.max(inside.astype(jnp.int32), axis=0, keepdims=True)
    chosen = jnp.sum(jnp.where(inside, ids, 0), axis=0, keepdims=True)
    sigma = 1.0 / (1.0 + jnp.exp(-logits_ref[...]))
    weight = (
        routed_scale
        * jnp.sum(jnp.where(inside, sigma, 0.0), axis=0, keepdims=True)
        / jnp.sum(sigma, axis=0, keepdims=True)
    )
    expert = lax.broadcasted_iota(jnp.int32, (window, rows), 0)
    onehot = jnp.where((expert == chosen) & (has > 0), 1.0, 0.0)
    earlier = lax.broadcasted_iota(jnp.int32, (rows, rows), 0) < lax.broadcasted_iota(
        jnp.int32, (rows, rows), 1
    )
    rank = jnp.dot(
        onehot.astype(jnp.bfloat16),
        jnp.where(earlier, 1.0, 0.0).astype(jnp.bfloat16),
        preferred_element_type=jnp.float32,
    )
    slot = jnp.sum(rank * onehot, axis=0, keepdims=True).astype(jnp.int32)
    place = chosen * CAP + slot
    pick = (lax.broadcasted_iota(jnp.int32, (window * CAP, rows), 0) == place) & (has > 0)
    place_ref[...] = jnp.where(pick, weight, 0.0).T
    pick = jnp.where(pick, 1.0, 0.0).astype(jnp.bfloat16)
    square = jnp.zeros((rows, 128), jnp.float32)
    for c in range(parts):
        load(c).wait()
        for i in range(c * piece, (c + 1) * piece, 128):
            value = x_buf[:, i : i + 128].astype(jnp.float32)
            square += value * value
    scale = lax.rsqrt(jnp.sum(square, axis=1, keepdims=True) / width + norm_eps)
    for c in range(parts):
        cut = slice(c * piece, (c + 1) * piece)
        normed = (x_buf[:, cut].astype(jnp.float32) * scale * gain_ref[:, cut]).astype(jnp.bfloat16)
        out_buf[:, cut] = jnp.dot(pick, normed, preferred_element_type=jnp.float32).astype(
            jnp.bfloat16
        )
        store(c).start()
    for c in range(parts):
        store(c).wait()


def dispatch(hidden_in, norm_gain, route_logits, expert_ids, window):
    rows, width = hidden_in.shape
    places, parts = window * CAP, 4
    vmem = pl.BlockSpec(memory_space=pltpu.VMEM)
    hbm = pl.BlockSpec(memory_space=pl.ANY)
    return pl.pallas_call(
        functools.partial(dispatch_kernel, window, parts),
        out_shape=[
            jax.ShapeDtypeStruct((places, width), jnp.bfloat16),
            jax.ShapeDtypeStruct((rows, places), jnp.float32),
        ],
        in_specs=[vmem] * 3 + [hbm],
        out_specs=[hbm, vmem],
        scratch_shapes=[
            pltpu.VMEM((rows, width), jnp.bfloat16),
            pltpu.VMEM((places, width), jnp.bfloat16),
            pltpu.SemaphoreType.DMA((parts,)),
            pltpu.SemaphoreType.DMA((parts,)),
        ],
        compiler_params=pltpu.CompilerParams(vmem_limit_bytes=58 * MIB),
        cost_estimate=pl.CostEstimate(
            flops=2 * rows * places * width,
            bytes_accessed=4 * rows * width,
            transcendentals=rows * 16,
        ),
        name="dispatch",
    )(expert_ids.T, route_logits.T, norm_gain.reshape(1, width), hidden_in)


def ffn_kernel(count, rows, parts, *refs):
    xs = refs[:count]
    gate_hbm, up_hbm, down_hbm = refs[count : count + 3]
    outs = refs[count + 3 : 2 * count + 3]
    x_buf, w_buf, d_buf, o_buf, acc, in_sem, w_sem, d_sem, out_sem = refs[2 * count + 3 :]
    depth = gate_hbm.shape[1]
    piece = depth // parts

    def loads(c):
        cut = pl.ds(pl.multiple_of(c * piece, piece), piece)
        for e in range(2):
            for j, source in enumerate((gate_hbm, up_hbm)):
                yield pltpu.make_async_copy(
                    source.at[e, cut],
                    w_buf.at[cut, pl.ds(256 * e + 128 * j, 128)],
                    w_sem.at[c, 2 * e + j],
                )
        for i in range(count):
            yield pltpu.make_async_copy(
                xs[i].at[:, cut], x_buf.at[pl.ds(i * rows, rows), cut], in_sem.at[c, i]
            )

    def stores(c):
        cut = pl.ds(pl.multiple_of(c * piece, piece), piece)
        for i in range(count):
            yield pltpu.make_async_copy(
                o_buf.at[pl.ds(i * rows, rows), cut], outs[i].at[:, cut], out_sem.at[c, i]
            )

    @pl.loop(0, parts)
    def _(c):
        for copy in loads(c):
            copy.start()

    down = [
        pltpu.make_async_copy(down_hbm.at[e], d_buf.at[pl.ds(128 * e, 128)], d_sem.at[e])
        for e in range(2)
    ]
    for copy in down:
        copy.start()
    acc[...] = jnp.zeros_like(acc)

    @pl.loop(0, parts)
    def _(c):
        for copy in loads(c):
            copy.wait()
        cut = pl.ds(pl.multiple_of(c * piece, piece), piece)
        acc[...] += jnp.dot(x_buf[:, cut], w_buf[cut, :], preferred_element_type=jnp.float32)

    first = lax.broadcasted_iota(jnp.int32, (rows * count, 128), 0) % (2 * CAP) < CAP
    gate = jnp.where(first, acc[:, :128], acc[:, 256:384])
    up = jnp.where(first, acc[:, 128:256], acc[:, 384:])
    active = gate / (1.0 + jnp.exp(-gate)) * up
    active = jnp.concatenate(
        [jnp.where(first, active, 0.0), jnp.where(first, 0.0, active)], axis=1
    ).astype(jnp.bfloat16)
    for copy in down:
        copy.wait()

    @pl.loop(0, parts)
    def _(c):
        cut = pl.ds(pl.multiple_of(c * piece, piece), piece)
        o_buf[:, cut] = jnp.dot(active, d_buf[:, cut], preferred_element_type=jnp.float32).astype(
            jnp.bfloat16
        )
        for copy in stores(c):
            copy.start()

    @pl.loop(0, parts)
    def _(c):
        for copy in stores(c):
            copy.wait()


def ffn(blocks, w_gate, w_up, w_down):
    chains, per_chain = len(blocks), len(blocks[0])
    flat = [block for part in blocks for block in part]
    count, rows, depth, parts = len(flat), flat[0].shape[0], w_gate.shape[1], 4
    total = rows * count
    done = pl.pallas_call(
        functools.partial(ffn_kernel, count, rows, parts),
        out_shape=[jax.ShapeDtypeStruct(block.shape, jnp.bfloat16) for block in flat],
        in_specs=[pl.BlockSpec(memory_space=pl.ANY)] * (count + 3),
        out_specs=[pl.BlockSpec(memory_space=pl.ANY)] * count,
        scratch_shapes=[
            pltpu.VMEM((total, depth), jnp.bfloat16),
            pltpu.VMEM((depth, 512), jnp.bfloat16),
            pltpu.VMEM((256, depth), jnp.bfloat16),
            pltpu.VMEM((total, depth), jnp.bfloat16),
            pltpu.VMEM((total, 512), jnp.float32),
            pltpu.SemaphoreType.DMA((parts, count)),
            pltpu.SemaphoreType.DMA((parts, 4)),
            pltpu.SemaphoreType.DMA((2,)),
            pltpu.SemaphoreType.DMA((parts, count)),
        ],
        compiler_params=pltpu.CompilerParams(vmem_limit_bytes=58 * MIB),
        cost_estimate=pl.CostEstimate(
            flops=2 * total * depth * 768,
            bytes_accessed=2 * depth * (768 + 2 * total),
            transcendentals=total * 128,
        ),
        name="ffn",
    )(*flat, w_gate, w_up, w_down)
    return [done[k * per_chain : (k + 1) * per_chain] for k in range(chains)]


def attend_kernel(
    step, table, lengths, q_ref, pool_hbm, more_hbm, out_ref, top_ref, total_ref, pages, sem
):
    own_pages = pool_hbm.shape[0]

    @pl.when(pl.program_id(0) == 0)
    def _():
        copies = [
            pltpu.make_async_copy(pool_hbm, pages.at[pl.ds(0, own_pages)], sem.at[0]),
            pltpu.make_async_copy(
                more_hbm, pages.at[pl.ds(own_pages, more_hbm.shape[0])], sem.at[1]
            ),
        ]
        for copy in copies:
            copy.start()
        for copy in copies:
            copy.wait()

    first = pl.program_id(0) * step
    keys = [
        jnp.concatenate([pages[table[(first + r) * MAXP + p]] for p in range(MAXP)], axis=0)
        for r in range(step)
    ]
    scores = jnp.concatenate(
        [
            lax.dot_general(
                keys[r], q_ref[r], (((1,), (1,)), ((), ())), preferred_element_type=jnp.float32
            )
            for r in range(step)
        ],
        axis=1,
    )
    scores = scores * softmax_scale
    column = lax.broadcasted_iota(jnp.int32, (1, step * HEADS), 1) // HEADS
    length = jnp.zeros_like(column)
    for r in range(step):
        length = jnp.where(column == r, lengths[first + r], length)
    valid = lax.broadcasted_iota(jnp.int32, scores.shape, 0) < length
    scores = jnp.where(valid, scores, -1e30)
    top = jnp.max(scores, axis=0, keepdims=True)
    expo = jnp.where(valid, jnp.exp(scores - top), 0.0)
    total = jnp.sum(expo, axis=0, keepdims=True)
    probs = (expo / total).astype(jnp.bfloat16)
    for r in range(step):
        cut = slice(r * HEADS, (r + 1) * HEADS)
        out_ref[r] = lax.dot_general(
            probs[:, cut],
            keys[r][:, :LATENT],
            (((0,), (0,)), ((), ())),
            preferred_element_type=jnp.float32,
        ).astype(jnp.bfloat16)
        top_ref[r : r + 1, :] = top[:, cut]
        total_ref[r : r + 1, :] = total[:, cut]


def attend_cached(query, pool, more, page_table, kv_lengths):
    rows, step = query.shape[0], 8
    entries = pool.shape[0] + more.shape[0]
    hbm = pl.BlockSpec(memory_space=pl.ANY)
    return pl.pallas_call(
        functools.partial(attend_kernel, step),
        out_shape=[
            jax.ShapeDtypeStruct((rows, HEADS, LATENT), jnp.bfloat16),
            jax.ShapeDtypeStruct((rows, HEADS), jnp.float32),
            jax.ShapeDtypeStruct((rows, HEADS), jnp.float32),
        ],
        grid_spec=pltpu.PrefetchScalarGridSpec(
            num_scalar_prefetch=2,
            grid=(rows // step,),
            in_specs=[pl.BlockSpec((step, HEADS, KVW), lambda i, t, n: (i, 0, 0)), hbm, hbm],
            out_specs=[
                pl.BlockSpec((step, HEADS, LATENT), lambda i, t, n: (i, 0, 0)),
                pl.BlockSpec((step, HEADS), lambda i, t, n: (i, 0)),
                pl.BlockSpec((step, HEADS), lambda i, t, n: (i, 0)),
            ],
            scratch_shapes=[
                pltpu.VMEM((entries, PAGE, KVW), jnp.bfloat16),
                pltpu.SemaphoreType.DMA((2,)),
            ],
        ),
        compiler_params=pltpu.CompilerParams(vmem_limit_bytes=58 * MIB),
        cost_estimate=pl.CostEstimate(
            flops=2 * rows * HEADS * MAXP * PAGE * (KVW + LATENT),
            bytes_accessed=2 * (query.size + entries * PAGE * KVW + rows * HEADS * LATENT),
            transcendentals=rows * HEADS * MAXP * PAGE,
        ),
        name="attend_cached",
    )(page_table.reshape(rows * MAXP), kv_lengths, query, pool, more)


def pack_kernel(count, *refs):
    blocks, joined = refs[: 2 * count], refs[2 * count : 3 * count]
    buf, in_sem, out_sem = refs[3 * count :]
    n = blocks[0].shape[0]
    loads = [
        pltpu.make_async_copy(blocks[i], buf.at[i // 2, pl.ds(i % 2 * n, n)], in_sem.at[i])
        for i in range(2 * count)
    ]
    stores = [pltpu.make_async_copy(buf.at[i], joined[i], out_sem.at[i]) for i in range(count)]
    for copy in loads:
        copy.start()
    for i in range(count):
        loads[2 * i].wait()
        loads[2 * i + 1].wait()
        stores[i].start()
    for copy in stores:
        copy.wait()


def pack(pairs):
    count, (n, width) = len(pairs), pairs[0][0].shape
    hbm = pl.BlockSpec(memory_space=pl.ANY)
    return pl.pallas_call(
        functools.partial(pack_kernel, count),
        out_shape=[jax.ShapeDtypeStruct((2 * n, width), jnp.bfloat16)] * count,
        in_specs=[hbm] * (2 * count),
        out_specs=[hbm] * count,
        scratch_shapes=[
            pltpu.VMEM((count, 2 * n, width), jnp.bfloat16),
            pltpu.SemaphoreType.DMA((2 * count,)),
            pltpu.SemaphoreType.DMA((count,)),
        ],
        compiler_params=pltpu.CompilerParams(vmem_limit_bytes=58 * MIB),
        cost_estimate=pl.CostEstimate(
            flops=0, bytes_accessed=8 * count * n * width, transcendentals=0
        ),
        name="pack",
    )(*(block for pair in pairs for block in pair))


def tail_kernel(
    parts,
    groups,
    hidden_hbm,
    back_hbm,
    gain_ref,
    cos_ref,
    sin_ref,
    top_ref,
    total_ref,
    place_ref,
    w_hbm,
    q_hbm,
    o_hbm,
    hidden_out_hbm,
    out_hbm,
    w_ref,
    q_ref,
    o_ref,
    hidden_ref,
    back_ref,
    hidden_buf,
    key_buf,
    own_buf,
    keep_buf,
    in_sem,
    w_sem,
    q_sem,
    o_sem,
    hidden_sem,
    out_sem,
):
    width = hidden_ref.shape[1]
    loads = [
        pltpu.make_async_copy(back_hbm, back_ref, in_sem.at[0]),
        pltpu.make_async_copy(hidden_hbm, hidden_ref, in_sem.at[1]),
    ]
    for copy in loads:
        copy.start()
    piece = width // parts
    per_group = HEADS // groups
    span, q_span = per_group * LATENT, per_group * KVW

    def w_load(c):
        cut = pl.ds(pl.multiple_of(c * piece, piece), piece)
        return pltpu.make_async_copy(w_hbm.at[cut], w_ref.at[cut], w_sem.at[c])

    def q_load(g):
        cut = pl.ds(pl.multiple_of(g * q_span, 128), q_span)
        return pltpu.make_async_copy(q_hbm.at[:, cut], q_ref.at[:, cut], q_sem.at[g])

    def o_load(g):
        cut = pl.ds(pl.multiple_of(g * span, span), span)
        return pltpu.make_async_copy(o_hbm.at[:, cut], o_ref.at[:, cut], o_sem.at[g])

    def store(g):
        cut = pl.ds(pl.multiple_of(g * span, span), span)
        return pltpu.make_async_copy(o_ref.at[:, cut], out_hbm.at[:, cut], out_sem.at[g])

    for c in range(parts):
        w_load(c).start()

    @pl.loop(0, groups)
    def _(g):
        q_load(g).start()

    @pl.loop(0, groups)
    def _(g):
        o_load(g).start()

    place = place_ref[...]
    pick = (place != 0.0).astype(jnp.bfloat16)
    weight = jnp.sum(place, axis=1, keepdims=True)
    projected = jnp.zeros((hidden_ref.shape[0], KVW), jnp.float32)
    for copy in loads:
        copy.wait()
    for c in range(parts):
        cut = slice(c * piece, (c + 1) * piece)
        picked = jnp.dot(pick, back_ref[:, cut], preferred_element_type=jnp.float32)
        hidden = (hidden_ref[:, cut].astype(jnp.float32) + weight * picked).astype(jnp.bfloat16)
        hidden_buf[:, cut] = hidden
        w_load(c).wait()
        projected += jnp.dot(hidden, w_ref[cut, :], preferred_element_type=jnp.float32)
    hidden_copy = pltpu.make_async_copy(hidden_buf, hidden_out_hbm, hidden_sem)
    hidden_copy.start()
    latent = rms_rows(projected[:, :LATENT], gain_ref[...])
    first = projected[:, LATENT : LATENT + 32]
    second = projected[:, LATENT + 32 :]
    cosine, sine = cos_ref[...], sin_ref[...]
    new_key = jnp.concatenate(
        [latent, first * cosine - second * sine, second * cosine + first * sine], axis=1
    )
    new_key = new_key.astype(jnp.bfloat16).astype(jnp.float32)
    key_buf[...] = jnp.concatenate([new_key, new_key], axis=1)
    lane = lax.broadcasted_iota(jnp.int32, (8, 128), 1)
    head = lax.broadcasted_iota(jnp.int32, (8, HEADS), 1)
    blocks = hidden_ref.shape[0] // 8
    own_buf[...] = jnp.zeros_like(own_buf)

    @pl.loop(0, HEADS // 2)
    def _(j):
        @pl.when(j % (per_group // 2) == 0)
        def _():
            q_load(j // (per_group // 2)).wait()

        cut = pl.ds(pl.multiple_of(j * 2 * KVW, 128), 2 * KVW)
        for b in range(blocks):
            rows = slice(8 * b, 8 * b + 8)
            product = q_ref[rows, cut].astype(jnp.float32) * key_buf[rows, :]
            tiles = [product[:, 128 * i : 128 * (i + 1)] for i in range(9)]
            low = (tiles[0] + tiles[1]) + (tiles[2] + tiles[3]) + jnp.where(lane < 64, tiles[4], 0.0)
            high = (tiles[5] + tiles[6]) + (tiles[7] + tiles[8])
            high = high + jnp.where(lane < 64, 0.0, tiles[4])
            low = jnp.sum(low, axis=1, keepdims=True)
            high = jnp.sum(high, axis=1, keepdims=True)
            own_buf[rows, :] = jnp.where(
                head == 2 * j, low, jnp.where(head == 2 * j + 1, high, own_buf[rows, :])
            )

    own = own_buf[...] * softmax_scale
    top_old = top_ref[...]
    top = jnp.maximum(top_old, own)
    part = total_ref[...] * jnp.exp(top_old - top)
    part_own = jnp.exp(own - top)
    inverse = 1.0 / (part + part_own)
    keep_buf[...] = part * inverse
    own_buf[...] = (part_own * inverse).astype(jnp.bfloat16).astype(jnp.float32)

    @pl.loop(0, groups)
    def _(g):
        o_load(g).wait()
        for b in range(blocks):
            rows = slice(8 * b, 8 * b + 8)
            key_low = key_buf[rows, :LATENT]
            keeps, adds = keep_buf[rows, :], own_buf[rows, :]
            for i in range(per_group):
                h = g * per_group + i
                keep = jnp.sum(jnp.where(head == h, keeps, 0.0), axis=1, keepdims=True)
                add = jnp.sum(jnp.where(head == h, adds, 0.0), axis=1, keepdims=True)
                cut = pl.ds(pl.multiple_of(h * LATENT, LATENT), LATENT)
                o_ref[rows, cut] = (
                    o_ref[rows, cut].astype(jnp.float32) * keep + add * key_low
                ).astype(jnp.bfloat16)
        store(g).start()

    @pl.loop(0, groups)
    def _(g):
        store(g).wait()

    hidden_copy.wait()


def tail(hidden_in, back, kv_gain, cosine, sine, top, total, place_weight, w_all, queries, o):
    rows, width = hidden_in.shape
    parts, groups = 7, 8
    vmem = pl.BlockSpec(memory_space=pltpu.VMEM)
    hbm = pl.BlockSpec(memory_space=pl.ANY)
    return pl.pallas_call(
        functools.partial(tail_kernel, parts, groups),
        out_shape=[
            jax.ShapeDtypeStruct((rows, width), jnp.bfloat16),
            jax.ShapeDtypeStruct((rows, HEADS * LATENT), jnp.bfloat16),
        ],
        in_specs=[hbm] * 2 + [vmem] * 6 + [hbm] * 3,
        out_specs=[hbm] * 2,
        scratch_shapes=[
            pltpu.VMEM(w_all.shape, jnp.bfloat16),
            pltpu.VMEM(queries.shape, jnp.bfloat16),
            pltpu.VMEM(o.shape, jnp.bfloat16),
            pltpu.VMEM((rows, width), jnp.bfloat16),
            pltpu.VMEM(back.shape, jnp.bfloat16),
            pltpu.VMEM((rows, width), jnp.bfloat16),
            pltpu.VMEM((rows, 2 * KVW), jnp.float32),
            pltpu.VMEM((rows, HEADS), jnp.float32),
            pltpu.VMEM((rows, HEADS), jnp.float32),
            pltpu.SemaphoreType.DMA((2,)),
            pltpu.SemaphoreType.DMA((parts,)),
            pltpu.SemaphoreType.DMA((groups,)),
            pltpu.SemaphoreType.DMA((groups,)),
            pltpu.SemaphoreType.DMA,
            pltpu.SemaphoreType.DMA((groups,)),
        ],
        compiler_params=pltpu.CompilerParams(vmem_limit_bytes=58 * MIB),
        cost_estimate=pl.CostEstimate(
            flops=2 * rows * width * KVW,
            bytes_accessed=2 * (w_all.size + queries.size + 2 * o.size),
            transcendentals=rows * HEADS * 2,
        ),
        name="tail",
    )(
        hidden_in,
        back,
        kv_gain.reshape(1, LATENT),
        cosine,
        sine,
        top,
        total,
        place_weight,
        w_all,
        queries,
        o,
    )


def plus(*terms):
    total = terms[0].astype(jnp.float32)
    for term in terms[1:]:
        total = total + term.astype(jnp.float32)
    return total.astype(jnp.bfloat16)


def after(values, *others):
    return lax.optimization_barrier((values, others))[0]


def body(
    hidden_in,
    norm_gain,
    route_logits,
    expert_ids,
    w_gate,
    w_up,
    w_down,
    w_latent,
    kv_gain,
    queries,
    page_pool,
    page_table,
    kv_lengths,
    migration,
):
    dp_count = lax.axis_size("dp")
    ex_count = lax.axis_size("expert")
    row_count = hidden_in.shape[0]
    local_experts = w_gate.shape[0]
    window = local_experts * dp_count
    width = hidden_in.shape[1]
    padded = w_latent.shape[0] + 8
    w_padded = jnp.concatenate([w_latent, w_latent[:8]], axis=0)
    w_plane = lax.all_gather(w_padded, "expert", axis=0, tiled=True)
    slots = local_experts * CAP
    packed, place_weight = dispatch(
        hidden_in, after(norm_gain, w_padded), route_logits, expert_ids, window
    )
    arrived = lax.all_to_all(
        packed.reshape(dp_count, slots, width), "dp", split_axis=0, concat_axis=0, tiled=True
    )
    outgoing = jnp.take(page_pool, migration.reshape(dp_count * MCAP), axis=0, mode="clip")
    query = queries.reshape(row_count, HEADS, KVW)
    arrived = after(arrived, outgoing, query)
    arrived = arrived.reshape(window * CAP, width)
    axes = (("z", "x"), ("x", "z"))
    both = range(2)
    n = arrived.shape[0] // 2
    rows = [arrived[k * n : (k + 1) * n] for k in both]
    weights = (w_gate, w_up, w_down)

    below = [shift(rows[k], axes[k][0], 1) for k in both]
    above = [shift(rows[k], axes[k][0], -1) for k in both]
    below, above = after((below, above))
    beyond = [shift(above[k], axes[k][0], -1) for k in both]
    low = pack([(rows[k], below[k]) for k in both])
    below_low = [shift(low[k], axes[k][1], 1) for k in both]
    low_too, beyond = after((low, beyond))
    above_low = [shift(low_too[k], axes[k][1], -1) for k in both]
    high = pack([(above[k], beyond[k]) for k in both])
    more = lax.all_to_all(
        after(outgoing, high).reshape(dp_count, MCAP, page_pool.shape[1]),
        "dp",
        split_axis=0,
        concat_axis=0,
        tiled=True,
    ).reshape(dp_count * MCAP, PAGE, KVW)
    high, w_plane = after((high, w_plane))
    w_plane = w_plane.reshape(ex_count, padded, KVW)[:, : w_latent.shape[0]]
    w_all = lax.all_gather(
        w_plane.reshape(ex_count * w_latent.shape[0], KVW), "dp", axis=0, tiled=True
    )
    pool = after(page_pool, high).reshape(page_pool.shape[0], PAGE, KVW)
    below_high = [shift(high[k], axes[k][1], 1) for k in both]
    above_high = [shift(high[k], axes[k][1], -1) for k in both]
    y_first = ffn([[low[k], high[k], below_low[k], above_low[k]] for k in both], *weights)
    below_low, above_high, below_high, above_low = after(
        (below_low, above_high, below_high, above_low), y_first, pool, more
    )
    far_low = [shift(below_low[k], axes[k][1], 1) for k in both]
    far_high = [shift(above_high[k], axes[k][1], -1) for k in both]
    y_second = ffn([[below_high[k], above_high[k]] for k in both], *weights)
    y_first = after(y_first, y_second)
    early_down = [shift(y_first[k][2], axes[k][1], -1) for k in both]
    early_up = [shift(y_second[k][1], axes[k][1], 1) for k in both]
    far_low, far_high = after((far_low, far_high), y_second)
    y_far = ffn([[far_low[k], far_high[k]] for k in both], *weights)
    y_far, early_down, early_up = after((y_far, early_down, early_up))
    relay_up = [shift(y_far[k][0], axes[k][1], 1) for k in both]
    relay_down = [shift(y_far[k][1], axes[k][1], -1) for k in both]
    query = after(query, y_far)
    cached, top, total = attend_cached(query, pool, more, page_table, kv_lengths)
    relay_up, relay_down = after((relay_up, relay_down), cached)
    late_up = [shift(plus(y_first[k][3], relay_up[k]), axes[k][1], 1) for k in both]
    late_down = [shift(plus(y_second[k][0], relay_down[k]), axes[k][1], -1) for k in both]
    cached = cached.reshape(row_count, HEADS * LATENT)
    late_up, late_down = after((late_up, late_down), cached)
    terms_low = [(y_first[k][0], late_up[k], early_down[k]) for k in both]
    terms_high = [(y_first[k][1], early_up[k], late_down[k]) for k in both]
    for_far = [plus(*(term[n:] for term in terms_high[k])) for k in both]
    for_below = [plus(*(term[n:] for term in terms_low[k])) for k in both]
    relayed = [shift(for_far[k], axes[k][0], 1) for k in both]
    from_above = [shift(for_below[k], axes[k][0], -1) for k in both]
    relayed, from_above = after((relayed, from_above))
    from_below = [
        shift(plus(*(term[:n] for term in terms_high[k]), relayed[k]), axes[k][0], 1) for k in both
    ]
    from_below = after(from_below)
    finished = [
        plus(*(term[:n] for term in terms_low[k]), from_below[k], from_above[k]) for k in both
    ]
    back = lax.all_to_all(
        jnp.concatenate(finished, axis=0).reshape(dp_count, slots, width),
        "dp",
        split_axis=0,
        concat_axis=0,
        tiled=True,
    ).reshape(window * CAP, width)

    half = (KVW - LATENT) // 2
    freq = 10000.0 ** (-jnp.arange(half, dtype=jnp.float32) / half)
    angle = kv_lengths.astype(jnp.float32)[:, None] * freq[None, :]
    return tuple(
        tail(
            hidden_in,
            back,
            kv_gain,
            jnp.cos(angle),
            jnp.sin(angle),
            top,
            total,
            place_weight,
            w_all,
            queries,
            cached,
        )
    )


def solution(mesh):
    return jax.shard_map(
        body,
        mesh=mesh,
        in_specs=(
            P(("dp", "expert"), None),
            P(),
            P(("dp", "expert"), None),
            P(("dp", "expert"), None),
            P("dp", None, "expert"),
            P("dp", None, "expert"),
            P("dp", "expert", None),
            P(("dp", "expert"), None),
            P(),
            P(("dp", "expert"), None),
            P(("dp", "expert"), None),
            P(("dp", "expert"), None),
            P(("dp", "expert")),
            P("dp", "expert", None, None),
        ),
        out_specs=(P(("dp", "expert"), None), P(("dp", "expert"), None)),
        check_vma=False,
    )
```

```python
import functools

import jax
import jax.numpy as jnp
from jax import lax
from jax.experimental import pallas as pl
from jax.experimental.pallas import tpu as pltpu
from jax.sharding import PartitionSpec as P

HEADS = 64
LATENT = 512
PAGE = 16
MAXP = 6
CAP = 4
MCAP = 4
KVW = 576
SIDE = 4

softmax_scale = 192.0 ** (-0.5)
routed_scale = 2.5
norm_eps = 1e-06
MIB = 1 << 20


def rms_rows(values, gain):
    stat = jnp.mean(values * values, axis=-1, keepdims=True)
    return values * lax.rsqrt(stat + norm_eps) * gain


def shift(value, axis, step):
    pairs = []
    for x in range(SIDE):
        for z in range(SIDE):
            to_x = (x + step) % SIDE if axis == "x" else x
            to_z = (z + step) % SIDE if axis == "z" else z
            pairs.append((x * SIDE + z, to_x * SIDE + to_z))
    return lax.ppermute(value, "expert", pairs)


def dispatch_kernel(
    window, parts, ids_ref, logits_ref, gain_ref, hidden_hbm, packed_hbm, place_ref, x_buf, out_buf, in_sem, out_sem
):
    rows, width = hidden_hbm.shape
    piece = width // parts

    def load(c):
        cut = pl.ds(c * piece, piece)
        return pltpu.make_async_copy(hidden_hbm.at[:, cut], x_buf.at[:, cut], in_sem.at[c])

    def store(c):
        cut = pl.ds(c * piece, piece)
        return pltpu.make_async_copy(out_buf.at[:, cut], packed_hbm.at[:, cut], out_sem.at[c])

    for c in range(parts):
        load(c).start()
    ids = ids_ref[...]
    inside = ids < window
    has = jnp.max(inside.astype(jnp.int32), axis=0, keepdims=True)
    chosen = jnp.sum(jnp.where(inside, ids, 0), axis=0, keepdims=True)
    sigma = 1.0 / (1.0 + jnp.exp(-logits_ref[...]))
    weight = (
        routed_scale
        * jnp.sum(jnp.where(inside, sigma, 0.0), axis=0, keepdims=True)
        / jnp.sum(sigma, axis=0, keepdims=True)
    )
    expert = lax.broadcasted_iota(jnp.int32, (window, rows), 0)
    onehot = jnp.where((expert == chosen) & (has > 0), 1.0, 0.0)
    earlier = lax.broadcasted_iota(jnp.int32, (rows, rows), 0) < lax.broadcasted_iota(
        jnp.int32, (rows, rows), 1
    )
    rank = jnp.dot(
        onehot.astype(jnp.bfloat16),
        jnp.where(earlier, 1.0, 0.0).astype(jnp.bfloat16),
        preferred_element_type=jnp.float32,
    )
    slot = jnp.sum(rank * onehot, axis=0, keepdims=True).astype(jnp.int32)
    place = chosen * CAP + slot
    pick = (lax.broadcasted_iota(jnp.int32, (window * CAP, rows), 0) == place) & (has > 0)
    place_ref[...] = jnp.where(pick, weight, 0.0).T
    pick = jnp.where(pick, 1.0, 0.0).astype(jnp.bfloat16)
    square = jnp.zeros((rows, 128), jnp.float32)
    for c in range(parts):
        load(c).wait()
        for i in range(c * piece, (c + 1) * piece, 128):
            value = x_buf[:, i : i + 128].astype(jnp.float32)
            square += value * value
    scale = lax.rsqrt(jnp.sum(square, axis=1, keepdims=True) / width + norm_eps)
    for c in range(parts):
        cut = slice(c * piece, (c + 1) * piece)
        normed = (x_buf[:, cut].astype(jnp.float32) * scale * gain_ref[:, cut]).astype(jnp.bfloat16)
        out_buf[:, cut] = jnp.dot(pick, normed, preferred_element_type=jnp.float32).astype(
            jnp.bfloat16
        )
        store(c).start()
    for c in range(parts):
        store(c).wait()


def dispatch(hidden_in, norm_gain, route_logits, expert_ids, window):
    rows, width = hidden_in.shape
    places, parts = window * CAP, 4
    vmem = pl.BlockSpec(memory_space=pltpu.VMEM)
    hbm = pl.BlockSpec(memory_space=pl.ANY)
    return pl.pallas_call(
        functools.partial(dispatch_kernel, window, parts),
        out_shape=[
            jax.ShapeDtypeStruct((places, width), jnp.bfloat16),
            jax.ShapeDtypeStruct((rows, places), jnp.float32),
        ],
        in_specs=[vmem] * 3 + [hbm],
        out_specs=[hbm, vmem],
        scratch_shapes=[
            pltpu.VMEM((rows, width), jnp.bfloat16),
            pltpu.VMEM((places, width), jnp.bfloat16),
            pltpu.SemaphoreType.DMA((parts,)),
            pltpu.SemaphoreType.DMA((parts,)),
        ],
        compiler_params=pltpu.CompilerParams(vmem_limit_bytes=58 * MIB),
        cost_estimate=pl.CostEstimate(
            flops=2 * rows * places * width,
            bytes_accessed=4 * rows * width,
            transcendentals=rows * 16,
        ),
        name="dispatch",
    )(expert_ids.T, route_logits.T, norm_gain.reshape(1, width), hidden_in)


def ffn_kernel(count, rows, parts, *refs):
    xs = refs[:count]
    gate_hbm, up_hbm, down_hbm = refs[count : count + 3]
    outs = refs[count + 3 : 2 * count + 3]
    x_buf, w_buf, d_buf, o_buf, acc, in_sem, w_sem, d_sem, out_sem = refs[2 * count + 3 :]
    depth = gate_hbm.shape[1]
    piece = depth // parts

    def loads(c):
        cut = pl.ds(pl.multiple_of(c * piece, piece), piece)
        for e in range(2):
            for j, source in enumerate((gate_hbm, up_hbm)):
                yield pltpu.make_async_copy(
                    source.at[e, cut],
                    w_buf.at[cut, pl.ds(256 * e + 128 * j, 128)],
                    w_sem.at[c, 2 * e + j],
                )
        for i in range(count):
            yield pltpu.make_async_copy(
                xs[i].at[:, cut], x_buf.at[pl.ds(i * rows, rows), cut], in_sem.at[c, i]
            )

    def stores(c):
        cut = pl.ds(pl.multiple_of(c * piece, piece), piece)
        for i in range(count):
            yield pltpu.make_async_copy(
                o_buf.at[pl.ds(i * rows, rows), cut], outs[i].at[:, cut], out_sem.at[c, i]
            )

    @pl.loop(0, parts)
    def _(c):
        for copy in loads(c):
            copy.start()

    down = [
        pltpu.make_async_copy(down_hbm.at[e], d_buf.at[pl.ds(128 * e, 128)], d_sem.at[e])
        for e in range(2)
    ]
    for copy in down:
        copy.start()
    acc[...] = jnp.zeros_like(acc)

    @pl.loop(0, parts)
    def _(c):
        for copy in loads(c):
            copy.wait()
        cut = pl.ds(pl.multiple_of(c * piece, piece), piece)
        acc[...] += jnp.dot(x_buf[:, cut], w_buf[cut, :], preferred_element_type=jnp.float32)

    first = lax.broadcasted_iota(jnp.int32, (rows * count, 128), 0) % (2 * CAP) < CAP
    gate = jnp.where(first, acc[:, :128], acc[:, 256:384])
    up = jnp.where(first, acc[:, 128:256], acc[:, 384:])
    active = gate / (1.0 + jnp.exp(-gate)) * up
    active = jnp.concatenate(
        [jnp.where(first, active, 0.0), jnp.where(first, 0.0, active)], axis=1
    ).astype(jnp.bfloat16)
    for copy in down:
        copy.wait()

    @pl.loop(0, parts)
    def _(c):
        cut = pl.ds(pl.multiple_of(c * piece, piece), piece)
        o_buf[:, cut] = jnp.dot(active, d_buf[:, cut], preferred_element_type=jnp.float32).astype(
            jnp.bfloat16
        )
        for copy in stores(c):
            copy.start()

    @pl.loop(0, parts)
    def _(c):
        for copy in stores(c):
            copy.wait()


def ffn(blocks, w_gate, w_up, w_down):
    chains, per_chain = len(blocks), len(blocks[0])
    flat = [block for part in blocks for block in part]
    count, rows, depth, parts = len(flat), flat[0].shape[0], w_gate.shape[1], 4
    total = rows * count
    done = pl.pallas_call(
        functools.partial(ffn_kernel, count, rows, parts),
        out_shape=[jax.ShapeDtypeStruct(block.shape, jnp.bfloat16) for block in flat],
        in_specs=[pl.BlockSpec(memory_space=pl.ANY)] * (count + 3),
        out_specs=[pl.BlockSpec(memory_space=pl.ANY)] * count,
        scratch_shapes=[
            pltpu.VMEM((total, depth), jnp.bfloat16),
            pltpu.VMEM((depth, 512), jnp.bfloat16),
            pltpu.VMEM((256, depth), jnp.bfloat16),
            pltpu.VMEM((total, depth), jnp.bfloat16),
            pltpu.VMEM((total, 512), jnp.float32),
            pltpu.SemaphoreType.DMA((parts, count)),
            pltpu.SemaphoreType.DMA((parts, 4)),
            pltpu.SemaphoreType.DMA((2,)),
            pltpu.SemaphoreType.DMA((parts, count)),
        ],
        compiler_params=pltpu.CompilerParams(vmem_limit_bytes=58 * MIB),
        cost_estimate=pl.CostEstimate(
            flops=2 * total * depth * 768,
            bytes_accessed=2 * depth * (768 + 2 * total),
            transcendentals=total * 128,
        ),
        name="ffn",
    )(*flat, w_gate, w_up, w_down)
    return [done[k * per_chain : (k + 1) * per_chain] for k in range(chains)]


def attend_kernel(
    step, table, lengths, q_ref, pool_hbm, more_hbm, out_ref, top_ref, total_ref, pages, sem
):
    own_pages = pool_hbm.shape[0]

    @pl.when(pl.program_id(0) == 0)
    def _():
        copies = [
            pltpu.make_async_copy(pool_hbm, pages.at[pl.ds(0, own_pages)], sem.at[0]),
            pltpu.make_async_copy(
                more_hbm, pages.at[pl.ds(own_pages, more_hbm.shape[0])], sem.at[1]
            ),
        ]
        for copy in copies:
            copy.start()
        for copy in copies:
            copy.wait()

    first = pl.program_id(0) * step
    keys = [
        jnp.concatenate([pages[table[(first + r) * MAXP + p]] for p in range(MAXP)], axis=0)
        for r in range(step)
    ]
    scores = jnp.concatenate(
        [
            lax.dot_general(
                keys[r], q_ref[r], (((1,), (1,)), ((), ())), preferred_element_type=jnp.float32
            )
            for r in range(step)
        ],
        axis=1,
    )
    scores = scores * softmax_scale
    column = lax.broadcasted_iota(jnp.int32, (1, step * HEADS), 1) // HEADS
    length = jnp.zeros_like(column)
    for r in range(step):
        length = jnp.where(column == r, lengths[first + r], length)
    valid = lax.broadcasted_iota(jnp.int32, scores.shape, 0) < length
    scores = jnp.where(valid, scores, -1e30)
    top = jnp.max(scores, axis=0, keepdims=True)
    expo = jnp.where(valid, jnp.exp(scores - top), 0.0)
    total = jnp.sum(expo, axis=0, keepdims=True)
    probs = (expo / total).astype(jnp.bfloat16)
    for r in range(step):
        cut = slice(r * HEADS, (r + 1) * HEADS)
        out_ref[r] = lax.dot_general(
            probs[:, cut],
            keys[r][:, :LATENT],
            (((0,), (0,)), ((), ())),
            preferred_element_type=jnp.float32,
        ).astype(jnp.bfloat16)
        top_ref[r : r + 1, :] = top[:, cut]
        total_ref[r : r + 1, :] = total[:, cut]


def attend_cached(query, pool, more, page_table, kv_lengths):
    rows, step = query.shape[0], 8
    entries = pool.shape[0] + more.shape[0]
    hbm = pl.BlockSpec(memory_space=pl.ANY)
    return pl.pallas_call(
        functools.partial(attend_kernel, step),
        out_shape=[
            jax.ShapeDtypeStruct((rows, HEADS, LATENT), jnp.bfloat16),
            jax.ShapeDtypeStruct((rows, HEADS), jnp.float32),
            jax.ShapeDtypeStruct((rows, HEADS), jnp.float32),
        ],
        grid_spec=pltpu.PrefetchScalarGridSpec(
            num_scalar_prefetch=2,
            grid=(rows // step,),
            in_specs=[pl.BlockSpec((step, HEADS, KVW), lambda i, t, n: (i, 0, 0)), hbm, hbm],
            out_specs=[
                pl.BlockSpec((step, HEADS, LATENT), lambda i, t, n: (i, 0, 0)),
                pl.BlockSpec((step, HEADS), lambda i, t, n: (i, 0)),
                pl.BlockSpec((step, HEADS), lambda i, t, n: (i, 0)),
            ],
            scratch_shapes=[
                pltpu.VMEM((entries, PAGE, KVW), jnp.bfloat16),
                pltpu.SemaphoreType.DMA((2,)),
            ],
        ),
        compiler_params=pltpu.CompilerParams(vmem_limit_bytes=58 * MIB),
        cost_estimate=pl.CostEstimate(
            flops=2 * rows * HEADS * MAXP * PAGE * (KVW + LATENT),
            bytes_accessed=2 * (query.size + entries * PAGE * KVW + rows * HEADS * LATENT),
            transcendentals=rows * HEADS * MAXP * PAGE,
        ),
        name="attend_cached",
    )(page_table.reshape(rows * MAXP), kv_lengths, query, pool, more)


def pack_kernel(count, *refs):
    blocks, joined = refs[: 2 * count], refs[2 * count : 3 * count]
    buf, in_sem, out_sem = refs[3 * count :]
    n = blocks[0].shape[0]
    loads = [
        pltpu.make_async_copy(blocks[i], buf.at[i // 2, pl.ds(i % 2 * n, n)], in_sem.at[i])
        for i in range(2 * count)
    ]
    stores = [pltpu.make_async_copy(buf.at[i], joined[i], out_sem.at[i]) for i in range(count)]
    for copy in loads:
        copy.start()
    for i in range(count):
        loads[2 * i].wait()
        loads[2 * i + 1].wait()
        stores[i].start()
    for copy in stores:
        copy.wait()


def pack(pairs):
    count, (n, width) = len(pairs), pairs[0][0].shape
    hbm = pl.BlockSpec(memory_space=pl.ANY)
    return pl.pallas_call(
        functools.partial(pack_kernel, count),
        out_shape=[jax.ShapeDtypeStruct((2 * n, width), jnp.bfloat16)] * count,
        in_specs=[hbm] * (2 * count),
        out_specs=[hbm] * count,
        scratch_shapes=[
            pltpu.VMEM((count, 2 * n, width), jnp.bfloat16),
            pltpu.SemaphoreType.DMA((2 * count,)),
            pltpu.SemaphoreType.DMA((count,)),
        ],
        compiler_params=pltpu.CompilerParams(vmem_limit_bytes=58 * MIB),
        cost_estimate=pl.CostEstimate(
            flops=0, bytes_accessed=8 * count * n * width, transcendentals=0
        ),
        name="pack",
    )(*(block for pair in pairs for block in pair))


def tail_kernel(
    parts,
    groups,
    hidden_hbm,
    back_hbm,
    gain_ref,
    cos_ref,
    sin_ref,
    top_ref,
    total_ref,
    place_ref,
    w_hbm,
    q_hbm,
    o_hbm,
    hidden_out_hbm,
    out_hbm,
    w_ref,
    q_ref,
    o_ref,
    hidden_ref,
    back_ref,
    hidden_buf,
    key_buf,
    own_buf,
    keep_buf,
    in_sem,
    w_sem,
    q_sem,
    o_sem,
    hidden_sem,
    out_sem,
):
    width = hidden_ref.shape[1]
    loads = [
        pltpu.make_async_copy(back_hbm, back_ref, in_sem.at[0]),
        pltpu.make_async_copy(hidden_hbm, hidden_ref, in_sem.at[1]),
    ]
    for copy in loads:
        copy.start()
    piece = width // parts
    per_group = HEADS // groups
    span, q_span = per_group * LATENT, per_group * KVW

    def w_load(c):
        cut = pl.ds(pl.multiple_of(c * piece, piece), piece)
        return pltpu.make_async_copy(w_hbm.at[cut], w_ref.at[cut], w_sem.at[c])

    def q_load(g):
        cut = pl.ds(pl.multiple_of(g * q_span, 128), q_span)
        return pltpu.make_async_copy(q_hbm.at[:, cut], q_ref.at[:, cut], q_sem.at[g])

    def o_load(g):
        cut = pl.ds(pl.multiple_of(g * span, span), span)
        return pltpu.make_async_copy(o_hbm.at[:, cut], o_ref.at[:, cut], o_sem.at[g])

    def store(g):
        cut = pl.ds(pl.multiple_of(g * span, span), span)
        return pltpu.make_async_copy(o_ref.at[:, cut], out_hbm.at[:, cut], out_sem.at[g])

    for c in range(parts):
        w_load(c).start()

    @pl.loop(0, groups)
    def _(g):
        q_load(g).start()

    @pl.loop(0, groups)
    def _(g):
        o_load(g).start()

    place = place_ref[...]
    pick = (place != 0.0).astype(jnp.bfloat16)
    weight = jnp.sum(place, axis=1, keepdims=True)
    projected = jnp.zeros((hidden_ref.shape[0], KVW), jnp.float32)
    for copy in loads:
        copy.wait()
    for c in range(parts):
        cut = slice(c * piece, (c + 1) * piece)
        picked = jnp.dot(pick, back_ref[:, cut], preferred_element_type=jnp.float32)
        hidden = (hidden_ref[:, cut].astype(jnp.float32) + weight * picked).astype(jnp.bfloat16)
        hidden_buf[:, cut] = hidden
        w_load(c).wait()
        projected += jnp.dot(hidden, w_ref[cut, :], preferred_element_type=jnp.float32)
    hidden_copy = pltpu.make_async_copy(hidden_buf, hidden_out_hbm, hidden_sem)
    hidden_copy.start()
    latent = rms_rows(projected[:, :LATENT], gain_ref[...])
    first = projected[:, LATENT : LATENT + 32]
    second = projected[:, LATENT + 32 :]
    cosine, sine = cos_ref[...], sin_ref[...]
    new_key = jnp.concatenate(
        [latent, first * cosine - second * sine, second * cosine + first * sine], axis=1
    )
    new_key = new_key.astype(jnp.bfloat16).astype(jnp.float32)
    key_buf[...] = jnp.concatenate([new_key, new_key], axis=1)
    lane = lax.broadcasted_iota(jnp.int32, (8, 128), 1)
    head = lax.broadcasted_iota(jnp.int32, (8, HEADS), 1)
    blocks = hidden_ref.shape[0] // 8
    own_buf[...] = jnp.zeros_like(own_buf)

    @pl.loop(0, HEADS // 2)
    def _(j):
        @pl.when(j % (per_group // 2) == 0)
        def _():
            q_load(j // (per_group // 2)).wait()

        cut = pl.ds(pl.multiple_of(j * 2 * KVW, 128), 2 * KVW)
        for b in range(blocks):
            rows = slice(8 * b, 8 * b + 8)
            product = q_ref[rows, cut].astype(jnp.float32) * key_buf[rows, :]
            tiles = [product[:, 128 * i : 128 * (i + 1)] for i in range(9)]
            low = (tiles[0] + tiles[1]) + (tiles[2] + tiles[3]) + jnp.where(lane < 64, tiles[4], 0.0)
            high = (tiles[5] + tiles[6]) + (tiles[7] + tiles[8])
            high = high + jnp.where(lane < 64, 0.0, tiles[4])
            low = jnp.sum(low, axis=1, keepdims=True)
            high = jnp.sum(high, axis=1, keepdims=True)
            own_buf[rows, :] = jnp.where(
                head == 2 * j, low, jnp.where(head == 2 * j + 1, high, own_buf[rows, :])
            )

    own = own_buf[...] * softmax_scale
    top_old = top_ref[...]
    top = jnp.maximum(top_old, own)
    part = total_ref[...] * jnp.exp(top_old - top)
    part_own = jnp.exp(own - top)
    inverse = 1.0 / (part + part_own)
    keep_buf[...] = part * inverse
    own_buf[...] = (part_own * inverse).astype(jnp.bfloat16).astype(jnp.float32)

    @pl.loop(0, groups)
    def _(g):
        o_load(g).wait()
        for b in range(blocks):
            rows = slice(8 * b, 8 * b + 8)
            key_low = key_buf[rows, :LATENT]
            keeps, adds = keep_buf[rows, :], own_buf[rows, :]
            for i in range(per_group):
                h = g * per_group + i
                keep = jnp.sum(jnp.where(head == h, keeps, 0.0), axis=1, keepdims=True)
                add = jnp.sum(jnp.where(head == h, adds, 0.0), axis=1, keepdims=True)
                cut = pl.ds(pl.multiple_of(h * LATENT, LATENT), LATENT)
                o_ref[rows, cut] = (
                    o_ref[rows, cut].astype(jnp.float32) * keep + add * key_low
                ).astype(jnp.bfloat16)
        store(g).start()

    @pl.loop(0, groups)
    def _(g):
        store(g).wait()

    hidden_copy.wait()


def tail(hidden_in, back, kv_gain, cosine, sine, top, total, place_weight, w_all, queries, o):
    rows, width = hidden_in.shape
    parts, groups = 7, 8
    vmem = pl.BlockSpec(memory_space=pltpu.VMEM)
    hbm = pl.BlockSpec(memory_space=pl.ANY)
    return pl.pallas_call(
        functools.partial(tail_kernel, parts, groups),
        out_shape=[
            jax.ShapeDtypeStruct((rows, width), jnp.bfloat16),
            jax.ShapeDtypeStruct((rows, HEADS * LATENT), jnp.bfloat16),
        ],
        in_specs=[hbm] * 2 + [vmem] * 6 + [hbm] * 3,
        out_specs=[hbm] * 2,
        scratch_shapes=[
            pltpu.VMEM(w_all.shape, jnp.bfloat16),
            pltpu.VMEM(queries.shape, jnp.bfloat16),
            pltpu.VMEM(o.shape, jnp.bfloat16),
            pltpu.VMEM((rows, width), jnp.bfloat16),
            pltpu.VMEM(back.shape, jnp.bfloat16),
            pltpu.VMEM((rows, width), jnp.bfloat16),
            pltpu.VMEM((rows, 2 * KVW), jnp.float32),
            pltpu.VMEM((rows, HEADS), jnp.float32),
            pltpu.VMEM((rows, HEADS), jnp.float32),
            pltpu.SemaphoreType.DMA((2,)),
            pltpu.SemaphoreType.DMA((parts,)),
            pltpu.SemaphoreType.DMA((groups,)),
            pltpu.SemaphoreType.DMA((groups,)),
            pltpu.SemaphoreType.DMA,
            pltpu.SemaphoreType.DMA((groups,)),
        ],
        compiler_params=pltpu.CompilerParams(vmem_limit_bytes=58 * MIB),
        cost_estimate=pl.CostEstimate(
            flops=2 * rows * width * KVW,
            bytes_accessed=2 * (w_all.size + queries.size + 2 * o.size),
            transcendentals=rows * HEADS * 2,
        ),
        name="tail",
    )(
        hidden_in,
        back,
        kv_gain.reshape(1, LATENT),
        cosine,
        sine,
        top,
        total,
        place_weight,
        w_all,
        queries,
        o,
    )


def plus(*terms):
    total = terms[0].astype(jnp.float32)
    for term in terms[1:]:
        total = total + term.astype(jnp.float32)
    return total.astype(jnp.bfloat16)


def after(values, *others):
    return lax.optimization_barrier((values, others))[0]


def body(
    hidden_in,
    norm_gain,
    route_logits,
    expert_ids,
    w_gate,
    w_up,
    w_down,
    w_latent,
    kv_gain,
    queries,
    page_pool,
    page_table,
    kv_lengths,
    migration,
):
    dp_count = lax.axis_size("dp")
    ex_count = lax.axis_size("expert")
    row_count = hidden_in.shape[0]
    local_experts = w_gate.shape[0]
    window = local_experts * dp_count
    width = hidden_in.shape[1]
    padded = w_latent.shape[0] + 8
    w_padded = jnp.concatenate([w_latent, w_latent[:8]], axis=0)
    w_plane = lax.all_gather(w_padded, "expert", axis=0, tiled=True)
    slots = local_experts * CAP
    packed, place_weight = dispatch(
        hidden_in, norm_gain, route_logits, expert_ids, window
    )
    arrived = lax.all_to_all(
        packed.reshape(dp_count, slots, width), "dp", split_axis=0, concat_axis=0, tiled=True
    )
    outgoing = jnp.take(page_pool, migration.reshape(dp_count * MCAP), axis=0, mode="clip")
    query = queries.reshape(row_count, HEADS, KVW)
    arrived = after(arrived, outgoing, query)
    arrived = arrived.reshape(window * CAP, width)
    axes = (("z", "x"), ("x", "z"))
    both = range(2)
    n = arrived.shape[0] // 2
    rows = [arrived[k * n : (k + 1) * n] for k in both]
    weights = (w_gate, w_up, w_down)

    below = [shift(rows[k], axes[k][0], 1) for k in both]
    above = [shift(rows[k], axes[k][0], -1) for k in both]
    below, above = after((below, above))
    beyond = [shift(above[k], axes[k][0], -1) for k in both]
    low = pack([(rows[k], below[k]) for k in both])
    below_low = [shift(low[k], axes[k][1], 1) for k in both]
    above_low = [shift(low[k], axes[k][1], -1) for k in both]
    high = pack([(above[k], beyond[k]) for k in both])
    more = lax.all_to_all(
        after(outgoing, below_low, above_low).reshape(dp_count, MCAP, page_pool.shape[1]),
        "dp",
        split_axis=0,
        concat_axis=0,
        tiled=True,
    ).reshape(dp_count * MCAP, PAGE, KVW)
    high, w_plane = after((high, w_plane))
    w_plane = w_plane.reshape(ex_count, padded, KVW)[:, : w_latent.shape[0]]
    w_all = lax.all_gather(
        w_plane.reshape(ex_count * w_latent.shape[0], KVW), "dp", axis=0, tiled=True
    )
    pool = after(page_pool, high).reshape(page_pool.shape[0], PAGE, KVW)
    below_high = [shift(high[k], axes[k][1], 1) for k in both]
    above_high = [shift(high[k], axes[k][1], -1) for k in both]
    y_first = ffn([[low[k], high[k], below_low[k], above_low[k]] for k in both], *weights)
    below_low, above_high, below_high, above_low = after(
        (below_low, above_high, below_high, above_low), y_first, pool, more
    )
    far_low = [shift(below_low[k], axes[k][1], 1) for k in both]
    far_high = [shift(above_high[k], axes[k][1], -1) for k in both]
    y_second = ffn([[below_high[k], above_high[k]] for k in both], *weights)
    y_first = after(y_first, y_second)
    early_down = [shift(y_first[k][2], axes[k][1], -1) for k in both]
    early_up = [shift(y_second[k][1], axes[k][1], 1) for k in both]
    far_low, far_high = after((far_low, far_high), y_second)
    y_far = ffn([[far_low[k], far_high[k]] for k in both], *weights)
    y_far, early_down, early_up = after((y_far, early_down, early_up))
    relay_up = [shift(y_far[k][0], axes[k][1], 1) for k in both]
    relay_down = [shift(y_far[k][1], axes[k][1], -1) for k in both]
    query = after(query, y_far)
    cached, top, total = attend_cached(query, pool, more, page_table, kv_lengths)
    relay_up, relay_down = after((relay_up, relay_down), cached)
    late_up = [shift(plus(y_first[k][3], relay_up[k]), axes[k][1], 1) for k in both]
    late_down = [shift(plus(y_second[k][0], relay_down[k]), axes[k][1], -1) for k in both]
    cached = cached.reshape(row_count, HEADS * LATENT)
    late_up, late_down = after((late_up, late_down), cached)
    terms_low = [(y_first[k][0], late_up[k], early_down[k]) for k in both]
    terms_high = [(y_first[k][1], early_up[k], late_down[k]) for k in both]
    for_far = [plus(*(term[n:] for term in terms_high[k])) for k in both]
    for_below = [plus(*(term[n:] for term in terms_low[k])) for k in both]
    relayed = [shift(for_far[k], axes[k][0], 1) for k in both]
    from_above = [shift(for_below[k], axes[k][0], -1) for k in both]
    relayed, from_above = after((relayed, from_above))
    from_below = [
        shift(plus(*(term[:n] for term in terms_high[k]), relayed[k]), axes[k][0], 1) for k in both
    ]
    from_below = after(from_below)
    finished = [
        plus(*(term[:n] for term in terms_low[k]), from_below[k], from_above[k]) for k in both
    ]
    back = lax.all_to_all(
        jnp.concatenate(finished, axis=0).reshape(dp_count, slots, width),
        "dp",
        split_axis=0,
        concat_axis=0,
        tiled=True,
    ).reshape(window * CAP, width)

    half = (KVW - LATENT) // 2
    freq = 10000.0 ** (-jnp.arange(half, dtype=jnp.float32) / half)
    angle = kv_lengths.astype(jnp.float32)[:, None] * freq[None, :]
    return tuple(
        tail(
            hidden_in,
            back,
            kv_gain,
            jnp.cos(angle),
            jnp.sin(angle),
            top,
            total,
            place_weight,
            w_all,
            queries,
            cached,
        )
    )


def solution(mesh):
    return jax.shard_map(
        body,
        mesh=mesh,
        in_specs=(
            P(("dp", "expert"), None),
            P(),
            P(("dp", "expert"), None),
            P(("dp", "expert"), None),
            P("dp", None, "expert"),
            P("dp", None, "expert"),
            P("dp", "expert", None),
            P(("dp", "expert"), None),
            P(),
            P(("dp", "expert"), None),
            P(("dp", "expert"), None),
            P(("dp", "expert"), None),
            P(("dp", "expert")),
            P("dp", "expert", None, None),
        ),
        out_specs=(P(("dp", "expert"), None), P(("dp", "expert"), None)),
        check_vma=False,
    )
```

```python
import functools

import jax
import jax.numpy as jnp
from jax import lax
from jax.experimental import pallas as pl
from jax.experimental.pallas import tpu as pltpu
from jax.sharding import PartitionSpec as P

HEADS = 64
LATENT = 512
PAGE = 16
MAXP = 6
CAP = 4
MCAP = 4
KVW = 576
SIDE = 4

softmax_scale = 192.0 ** (-0.5)
routed_scale = 2.5
norm_eps = 1e-06
MIB = 1 << 20


def rms_rows(values, gain):
    stat = jnp.mean(values * values, axis=-1, keepdims=True)
    return values * lax.rsqrt(stat + norm_eps) * gain


def shift(value, axis, step):
    pairs = []
    for x in range(SIDE):
        for z in range(SIDE):
            to_x = (x + step) % SIDE if axis == "x" else x
            to_z = (z + step) % SIDE if axis == "z" else z
            pairs.append((x * SIDE + z, to_x * SIDE + to_z))
    return lax.ppermute(value, "expert", pairs)


def dispatch_kernel(
    window, parts, ids_ref, logits_ref, gain_ref, hidden_hbm, packed_hbm, place_ref, x_buf, out_buf, in_sem, out_sem
):
    rows, width = hidden_hbm.shape
    piece = width // parts

    def load(c):
        cut = pl.ds(c * piece, piece)
        return pltpu.make_async_copy(hidden_hbm.at[:, cut], x_buf.at[:, cut], in_sem.at[c])

    def store(c):
        cut = pl.ds(c * piece, piece)
        return pltpu.make_async_copy(out_buf.at[:, cut], packed_hbm.at[:, cut], out_sem.at[c])

    for c in range(parts):
        load(c).start()
    ids = ids_ref[...]
    inside = ids < window
    has = jnp.max(inside.astype(jnp.int32), axis=0, keepdims=True)
    chosen = jnp.sum(jnp.where(inside, ids, 0), axis=0, keepdims=True)
    sigma = 1.0 / (1.0 + jnp.exp(-logits_ref[...]))
    weight = (
        routed_scale
        * jnp.sum(jnp.where(inside, sigma, 0.0), axis=0, keepdims=True)
        / jnp.sum(sigma, axis=0, keepdims=True)
    )
    expert = lax.broadcasted_iota(jnp.int32, (window, rows), 0)
    onehot = jnp.where((expert == chosen) & (has > 0), 1.0, 0.0)
    earlier = lax.broadcasted_iota(jnp.int32, (rows, rows), 0) < lax.broadcasted_iota(
        jnp.int32, (rows, rows), 1
    )
    rank = jnp.dot(
        onehot.astype(jnp.bfloat16),
        jnp.where(earlier, 1.0, 0.0).astype(jnp.bfloat16),
        preferred_element_type=jnp.float32,
    )
    slot = jnp.sum(rank * onehot, axis=0, keepdims=True).astype(jnp.int32)
    place = chosen * CAP + slot
    pick = (lax.broadcasted_iota(jnp.int32, (window * CAP, rows), 0) == place) & (has > 0)
    place_ref[...] = jnp.where(pick, weight, 0.0).T
    pick = jnp.where(pick, 1.0, 0.0).astype(jnp.bfloat16)
    square = jnp.zeros((rows, 128), jnp.float32)
    for c in range(parts):
        load(c).wait()
        for i in range(c * piece, (c + 1) * piece, 128):
            value = x_buf[:, i : i + 128].astype(jnp.float32)
            square += value * value
    scale = lax.rsqrt(jnp.sum(square, axis=1, keepdims=True) / width + norm_eps)
    for c in range(parts):
        cut = slice(c * piece, (c + 1) * piece)
        normed = (x_buf[:, cut].astype(jnp.float32) * scale * gain_ref[:, cut]).astype(jnp.bfloat16)
        out_buf[:, cut] = jnp.dot(pick, normed, preferred_element_type=jnp.float32).astype(
            jnp.bfloat16
        )
        store(c).start()
    for c in range(parts):
        store(c).wait()


def dispatch(hidden_in, norm_gain, route_logits, expert_ids, window):
    rows, width = hidden_in.shape
    places, parts = window * CAP, 4
    vmem = pl.BlockSpec(memory_space=pltpu.VMEM)
    hbm = pl.BlockSpec(memory_space=pl.ANY)
    return pl.pallas_call(
        functools.partial(dispatch_kernel, window, parts),
        out_shape=[
            jax.ShapeDtypeStruct((places, width), jnp.bfloat16),
            jax.ShapeDtypeStruct((rows, places), jnp.float32),
        ],
        in_specs=[vmem] * 3 + [hbm],
        out_specs=[hbm, vmem],
        scratch_shapes=[
            pltpu.VMEM((rows, width), jnp.bfloat16),
            pltpu.VMEM((places, width), jnp.bfloat16),
            pltpu.SemaphoreType.DMA((parts,)),
            pltpu.SemaphoreType.DMA((parts,)),
        ],
        compiler_params=pltpu.CompilerParams(vmem_limit_bytes=58 * MIB),
        cost_estimate=pl.CostEstimate(
            flops=2 * rows * places * width,
            bytes_accessed=4 * rows * width,
            transcendentals=rows * 16,
        ),
        name="dispatch",
    )(expert_ids.T, route_logits.T, norm_gain.reshape(1, width), hidden_in)


def ffn_kernel(count, rows, parts, *refs):
    xs = refs[:count]
    gate_hbm, up_hbm, down_hbm = refs[count : count + 3]
    outs = refs[count + 3 : 2 * count + 3]
    x_buf, w_buf, d_buf, o_buf, acc, in_sem, w_sem, d_sem, out_sem = refs[2 * count + 3 :]
    depth = gate_hbm.shape[1]
    piece = depth // parts

    def loads(c):
        cut = pl.ds(pl.multiple_of(c * piece, piece), piece)
        for e in range(2):
            for j, source in enumerate((gate_hbm, up_hbm)):
                yield pltpu.make_async_copy(
                    source.at[e, cut],
                    w_buf.at[cut, pl.ds(256 * e + 128 * j, 128)],
                    w_sem.at[c, 2 * e + j],
                )
        for i in range(count):
            yield pltpu.make_async_copy(
                xs[i].at[:, cut], x_buf.at[pl.ds(i * rows, rows), cut], in_sem.at[c, i]
            )

    def stores(c):
        cut = pl.ds(pl.multiple_of(c * piece, piece), piece)
        for i in range(count):
            yield pltpu.make_async_copy(
                o_buf.at[pl.ds(i * rows, rows), cut], outs[i].at[:, cut], out_sem.at[c, i]
            )

    @pl.loop(0, parts)
    def _(c):
        for copy in loads(c):
            copy.start()

    down = [
        pltpu.make_async_copy(down_hbm.at[e], d_buf.at[pl.ds(128 * e, 128)], d_sem.at[e])
        for e in range(2)
    ]
    for copy in down:
        copy.start()
    acc[...] = jnp.zeros_like(acc)

    @pl.loop(0, parts)
    def _(c):
        for copy in loads(c):
            copy.wait()
        cut = pl.ds(pl.multiple_of(c * piece, piece), piece)
        acc[...] += jnp.dot(x_buf[:, cut], w_buf[cut, :], preferred_element_type=jnp.float32)

    first = lax.broadcasted_iota(jnp.int32, (rows * count, 128), 0) % (2 * CAP) < CAP
    gate = jnp.where(first, acc[:, :128], acc[:, 256:384])
    up = jnp.where(first, acc[:, 128:256], acc[:, 384:])
    active = gate / (1.0 + jnp.exp(-gate)) * up
    active = jnp.concatenate(
        [jnp.where(first, active, 0.0), jnp.where(first, 0.0, active)], axis=1
    ).astype(jnp.bfloat16)
    for copy in down:
        copy.wait()

    @pl.loop(0, parts)
    def _(c):
        cut = pl.ds(pl.multiple_of(c * piece, piece), piece)
        o_buf[:, cut] = jnp.dot(active, d_buf[:, cut], preferred_element_type=jnp.float32).astype(
            jnp.bfloat16
        )
        for copy in stores(c):
            copy.start()

    @pl.loop(0, parts)
    def _(c):
        for copy in stores(c):
            copy.wait()


def ffn(blocks, w_gate, w_up, w_down):
    chains, per_chain = len(blocks), len(blocks[0])
    flat = [block for part in blocks for block in part]
    count, rows, depth, parts = len(flat), flat[0].shape[0], w_gate.shape[1], 4
    total = rows * count
    done = pl.pallas_call(
        functools.partial(ffn_kernel, count, rows, parts),
        out_shape=[jax.ShapeDtypeStruct(block.shape, jnp.bfloat16) for block in flat],
        in_specs=[pl.BlockSpec(memory_space=pl.ANY)] * (count + 3),
        out_specs=[pl.BlockSpec(memory_space=pl.ANY)] * count,
        scratch_shapes=[
            pltpu.VMEM((total, depth), jnp.bfloat16),
            pltpu.VMEM((depth, 512), jnp.bfloat16),
            pltpu.VMEM((256, depth), jnp.bfloat16),
            pltpu.VMEM((total, depth), jnp.bfloat16),
            pltpu.VMEM((total, 512), jnp.float32),
            pltpu.SemaphoreType.DMA((parts, count)),
            pltpu.SemaphoreType.DMA((parts, 4)),
            pltpu.SemaphoreType.DMA((2,)),
            pltpu.SemaphoreType.DMA((parts, count)),
        ],
        compiler_params=pltpu.CompilerParams(vmem_limit_bytes=58 * MIB),
        cost_estimate=pl.CostEstimate(
            flops=2 * total * depth * 768,
            bytes_accessed=2 * depth * (768 + 2 * total),
            transcendentals=total * 128,
        ),
        name="ffn",
    )(*flat, w_gate, w_up, w_down)
    return [done[k * per_chain : (k + 1) * per_chain] for k in range(chains)]


def attend_kernel(
    step, table, lengths, q_ref, pool_hbm, more_hbm, out_ref, top_ref, total_ref, pages, sem
):
    own_pages = pool_hbm.shape[0]

    @pl.when(pl.program_id(0) == 0)
    def _():
        copies = [
            pltpu.make_async_copy(pool_hbm, pages.at[pl.ds(0, own_pages)], sem.at[0]),
            pltpu.make_async_copy(
                more_hbm, pages.at[pl.ds(own_pages, more_hbm.shape[0])], sem.at[1]
            ),
        ]
        for copy in copies:
            copy.start()
        for copy in copies:
            copy.wait()

    first = pl.program_id(0) * step
    keys = [
        jnp.concatenate([pages[table[(first + r) * MAXP + p]] for p in range(MAXP)], axis=0)
        for r in range(step)
    ]
    scores = jnp.concatenate(
        [
            lax.dot_general(
                keys[r], q_ref[r], (((1,), (1,)), ((), ())), preferred_element_type=jnp.float32
            )
            for r in range(step)
        ],
        axis=1,
    )
    scores = scores * softmax_scale
    column = lax.broadcasted_iota(jnp.int32, (1, step * HEADS), 1) // HEADS
    length = jnp.zeros_like(column)
    for r in range(step):
        length = jnp.where(column == r, lengths[first + r], length)
    valid = lax.broadcasted_iota(jnp.int32, scores.shape, 0) < length
    scores = jnp.where(valid, scores, -1e30)
    top = jnp.max(scores, axis=0, keepdims=True)
    expo = jnp.where(valid, jnp.exp(scores - top), 0.0)
    total = jnp.sum(expo, axis=0, keepdims=True)
    probs = (expo / total).astype(jnp.bfloat16)
    for r in range(step):
        cut = slice(r * HEADS, (r + 1) * HEADS)
        out_ref[r] = lax.dot_general(
            probs[:, cut],
            keys[r][:, :LATENT],
            (((0,), (0,)), ((), ())),
            preferred_element_type=jnp.float32,
        ).astype(jnp.bfloat16)
        top_ref[r : r + 1, :] = top[:, cut]
        total_ref[r : r + 1, :] = total[:, cut]


def attend_cached(query, pool, more, page_table, kv_lengths):
    rows, step = query.shape[0], 8
    entries = pool.shape[0] + more.shape[0]
    hbm = pl.BlockSpec(memory_space=pl.ANY)
    return pl.pallas_call(
        functools.partial(attend_kernel, step),
        out_shape=[
            jax.ShapeDtypeStruct((rows, HEADS, LATENT), jnp.bfloat16),
            jax.ShapeDtypeStruct((rows, HEADS), jnp.float32),
            jax.ShapeDtypeStruct((rows, HEADS), jnp.float32),
        ],
        grid_spec=pltpu.PrefetchScalarGridSpec(
            num_scalar_prefetch=2,
            grid=(rows // step,),
            in_specs=[pl.BlockSpec((step, HEADS, KVW), lambda i, t, n: (i, 0, 0)), hbm, hbm],
            out_specs=[
                pl.BlockSpec((step, HEADS, LATENT), lambda i, t, n: (i, 0, 0)),
                pl.BlockSpec((step, HEADS), lambda i, t, n: (i, 0)),
                pl.BlockSpec((step, HEADS), lambda i, t, n: (i, 0)),
            ],
            scratch_shapes=[
                pltpu.VMEM((entries, PAGE, KVW), jnp.bfloat16),
                pltpu.SemaphoreType.DMA((2,)),
            ],
        ),
        compiler_params=pltpu.CompilerParams(vmem_limit_bytes=58 * MIB),
        cost_estimate=pl.CostEstimate(
            flops=2 * rows * HEADS * MAXP * PAGE * (KVW + LATENT),
            bytes_accessed=2 * (query.size + entries * PAGE * KVW + rows * HEADS * LATENT),
            transcendentals=rows * HEADS * MAXP * PAGE,
        ),
        name="attend_cached",
    )(page_table.reshape(rows * MAXP), kv_lengths, query, pool, more)


def pack_kernel(count, *refs):
    blocks, joined = refs[: 2 * count], refs[2 * count : 3 * count]
    buf, in_sem, out_sem = refs[3 * count :]
    n = blocks[0].shape[0]
    loads = [
        pltpu.make_async_copy(blocks[i], buf.at[i // 2, pl.ds(i % 2 * n, n)], in_sem.at[i])
        for i in range(2 * count)
    ]
    stores = [pltpu.make_async_copy(buf.at[i], joined[i], out_sem.at[i]) for i in range(count)]
    for copy in loads:
        copy.start()
    for i in range(count):
        loads[2 * i].wait()
        loads[2 * i + 1].wait()
        stores[i].start()
    for copy in stores:
        copy.wait()


def pack(pairs):
    count, (n, width) = len(pairs), pairs[0][0].shape
    hbm = pl.BlockSpec(memory_space=pl.ANY)
    return pl.pallas_call(
        functools.partial(pack_kernel, count),
        out_shape=[jax.ShapeDtypeStruct((2 * n, width), jnp.bfloat16)] * count,
        in_specs=[hbm] * (2 * count),
        out_specs=[hbm] * count,
        scratch_shapes=[
            pltpu.VMEM((count, 2 * n, width), jnp.bfloat16),
            pltpu.SemaphoreType.DMA((2 * count,)),
            pltpu.SemaphoreType.DMA((count,)),
        ],
        compiler_params=pltpu.CompilerParams(vmem_limit_bytes=58 * MIB),
        cost_estimate=pl.CostEstimate(
            flops=0, bytes_accessed=8 * count * n * width, transcendentals=0
        ),
        name="pack",
    )(*(block for pair in pairs for block in pair))


def tail_kernel(
    parts,
    groups,
    hidden_hbm,
    back_hbm,
    gain_ref,
    cos_ref,
    sin_ref,
    top_ref,
    total_ref,
    place_ref,
    w_hbm,
    q_hbm,
    o_hbm,
    hidden_out_hbm,
    out_hbm,
    w_ref,
    q_ref,
    o_ref,
    hidden_ref,
    back_ref,
    hidden_buf,
    key_buf,
    own_buf,
    keep_buf,
    in_sem,
    w_sem,
    q_sem,
    o_sem,
    hidden_sem,
    out_sem,
):
    width = hidden_ref.shape[1]
    loads = [
        pltpu.make_async_copy(back_hbm, back_ref, in_sem.at[0]),
        pltpu.make_async_copy(hidden_hbm, hidden_ref, in_sem.at[1]),
    ]
    for copy in loads:
        copy.start()
    piece = width // parts
    per_group = HEADS // groups
    span, q_span = per_group * LATENT, per_group * KVW

    def w_load(c):
        cut = pl.ds(pl.multiple_of(c * piece, piece), piece)
        return pltpu.make_async_copy(w_hbm.at[cut], w_ref.at[cut], w_sem.at[c])

    def q_load(g):
        cut = pl.ds(pl.multiple_of(g * q_span, 128), q_span)
        return pltpu.make_async_copy(q_hbm.at[:, cut], q_ref.at[:, cut], q_sem.at[g])

    def o_load(g):
        cut = pl.ds(pl.multiple_of(g * span, span), span)
        return pltpu.make_async_copy(o_hbm.at[:, cut], o_ref.at[:, cut], o_sem.at[g])

    def store(g):
        cut = pl.ds(pl.multiple_of(g * span, span), span)
        return pltpu.make_async_copy(o_ref.at[:, cut], out_hbm.at[:, cut], out_sem.at[g])

    for c in range(parts):
        w_load(c).start()

    @pl.loop(0, groups)
    def _(g):
        q_load(g).start()

    @pl.loop(0, groups)
    def _(g):
        o_load(g).start()

    place = place_ref[...]
    pick = (place != 0.0).astype(jnp.bfloat16)
    weight = jnp.sum(place, axis=1, keepdims=True)
    projected = jnp.zeros((hidden_ref.shape[0], KVW), jnp.float32)
    for copy in loads:
        copy.wait()
    for c in range(parts):
        cut = slice(c * piece, (c + 1) * piece)
        picked = jnp.dot(pick, back_ref[:, cut], preferred_element_type=jnp.float32)
        hidden = (hidden_ref[:, cut].astype(jnp.float32) + weight * picked).astype(jnp.bfloat16)
        hidden_buf[:, cut] = hidden
        w_load(c).wait()
        projected += jnp.dot(hidden, w_ref[cut, :], preferred_element_type=jnp.float32)
    hidden_copy = pltpu.make_async_copy(hidden_buf, hidden_out_hbm, hidden_sem)
    hidden_copy.start()
    latent = rms_rows(projected[:, :LATENT], gain_ref[...])
    first = projected[:, LATENT : LATENT + 32]
    second = projected[:, LATENT + 32 :]
    cosine, sine = cos_ref[...], sin_ref[...]
    new_key = jnp.concatenate(
        [latent, first * cosine - second * sine, second * cosine + first * sine], axis=1
    )
    new_key = new_key.astype(jnp.bfloat16).astype(jnp.float32)
    key_buf[...] = jnp.concatenate([new_key, new_key], axis=1)
    lane = lax.broadcasted_iota(jnp.int32, (8, 128), 1)
    head = lax.broadcasted_iota(jnp.int32, (8, HEADS), 1)
    blocks = hidden_ref.shape[0] // 8
    own_buf[...] = jnp.zeros_like(own_buf)

    @pl.loop(0, HEADS // 2)
    def _(j):
        @pl.when(j % (per_group // 2) == 0)
        def _():
            q_load(j // (per_group // 2)).wait()

        cut = pl.ds(pl.multiple_of(j * 2 * KVW, 128), 2 * KVW)
        for b in range(blocks):
            rows = slice(8 * b, 8 * b + 8)
            product = q_ref[rows, cut].astype(jnp.float32) * key_buf[rows, :]
            tiles = [product[:, 128 * i : 128 * (i + 1)] for i in range(9)]
            low = (tiles[0] + tiles[1]) + (tiles[2] + tiles[3]) + jnp.where(lane < 64, tiles[4], 0.0)
            high = (tiles[5] + tiles[6]) + (tiles[7] + tiles[8])
            high = high + jnp.where(lane < 64, 0.0, tiles[4])
            low = jnp.sum(low, axis=1, keepdims=True)
            high = jnp.sum(high, axis=1, keepdims=True)
            own_buf[rows, :] = jnp.where(
                head == 2 * j, low, jnp.where(head == 2 * j + 1, high, own_buf[rows, :])
            )

    own = own_buf[...] * softmax_scale
    top_old = top_ref[...]
    top = jnp.maximum(top_old, own)
    part = total_ref[...] * jnp.exp(top_old - top)
    part_own = jnp.exp(own - top)
    inverse = 1.0 / (part + part_own)
    keep_buf[...] = part * inverse
    own_buf[...] = (part_own * inverse).astype(jnp.bfloat16).astype(jnp.float32)

    @pl.loop(0, groups)
    def _(g):
        o_load(g).wait()
        for b in range(blocks):
            rows = slice(8 * b, 8 * b + 8)
            key_low = key_buf[rows, :LATENT]
            keeps, adds = keep_buf[rows, :], own_buf[rows, :]
            for i in range(per_group):
                h = g * per_group + i
                keep = jnp.sum(jnp.where(head == h, keeps, 0.0), axis=1, keepdims=True)
                add = jnp.sum(jnp.where(head == h, adds, 0.0), axis=1, keepdims=True)
                cut = pl.ds(pl.multiple_of(h * LATENT, LATENT), LATENT)
                o_ref[rows, cut] = (
                    o_ref[rows, cut].astype(jnp.float32) * keep + add * key_low
                ).astype(jnp.bfloat16)
        store(g).start()

    @pl.loop(0, groups)
    def _(g):
        store(g).wait()

    hidden_copy.wait()


def tail(hidden_in, back, kv_gain, cosine, sine, top, total, place_weight, w_all, queries, o):
    rows, width = hidden_in.shape
    parts, groups = 7, 8
    vmem = pl.BlockSpec(memory_space=pltpu.VMEM)
    hbm = pl.BlockSpec(memory_space=pl.ANY)
    return pl.pallas_call(
        functools.partial(tail_kernel, parts, groups),
        out_shape=[
            jax.ShapeDtypeStruct((rows, width), jnp.bfloat16),
            jax.ShapeDtypeStruct((rows, HEADS * LATENT), jnp.bfloat16),
        ],
        in_specs=[hbm] * 2 + [vmem] * 6 + [hbm] * 3,
        out_specs=[hbm] * 2,
        scratch_shapes=[
            pltpu.VMEM(w_all.shape, jnp.bfloat16),
            pltpu.VMEM(queries.shape, jnp.bfloat16),
            pltpu.VMEM(o.shape, jnp.bfloat16),
            pltpu.VMEM((rows, width), jnp.bfloat16),
            pltpu.VMEM(back.shape, jnp.bfloat16),
            pltpu.VMEM((rows, width), jnp.bfloat16),
            pltpu.VMEM((rows, 2 * KVW), jnp.float32),
            pltpu.VMEM((rows, HEADS), jnp.float32),
            pltpu.VMEM((rows, HEADS), jnp.float32),
            pltpu.SemaphoreType.DMA((2,)),
            pltpu.SemaphoreType.DMA((parts,)),
            pltpu.SemaphoreType.DMA((groups,)),
            pltpu.SemaphoreType.DMA((groups,)),
            pltpu.SemaphoreType.DMA,
            pltpu.SemaphoreType.DMA((groups,)),
        ],
        compiler_params=pltpu.CompilerParams(vmem_limit_bytes=58 * MIB),
        cost_estimate=pl.CostEstimate(
            flops=2 * rows * width * KVW,
            bytes_accessed=2 * (w_all.size + queries.size + 2 * o.size),
            transcendentals=rows * HEADS * 2,
        ),
        name="tail",
    )(
        hidden_in,
        back,
        kv_gain.reshape(1, LATENT),
        cosine,
        sine,
        top,
        total,
        place_weight,
        w_all,
        queries,
        o,
    )


def plus(*terms):
    total = terms[0].astype(jnp.float32)
    for term in terms[1:]:
        total = total + term.astype(jnp.float32)
    return total.astype(jnp.bfloat16)


def after(values, *others):
    return lax.optimization_barrier((values, others))[0]


def body(
    hidden_in,
    norm_gain,
    route_logits,
    expert_ids,
    w_gate,
    w_up,
    w_down,
    w_latent,
    kv_gain,
    queries,
    page_pool,
    page_table,
    kv_lengths,
    migration,
):
    dp_count = lax.axis_size("dp")
    ex_count = lax.axis_size("expert")
    row_count = hidden_in.shape[0]
    local_experts = w_gate.shape[0]
    window = local_experts * dp_count
    width = hidden_in.shape[1]
    padded = w_latent.shape[0] + 8
    w_padded = jnp.concatenate([w_latent, w_latent[:8]], axis=0)
    w_plane = lax.all_gather(w_padded, "expert", axis=0, tiled=True)
    slots = local_experts * CAP
    packed, place_weight = dispatch(
        hidden_in, norm_gain, route_logits, expert_ids, window
    )
    arrived = lax.all_to_all(
        packed.reshape(dp_count, slots, width), "dp", split_axis=0, concat_axis=0, tiled=True
    )
    outgoing = jnp.take(page_pool, migration.reshape(dp_count * MCAP), axis=0, mode="clip")
    query = queries.reshape(row_count, HEADS, KVW)
    arrived = after(arrived, outgoing, query)
    arrived = arrived.reshape(window * CAP, width)
    axes = (("z", "x"), ("x", "z"))
    both = range(2)
    n = arrived.shape[0] // 2
    rows = [arrived[k * n : (k + 1) * n] for k in both]
    weights = (w_gate, w_up, w_down)

    below = [shift(rows[k], axes[k][0], 1) for k in both]
    above = [shift(rows[k], axes[k][0], -1) for k in both]
    below, above = after((below, above))
    beyond = [shift(above[k], axes[k][0], -1) for k in both]
    low = pack([(rows[k], below[k]) for k in both])
    below_low = [shift(low[k], axes[k][1], 1) for k in both]
    low_too, beyond = after((low, beyond))
    above_low = [shift(low_too[k], axes[k][1], -1) for k in both]
    high = pack([(above[k], beyond[k]) for k in both])
    more = lax.all_to_all(
        after(outgoing, high).reshape(dp_count, MCAP, page_pool.shape[1]),
        "dp",
        split_axis=0,
        concat_axis=0,
        tiled=True,
    )
    high, w_plane = after((high, w_plane))
    w_plane = w_plane.reshape(ex_count, padded, KVW)[:, : w_latent.shape[0]]
    w_all = lax.all_gather(
        w_plane.reshape(ex_count * w_latent.shape[0], KVW), "dp", axis=0, tiled=True
    )
    pool = after(page_pool, high).reshape(page_pool.shape[0], PAGE, KVW)
    below_high = [shift(high[k], axes[k][1], 1) for k in both]
    above_high = [shift(high[k], axes[k][1], -1) for k in both]
    low, more = after((low, more))
    y_first = ffn([[low[k], high[k], below_low[k], above_low[k]] for k in both], *weights)
    far_low = [shift(after(below_low[k], y_first), axes[k][1], 1) for k in both]
    far_high = [shift(after(above_high[k], y_first), axes[k][1], -1) for k in both]
    more = after(more, y_first).reshape(dp_count * MCAP, PAGE, KVW)
    below_high, above_high = after((below_high, above_high), y_first, pool, more)
    y_second = ffn([[below_high[k], above_high[k]] for k in both], *weights)
    y_first = after(y_first, y_second)
    early_down = [shift(y_first[k][2], axes[k][1], -1) for k in both]
    early_up = [shift(y_second[k][1], axes[k][1], 1) for k in both]
    far_low, far_high = after((far_low, far_high), y_second)
    y_far = ffn([[far_low[k], far_high[k]] for k in both], *weights)
    relay_up = [shift(after(y_far[k][0], early_up[k]), axes[k][1], 1) for k in both]
    relay_down = [shift(after(y_far[k][1], early_down[k]), axes[k][1], -1) for k in both]
    query = after(query, y_far)
    cached, top, total = attend_cached(query, pool, more, page_table, kv_lengths)
    relay_up, relay_down = after((relay_up, relay_down), cached)
    late_up = [shift(plus(y_first[k][3], relay_up[k]), axes[k][1], 1) for k in both]
    late_down = [shift(plus(y_second[k][0], relay_down[k]), axes[k][1], -1) for k in both]
    cached = cached.reshape(row_count, HEADS * LATENT)
    late_up, late_down = after((late_up, late_down), cached)
    terms_low = [(y_first[k][0], late_up[k], early_down[k]) for k in both]
    terms_high = [(y_first[k][1], early_up[k], late_down[k]) for k in both]
    for_far = [plus(*(term[n:] for term in terms_high[k])) for k in both]
    for_below = [plus(*(term[n:] for term in terms_low[k])) for k in both]
    relayed = [shift(for_far[k], axes[k][0], 1) for k in both]
    from_above = [shift(for_below[k], axes[k][0], -1) for k in both]
    relayed, from_above = after((relayed, from_above))
    from_below = [
        shift(plus(*(term[:n] for term in terms_high[k]), relayed[k]), axes[k][0], 1) for k in both
    ]
    from_below = after(from_below)
    finished = [
        plus(*(term[:n] for term in terms_low[k]), from_below[k], from_above[k]) for k in both
    ]
    back = lax.all_to_all(
        jnp.concatenate(finished, axis=0).reshape(dp_count, slots, width),
        "dp",
        split_axis=0,
        concat_axis=0,
        tiled=True,
    ).reshape(window * CAP, width)

    half = (KVW - LATENT) // 2
    freq = 10000.0 ** (-jnp.arange(half, dtype=jnp.float32) / half)
    angle = kv_lengths.astype(jnp.float32)[:, None] * freq[None, :]
    return tuple(
        tail(
            hidden_in,
            back,
            kv_gain,
            jnp.cos(angle),
            jnp.sin(angle),
            top,
            total,
            place_weight,
            w_all,
            queries,
            cached,
        )
    )


def solution(mesh):
    return jax.shard_map(
        body,
        mesh=mesh,
        in_specs=(
            P(("dp", "expert"), None),
            P(),
            P(("dp", "expert"), None),
            P(("dp", "expert"), None),
            P("dp", None, "expert"),
            P("dp", None, "expert"),
            P("dp", "expert", None),
            P(("dp", "expert"), None),
            P(),
            P(("dp", "expert"), None),
            P(("dp", "expert"), None),
            P(("dp", "expert"), None),
            P(("dp", "expert")),
            P("dp", "expert", None, None),
        ),
        out_specs=(P(("dp", "expert"), None), P(("dp", "expert"), None)),
        check_vma=False,
    )
```

```python
import functools

import jax
import jax.numpy as jnp
from jax import lax
from jax.experimental import pallas as pl
from jax.experimental.pallas import tpu as pltpu
from jax.sharding import PartitionSpec as P

HEADS = 64
LATENT = 512
PAGE = 16
MAXP = 6
CAP = 4
MCAP = 4
KVW = 576
SIDE = 4

softmax_scale = 192.0 ** (-0.5)
routed_scale = 2.5
norm_eps = 1e-06
MIB = 1 << 20


def rms_rows(values, gain):
    stat = jnp.mean(values * values, axis=-1, keepdims=True)
    return values * lax.rsqrt(stat + norm_eps) * gain


def shift(value, axis, step):
    pairs = []
    for x in range(SIDE):
        for z in range(SIDE):
            to_x = (x + step) % SIDE if axis == "x" else x
            to_z = (z + step) % SIDE if axis == "z" else z
            pairs.append((x * SIDE + z, to_x * SIDE + to_z))
    return lax.ppermute(value, "expert", pairs)


def dispatch_kernel(
    window, parts, ids_ref, logits_ref, gain_ref, hidden_hbm, packed_hbm, place_ref, x_buf, out_buf, in_sem, out_sem
):
    rows, width = hidden_hbm.shape
    piece = width // parts

    def load(c):
        cut = pl.ds(c * piece, piece)
        return pltpu.make_async_copy(hidden_hbm.at[:, cut], x_buf.at[:, cut], in_sem.at[c])

    def store(c):
        cut = pl.ds(c * piece, piece)
        return pltpu.make_async_copy(out_buf.at[:, cut], packed_hbm.at[:, cut], out_sem.at[c])

    for c in range(parts):
        load(c).start()
    ids = ids_ref[...]
    inside = ids < window
    has = jnp.max(inside.astype(jnp.int32), axis=0, keepdims=True)
    chosen = jnp.sum(jnp.where(inside, ids, 0), axis=0, keepdims=True)
    sigma = 1.0 / (1.0 + jnp.exp(-logits_ref[...]))
    weight = (
        routed_scale
        * jnp.sum(jnp.where(inside, sigma, 0.0), axis=0, keepdims=True)
        / jnp.sum(sigma, axis=0, keepdims=True)
    )
    expert = lax.broadcasted_iota(jnp.int32, (window, rows), 0)
    onehot = jnp.where((expert == chosen) & (has > 0), 1.0, 0.0)
    earlier = lax.broadcasted_iota(jnp.int32, (rows, rows), 0) < lax.broadcasted_iota(
        jnp.int32, (rows, rows), 1
    )
    rank = jnp.dot(
        onehot.astype(jnp.bfloat16),
        jnp.where(earlier, 1.0, 0.0).astype(jnp.bfloat16),
        preferred_element_type=jnp.float32,
    )
    slot = jnp.sum(rank * onehot, axis=0, keepdims=True).astype(jnp.int32)
    place = chosen * CAP + slot
    pick = (lax.broadcasted_iota(jnp.int32, (window * CAP, rows), 0) == place) & (has > 0)
    place_ref[...] = jnp.where(pick, weight, 0.0).T
    pick = jnp.where(pick, 1.0, 0.0).astype(jnp.bfloat16)
    square = jnp.zeros((rows, 128), jnp.float32)
    for c in range(parts):
        load(c).wait()
        for i in range(c * piece, (c + 1) * piece, 128):
            value = x_buf[:, i : i + 128].astype(jnp.float32)
            square += value * value
    scale = lax.rsqrt(jnp.sum(square, axis=1, keepdims=True) / width + norm_eps)
    for c in range(parts):
        cut = slice(c * piece, (c + 1) * piece)
        normed = (x_buf[:, cut].astype(jnp.float32) * scale * gain_ref[:, cut]).astype(jnp.bfloat16)
        out_buf[:, cut] = jnp.dot(pick, normed, preferred_element_type=jnp.float32).astype(
            jnp.bfloat16
        )
        store(c).start()
    for c in range(parts):
        store(c).wait()


def dispatch(hidden_in, norm_gain, route_logits, expert_ids, window):
    rows, width = hidden_in.shape
    places, parts = window * CAP, 4
    vmem = pl.BlockSpec(memory_space=pltpu.VMEM)
    hbm = pl.BlockSpec(memory_space=pl.ANY)
    return pl.pallas_call(
        functools.partial(dispatch_kernel, window, parts),
        out_shape=[
            jax.ShapeDtypeStruct((places, width), jnp.bfloat16),
            jax.ShapeDtypeStruct((rows, places), jnp.float32),
        ],
        in_specs=[vmem] * 3 + [hbm],
        out_specs=[hbm, vmem],
        scratch_shapes=[
            pltpu.VMEM((rows, width), jnp.bfloat16),
            pltpu.VMEM((places, width), jnp.bfloat16),
            pltpu.SemaphoreType.DMA((parts,)),
            pltpu.SemaphoreType.DMA((parts,)),
        ],
        compiler_params=pltpu.CompilerParams(vmem_limit_bytes=58 * MIB),
        cost_estimate=pl.CostEstimate(
            flops=2 * rows * places * width,
            bytes_accessed=4 * rows * width,
            transcendentals=rows * 16,
        ),
        name="dispatch",
    )(expert_ids.T, route_logits.T, norm_gain.reshape(1, width), hidden_in)


def ffn_kernel(count, rows, parts, *refs):
    xs = refs[:count]
    gate_hbm, up_hbm, down_hbm = refs[count : count + 3]
    outs = refs[count + 3 : 2 * count + 3]
    x_buf, w_buf, d_buf, o_buf, acc, in_sem, w_sem, d_sem, out_sem = refs[2 * count + 3 :]
    depth = gate_hbm.shape[1]
    piece = depth // parts

    def loads(c):
        cut = pl.ds(pl.multiple_of(c * piece, piece), piece)
        for e in range(2):
            for j, source in enumerate((gate_hbm, up_hbm)):
                yield pltpu.make_async_copy(
                    source.at[e, cut],
                    w_buf.at[cut, pl.ds(256 * e + 128 * j, 128)],
                    w_sem.at[c, 2 * e + j],
                )
        for i in range(count):
            yield pltpu.make_async_copy(
                xs[i].at[:, cut], x_buf.at[pl.ds(i * rows, rows), cut], in_sem.at[c, i]
            )

    def stores(c):
        cut = pl.ds(pl.multiple_of(c * piece, piece), piece)
        for i in range(count):
            yield pltpu.make_async_copy(
                o_buf.at[pl.ds(i * rows, rows), cut], outs[i].at[:, cut], out_sem.at[c, i]
            )

    @pl.loop(0, parts)
    def _(c):
        for copy in loads(c):
            copy.start()

    down = [
        pltpu.make_async_copy(down_hbm.at[e], d_buf.at[pl.ds(128 * e, 128)], d_sem.at[e])
        for e in range(2)
    ]
    for copy in down:
        copy.start()
    acc[...] = jnp.zeros_like(acc)

    @pl.loop(0, parts)
    def _(c):
        for copy in loads(c):
            copy.wait()
        cut = pl.ds(pl.multiple_of(c * piece, piece), piece)
        acc[...] += jnp.dot(x_buf[:, cut], w_buf[cut, :], preferred_element_type=jnp.float32)

    first = lax.broadcasted_iota(jnp.int32, (rows * count, 128), 0) % (2 * CAP) < CAP
    gate = jnp.where(first, acc[:, :128], acc[:, 256:384])
    up = jnp.where(first, acc[:, 128:256], acc[:, 384:])
    active = gate / (1.0 + jnp.exp(-gate)) * up
    active = jnp.concatenate(
        [jnp.where(first, active, 0.0), jnp.where(first, 0.0, active)], axis=1
    ).astype(jnp.bfloat16)
    for copy in down:
        copy.wait()

    @pl.loop(0, parts)
    def _(c):
        cut = pl.ds(pl.multiple_of(c * piece, piece), piece)
        o_buf[:, cut] = jnp.dot(active, d_buf[:, cut], preferred_element_type=jnp.float32).astype(
            jnp.bfloat16
        )
        for copy in stores(c):
            copy.start()

    @pl.loop(0, parts)
    def _(c):
        for copy in stores(c):
            copy.wait()


def ffn(blocks, w_gate, w_up, w_down):
    chains, per_chain = len(blocks), len(blocks[0])
    flat = [block for part in blocks for block in part]
    count, rows, depth, parts = len(flat), flat[0].shape[0], w_gate.shape[1], 4
    total = rows * count
    done = pl.pallas_call(
        functools.partial(ffn_kernel, count, rows, parts),
        out_shape=[jax.ShapeDtypeStruct(block.shape, jnp.bfloat16) for block in flat],
        in_specs=[pl.BlockSpec(memory_space=pl.ANY)] * (count + 3),
        out_specs=[pl.BlockSpec(memory_space=pl.ANY)] * count,
        scratch_shapes=[
            pltpu.VMEM((total, depth), jnp.bfloat16),
            pltpu.VMEM((depth, 512), jnp.bfloat16),
            pltpu.VMEM((256, depth), jnp.bfloat16),
            pltpu.VMEM((total, depth), jnp.bfloat16),
            pltpu.VMEM((total, 512), jnp.float32),
            pltpu.SemaphoreType.DMA((parts, count)),
            pltpu.SemaphoreType.DMA((parts, 4)),
            pltpu.SemaphoreType.DMA((2,)),
            pltpu.SemaphoreType.DMA((parts, count)),
        ],
        compiler_params=pltpu.CompilerParams(vmem_limit_bytes=58 * MIB),
        cost_estimate=pl.CostEstimate(
            flops=2 * total * depth * 768,
            bytes_accessed=2 * depth * (768 + 2 * total),
            transcendentals=total * 128,
        ),
        name="ffn",
    )(*flat, w_gate, w_up, w_down)
    return [done[k * per_chain : (k + 1) * per_chain] for k in range(chains)]


def attend_kernel(
    step, table, lengths, q_ref, pool_hbm, more_hbm, out_ref, top_ref, total_ref, pages, sem
):
    own_pages = pool_hbm.shape[0]

    @pl.when(pl.program_id(0) == 0)
    def _():
        copies = [
            pltpu.make_async_copy(pool_hbm, pages.at[pl.ds(0, own_pages)], sem.at[0]),
            pltpu.make_async_copy(
                more_hbm, pages.at[pl.ds(own_pages, more_hbm.shape[0])], sem.at[1]
            ),
        ]
        for copy in copies:
            copy.start()
        for copy in copies:
            copy.wait()

    first = pl.program_id(0) * step
    keys = [
        jnp.concatenate([pages[table[(first + r) * MAXP + p]] for p in range(MAXP)], axis=0)
        for r in range(step)
    ]
    scores = jnp.concatenate(
        [
            lax.dot_general(
                keys[r], q_ref[r], (((1,), (1,)), ((), ())), preferred_element_type=jnp.float32
            )
            for r in range(step)
        ],
        axis=1,
    )
    scores = scores * softmax_scale
    column = lax.broadcasted_iota(jnp.int32, (1, step * HEADS), 1) // HEADS
    length = jnp.zeros_like(column)
    for r in range(step):
        length = jnp.where(column == r, lengths[first + r], length)
    valid = lax.broadcasted_iota(jnp.int32, scores.shape, 0) < length
    scores = jnp.where(valid, scores, -1e30)
    top = jnp.max(scores, axis=0, keepdims=True)
    expo = jnp.where(valid, jnp.exp(scores - top), 0.0)
    total = jnp.sum(expo, axis=0, keepdims=True)
    probs = (expo / total).astype(jnp.bfloat16)
    for r in range(step):
        cut = slice(r * HEADS, (r + 1) * HEADS)
        out_ref[r] = lax.dot_general(
            probs[:, cut],
            keys[r][:, :LATENT],
            (((0,), (0,)), ((), ())),
            preferred_element_type=jnp.float32,
        ).astype(jnp.bfloat16)
        top_ref[r : r + 1, :] = top[:, cut]
        total_ref[r : r + 1, :] = total[:, cut]


def attend_cached(query, pool, more, page_table, kv_lengths):
    rows, step = query.shape[0], 8
    entries = pool.shape[0] + more.shape[0]
    hbm = pl.BlockSpec(memory_space=pl.ANY)
    return pl.pallas_call(
        functools.partial(attend_kernel, step),
        out_shape=[
            jax.ShapeDtypeStruct((rows, HEADS, LATENT), jnp.bfloat16),
            jax.ShapeDtypeStruct((rows, HEADS), jnp.float32),
            jax.ShapeDtypeStruct((rows, HEADS), jnp.float32),
        ],
        grid_spec=pltpu.PrefetchScalarGridSpec(
            num_scalar_prefetch=2,
            grid=(rows // step,),
            in_specs=[pl.BlockSpec((step, HEADS, KVW), lambda i, t, n: (i, 0, 0)), hbm, hbm],
            out_specs=[
                pl.BlockSpec((step, HEADS, LATENT), lambda i, t, n: (i, 0, 0)),
                pl.BlockSpec((step, HEADS), lambda i, t, n: (i, 0)),
                pl.BlockSpec((step, HEADS), lambda i, t, n: (i, 0)),
            ],
            scratch_shapes=[
                pltpu.VMEM((entries, PAGE, KVW), jnp.bfloat16),
                pltpu.SemaphoreType.DMA((2,)),
            ],
        ),
        compiler_params=pltpu.CompilerParams(vmem_limit_bytes=58 * MIB),
        cost_estimate=pl.CostEstimate(
            flops=2 * rows * HEADS * MAXP * PAGE * (KVW + LATENT),
            bytes_accessed=2 * (query.size + entries * PAGE * KVW + rows * HEADS * LATENT),
            transcendentals=rows * HEADS * MAXP * PAGE,
        ),
        name="attend_cached",
    )(page_table.reshape(rows * MAXP), kv_lengths, query, pool, more)


def pack_kernel(count, *refs):
    blocks, joined = refs[: 2 * count], refs[2 * count : 3 * count]
    buf, in_sem, out_sem = refs[3 * count :]
    n = blocks[0].shape[0]
    loads = [
        pltpu.make_async_copy(blocks[i], buf.at[i // 2, pl.ds(i % 2 * n, n)], in_sem.at[i])
        for i in range(2 * count)
    ]
    stores = [pltpu.make_async_copy(buf.at[i], joined[i], out_sem.at[i]) for i in range(count)]
    for copy in loads:
        copy.start()
    for i in range(count):
        loads[2 * i].wait()
        loads[2 * i + 1].wait()
        stores[i].start()
    for copy in stores:
        copy.wait()


def pack(pairs):
    count, (n, width) = len(pairs), pairs[0][0].shape
    hbm = pl.BlockSpec(memory_space=pl.ANY)
    return pl.pallas_call(
        functools.partial(pack_kernel, count),
        out_shape=[jax.ShapeDtypeStruct((2 * n, width), jnp.bfloat16)] * count,
        in_specs=[hbm] * (2 * count),
        out_specs=[hbm] * count,
        scratch_shapes=[
            pltpu.VMEM((count, 2 * n, width), jnp.bfloat16),
            pltpu.SemaphoreType.DMA((2 * count,)),
            pltpu.SemaphoreType.DMA((count,)),
        ],
        compiler_params=pltpu.CompilerParams(vmem_limit_bytes=58 * MIB),
        cost_estimate=pl.CostEstimate(
            flops=0, bytes_accessed=8 * count * n * width, transcendentals=0
        ),
        name="pack",
    )(*(block for pair in pairs for block in pair))


def tail_kernel(
    parts,
    groups,
    hidden_hbm,
    back_hbm,
    gain_ref,
    cos_ref,
    sin_ref,
    top_ref,
    total_ref,
    place_ref,
    w_hbm,
    q_hbm,
    o_hbm,
    hidden_out_hbm,
    out_hbm,
    w_ref,
    q_ref,
    o_ref,
    hidden_ref,
    back_ref,
    hidden_buf,
    key_buf,
    own_buf,
    keep_buf,
    in_sem,
    w_sem,
    q_sem,
    o_sem,
    hidden_sem,
    out_sem,
):
    width = hidden_ref.shape[1]
    loads = [
        pltpu.make_async_copy(back_hbm, back_ref, in_sem.at[0]),
        pltpu.make_async_copy(hidden_hbm, hidden_ref, in_sem.at[1]),
    ]
    for copy in loads:
        copy.start()
    piece = width // parts
    per_group = HEADS // groups
    span, q_span = per_group * LATENT, per_group * KVW

    def w_load(c):
        cut = pl.ds(pl.multiple_of(c * piece, piece), piece)
        return pltpu.make_async_copy(w_hbm.at[cut], w_ref.at[cut], w_sem.at[c])

    def q_load(g):
        cut = pl.ds(pl.multiple_of(g * q_span, 128), q_span)
        return pltpu.make_async_copy(q_hbm.at[:, cut], q_ref.at[:, cut], q_sem.at[g])

    def o_load(g):
        cut = pl.ds(pl.multiple_of(g * span, span), span)
        return pltpu.make_async_copy(o_hbm.at[:, cut], o_ref.at[:, cut], o_sem.at[g])

    def store(g):
        cut = pl.ds(pl.multiple_of(g * span, span), span)
        return pltpu.make_async_copy(o_ref.at[:, cut], out_hbm.at[:, cut], out_sem.at[g])

    for c in range(parts):
        w_load(c).start()

    @pl.loop(0, groups)
    def _(g):
        q_load(g).start()

    @pl.loop(0, groups)
    def _(g):
        o_load(g).start()

    place = place_ref[...]
    pick = (place != 0.0).astype(jnp.bfloat16)
    weight = jnp.sum(place, axis=1, keepdims=True)
    projected = jnp.zeros((hidden_ref.shape[0], KVW), jnp.float32)
    for copy in loads:
        copy.wait()
    for c in range(parts):
        cut = slice(c * piece, (c + 1) * piece)
        picked = jnp.dot(pick, back_ref[:, cut], preferred_element_type=jnp.float32)
        hidden = (hidden_ref[:, cut].astype(jnp.float32) + weight * picked).astype(jnp.bfloat16)
        hidden_buf[:, cut] = hidden
        w_load(c).wait()
        projected += jnp.dot(hidden, w_ref[cut, :], preferred_element_type=jnp.float32)
    hidden_copy = pltpu.make_async_copy(hidden_buf, hidden_out_hbm, hidden_sem)
    hidden_copy.start()
    latent = rms_rows(projected[:, :LATENT], gain_ref[...])
    first = projected[:, LATENT : LATENT + 32]
    second = projected[:, LATENT + 32 :]
    cosine, sine = cos_ref[...], sin_ref[...]
    new_key = jnp.concatenate(
        [latent, first * cosine - second * sine, second * cosine + first * sine], axis=1
    )
    new_key = new_key.astype(jnp.bfloat16).astype(jnp.float32)
    key_buf[...] = jnp.concatenate([new_key, new_key], axis=1)
    lane = lax.broadcasted_iota(jnp.int32, (8, 128), 1)
    head = lax.broadcasted_iota(jnp.int32, (8, HEADS), 1)
    blocks = hidden_ref.shape[0] // 8
    own_buf[...] = jnp.zeros_like(own_buf)

    @pl.loop(0, HEADS // 2)
    def _(j):
        @pl.when(j % (per_group // 2) == 0)
        def _():
            q_load(j // (per_group // 2)).wait()

        cut = pl.ds(pl.multiple_of(j * 2 * KVW, 128), 2 * KVW)
        for b in range(blocks):
            rows = slice(8 * b, 8 * b + 8)
            product = q_ref[rows, cut].astype(jnp.float32) * key_buf[rows, :]
            tiles = [product[:, 128 * i : 128 * (i + 1)] for i in range(9)]
            low = (tiles[0] + tiles[1]) + (tiles[2] + tiles[3]) + jnp.where(lane < 64, tiles[4], 0.0)
            high = (tiles[5] + tiles[6]) + (tiles[7] + tiles[8])
            high = high + jnp.where(lane < 64, 0.0, tiles[4])
            low = jnp.sum(low, axis=1, keepdims=True)
            high = jnp.sum(high, axis=1, keepdims=True)
            own_buf[rows, :] = jnp.where(
                head == 2 * j, low, jnp.where(head == 2 * j + 1, high, own_buf[rows, :])
            )

    own = own_buf[...] * softmax_scale
    top_old = top_ref[...]
    top = jnp.maximum(top_old, own)
    part = total_ref[...] * jnp.exp(top_old - top)
    part_own = jnp.exp(own - top)
    inverse = 1.0 / (part + part_own)
    keep_buf[...] = part * inverse
    own_buf[...] = (part_own * inverse).astype(jnp.bfloat16).astype(jnp.float32)

    @pl.loop(0, groups)
    def _(g):
        o_load(g).wait()
        for b in range(blocks):
            rows = slice(8 * b, 8 * b + 8)
            key_low = key_buf[rows, :LATENT]
            keeps, adds = keep_buf[rows, :], own_buf[rows, :]
            for i in range(per_group):
                h = g * per_group + i
                keep = jnp.sum(jnp.where(head == h, keeps, 0.0), axis=1, keepdims=True)
                add = jnp.sum(jnp.where(head == h, adds, 0.0), axis=1, keepdims=True)
                cut = pl.ds(pl.multiple_of(h * LATENT, LATENT), LATENT)
                o_ref[rows, cut] = (
                    o_ref[rows, cut].astype(jnp.float32) * keep + add * key_low
                ).astype(jnp.bfloat16)
        store(g).start()

    @pl.loop(0, groups)
    def _(g):
        store(g).wait()

    hidden_copy.wait()


def tail(hidden_in, back, kv_gain, cosine, sine, top, total, place_weight, w_all, queries, o):
    rows, width = hidden_in.shape
    parts, groups = 7, 8
    vmem = pl.BlockSpec(memory_space=pltpu.VMEM)
    hbm = pl.BlockSpec(memory_space=pl.ANY)
    return pl.pallas_call(
        functools.partial(tail_kernel, parts, groups),
        out_shape=[
            jax.ShapeDtypeStruct((rows, width), jnp.bfloat16),
            jax.ShapeDtypeStruct((rows, HEADS * LATENT), jnp.bfloat16),
        ],
        in_specs=[hbm] * 2 + [vmem] * 6 + [hbm] * 3,
        out_specs=[hbm] * 2,
        scratch_shapes=[
            pltpu.VMEM(w_all.shape, jnp.bfloat16),
            pltpu.VMEM(queries.shape, jnp.bfloat16),
            pltpu.VMEM(o.shape, jnp.bfloat16),
            pltpu.VMEM((rows, width), jnp.bfloat16),
            pltpu.VMEM(back.shape, jnp.bfloat16),
            pltpu.VMEM((rows, width), jnp.bfloat16),
            pltpu.VMEM((rows, 2 * KVW), jnp.float32),
            pltpu.VMEM((rows, HEADS), jnp.float32),
            pltpu.VMEM((rows, HEADS), jnp.float32),
            pltpu.SemaphoreType.DMA((2,)),
            pltpu.SemaphoreType.DMA((parts,)),
            pltpu.SemaphoreType.DMA((groups,)),
            pltpu.SemaphoreType.DMA((groups,)),
            pltpu.SemaphoreType.DMA,
            pltpu.SemaphoreType.DMA((groups,)),
        ],
        compiler_params=pltpu.CompilerParams(vmem_limit_bytes=58 * MIB),
        cost_estimate=pl.CostEstimate(
            flops=2 * rows * width * KVW,
            bytes_accessed=2 * (w_all.size + queries.size + 2 * o.size),
            transcendentals=rows * HEADS * 2,
        ),
        name="tail",
    )(
        hidden_in,
        back,
        kv_gain.reshape(1, LATENT),
        cosine,
        sine,
        top,
        total,
        place_weight,
        w_all,
        queries,
        o,
    )


def plus(*terms):
    total = terms[0].astype(jnp.float32)
    for term in terms[1:]:
        total = total + term.astype(jnp.float32)
    return total.astype(jnp.bfloat16)


def after(values, *others):
    return lax.optimization_barrier((values, others))[0]


def body(
    hidden_in,
    norm_gain,
    route_logits,
    expert_ids,
    w_gate,
    w_up,
    w_down,
    w_latent,
    kv_gain,
    queries,
    page_pool,
    page_table,
    kv_lengths,
    migration,
):
    dp_count = lax.axis_size("dp")
    ex_count = lax.axis_size("expert")
    row_count = hidden_in.shape[0]
    local_experts = w_gate.shape[0]
    window = local_experts * dp_count
    width = hidden_in.shape[1]
    padded = w_latent.shape[0] + 8
    w_padded = jnp.concatenate([w_latent, w_latent[:8]], axis=0)
    w_plane = lax.all_gather(w_padded, "expert", axis=0, tiled=True)
    slots = local_experts * CAP
    packed, place_weight = dispatch(
        hidden_in, norm_gain, route_logits, expert_ids, window
    )
    arrived = lax.all_to_all(
        packed.reshape(dp_count, slots, width), "dp", split_axis=0, concat_axis=0, tiled=True
    )
    outgoing = jnp.take(page_pool, migration.reshape(dp_count * MCAP), axis=0, mode="clip")
    query = queries.reshape(row_count, HEADS, KVW)
    arrived = after(arrived, outgoing, query)
    arrived = arrived.reshape(window * CAP, width)
    axes = (("z", "x"), ("x", "z"))
    both = range(2)
    n = arrived.shape[0] // 2
    rows = [arrived[k * n : (k + 1) * n] for k in both]
    weights = (w_gate, w_up, w_down)

    below = [shift(rows[k], axes[k][0], 1) for k in both]
    above = [shift(rows[k], axes[k][0], -1) for k in both]
    below, above = after((below, above))
    beyond = [shift(above[k], axes[k][0], -1) for k in both]
    low = pack([(rows[k], below[k]) for k in both])
    below_low = [shift(low[k], axes[k][1], 1) for k in both]
    low_too, beyond = after((low, beyond))
    above_low = [shift(low_too[k], axes[k][1], -1) for k in both]
    high = pack([(above[k], beyond[k]) for k in both])
    more = lax.all_to_all(
        after(outgoing, below_low, above_low).reshape(dp_count, MCAP, page_pool.shape[1]),
        "dp",
        split_axis=0,
        concat_axis=0,
        tiled=True,
    )
    high, w_plane = after((high, w_plane))
    w_plane = w_plane.reshape(ex_count, padded, KVW)[:, : w_latent.shape[0]]
    w_all = lax.all_gather(
        w_plane.reshape(ex_count * w_latent.shape[0], KVW), "dp", axis=0, tiled=True
    )
    pool = after(page_pool, high).reshape(page_pool.shape[0], PAGE, KVW)
    below_high = [shift(high[k], axes[k][1], 1) for k in both]
    above_high = [shift(high[k], axes[k][1], -1) for k in both]
    y_first = ffn([[low[k], high[k], below_low[k], above_low[k]] for k in both], *weights)
    more = more.reshape(dp_count * MCAP, PAGE, KVW)
    far_low = [shift(after(below_low[k], y_first, more), axes[k][1], 1) for k in both]
    far_high = [shift(after(above_high[k], y_first), axes[k][1], -1) for k in both]
    below_high, above_high = after((below_high, above_high), y_first, pool)
    y_second = ffn([[below_high[k], above_high[k]] for k in both], *weights)
    y_first = after(y_first, y_second)
    early_down = [shift(y_first[k][2], axes[k][1], -1) for k in both]
    early_up = [shift(y_second[k][1], axes[k][1], 1) for k in both]
    far_low, far_high = after((far_low, far_high), y_second)
    y_far = ffn([[far_low[k], far_high[k]] for k in both], *weights)
    relay_up = [shift(after(y_far[k][0], early_up[k]), axes[k][1], 1) for k in both]
    relay_down = [shift(after(y_far[k][1], early_down[k]), axes[k][1], -1) for k in both]
    query = after(query, y_far)
    cached, top, total = attend_cached(query, pool, more, page_table, kv_lengths)
    relay_up, relay_down = after((relay_up, relay_down), cached)
    late_up = [shift(plus(y_first[k][3], relay_up[k]), axes[k][1], 1) for k in both]
    late_down = [shift(plus(y_second[k][0], relay_down[k]), axes[k][1], -1) for k in both]
    cached = cached.reshape(row_count, HEADS * LATENT)
    late_up, late_down = after((late_up, late_down), cached)
    terms_low = [(y_first[k][0], late_up[k], early_down[k]) for k in both]
    terms_high = [(y_first[k][1], early_up[k], late_down[k]) for k in both]
    for_far = [plus(*(term[n:] for term in terms_high[k])) for k in both]
    for_below = [plus(*(term[n:] for term in terms_low[k])) for k in both]
    relayed = [shift(for_far[k], axes[k][0], 1) for k in both]
    from_above = [shift(for_below[k], axes[k][0], -1) for k in both]
    relayed, from_above = after((relayed, from_above))
    from_below = [
        shift(plus(*(term[:n] for term in terms_high[k]), relayed[k]), axes[k][0], 1) for k in both
    ]
    from_below = after(from_below)
    finished = [
        plus(*(term[:n] for term in terms_low[k]), from_below[k], from_above[k]) for k in both
    ]
    back = lax.all_to_all(
        jnp.concatenate(finished, axis=0).reshape(dp_count, slots, width),
        "dp",
        split_axis=0,
        concat_axis=0,
        tiled=True,
    ).reshape(window * CAP, width)

    half = (KVW - LATENT) // 2
    freq = 10000.0 ** (-jnp.arange(half, dtype=jnp.float32) / half)
    angle = kv_lengths.astype(jnp.float32)[:, None] * freq[None, :]
    return tuple(
        tail(
            hidden_in,
            back,
            kv_gain,
            jnp.cos(angle),
            jnp.sin(angle),
            top,
            total,
            place_weight,
            w_all,
            queries,
            cached,
        )
    )


def solution(mesh):
    return jax.shard_map(
        body,
        mesh=mesh,
        in_specs=(
            P(("dp", "expert"), None),
            P(),
            P(("dp", "expert"), None),
            P(("dp", "expert"), None),
            P("dp", None, "expert"),
            P("dp", None, "expert"),
            P("dp", "expert", None),
            P(("dp", "expert"), None),
            P(),
            P(("dp", "expert"), None),
            P(("dp", "expert"), None),
            P(("dp", "expert"), None),
            P(("dp", "expert")),
            P("dp", "expert", None, None),
        ),
        out_specs=(P(("dp", "expert"), None), P(("dp", "expert"), None)),
        check_vma=False,
    )
```
